512 devices in a mesh: section: 16 (over z), batch: 32 (over x, y, core).
Axes of the slice: x: 4, y: 4, z: 16, core: 2. Of those that a mesh axis runs over, the one named last changes fastest.
Arguments:
- images: bfloat16 [32, 256, 1536], P('batch'), may hold values from -10 to 10
- weights: bfloat16 [16, 6, 256, 256], P('section'), may hold values from -0.375 to 0.375
- bn_mean: float32 [16, 1536], P('section'), may hold values from -3 to 3
- bn_var: float32 [16, 1536], P('section'), may hold values from 0.25 to 2
- bn_gain: float32 [16, 1536], P('section'), may hold values from 0.1 to 1.9
- bn_bias: float32 [16, 1536], P('section'), may hold values from -3 to 3
Outputs:
- image_grad: bfloat16 [32, 256, 1536], P('batch', 'section')
- loss_value: float32 [], replicated
The draws below stay inside these ranges and needn't reach their ends.
All inputs are finite; a program needn't handle non-finite values.
Results may differ from the reference program's by a relative error of at most 0.013.
Values may be sent and summed in bfloat16 or wider, within the bound.
No kernel may reach another device: no remote copies, remote signals or barrier semaphores. Data moves between devices by JAX's collectives and lax.ppermute only.
A program may use at most 64 MiB of HBM per device.

```python
import math
import jax
import jax.numpy as jnp
from jax import lax

CW = 1536
GW = 256
BLOCK = 512
MICRO = 8
ROWS = 32
LAYERS = 16
N_BATCH = 32


def draw_images(key, part):
    key_noise = jax.random.fold_in(key, 11)
    key_offset = jax.random.fold_in(key, 23)
    key_mixing = jax.random.fold_in(key, 53)
    shape = (N_BATCH, MICRO * ROWS, CW)
    block_count = CW // BLOCK
    offsets = jnp.clip(jax.random.normal(key_offset, (CW,), jnp.float32), -3.0, 3.0)
    ramp = jnp.arange(N_BATCH, dtype=jnp.float32) / max(N_BATCH - 1, 1)
    mix_noise = jnp.clip(jax.random.normal(key_mixing, (block_count, BLOCK, BLOCK), jnp.float32), -4.0, 4.0)
    mixing = jnp.eye(BLOCK, dtype=jnp.float32)[None] + mix_noise * (0.6 / BLOCK ** 0.5)
    noise = jnp.clip(jax.random.normal(key_noise, shape, jnp.float32), -6.0, 6.0) * 0.8
    factor = 0.3 + 1.2 * ramp
    blocks = noise.reshape(N_BATCH, MICRO * ROWS, block_count, BLOCK)
    mixed = jnp.einsum('nrbi,bij->nrbj', blocks, mixing, precision=lax.Precision.HIGHEST).reshape(shape)
    values = jnp.clip(mixed + factor[:, None, None] * offsets[None, None, :], -9.9, 9.9)
    return values.astype(jnp.bfloat16)


def block_levels(rng, shape, cuts, smallest, high):
    def one(axis_at, shards_of):
        draws = jax.random.uniform(jax.random.fold_in(jax.random.fold_in(rng, 6), axis_at), (shards_of,), jnp.float32, smallest / len(cuts), high / len(cuts))
        return jnp.repeat(jnp.exp(draws), shape[axis_at] // shards_of).reshape((-1,) + (1,) * (len(shape) - axis_at - 1))

    factor_of = one(*cuts[0])
    for cut in cuts[1:]:
        factor_of = factor_of * one(*cut)
    return factor_of


def centred(stream_key, dims, width, limit, cuts=(), kind=jnp.bfloat16):
    array = width * jax.random.normal(stream_key, dims, jnp.float32)
    if cuts:
        array = array * block_levels(stream_key, dims, cuts, -0.22, 0.18)
    return jnp.clip(array, -limit, limit).astype(kind)


def setup_inputs(seed: int = 0) -> dict:
    arg_keys = jax.random.split(jax.random.key(seed), 7)
    images = draw_images(jax.random.fold_in(arg_keys[6], 71), 0)
    weights = centred(arg_keys[1], (LAYERS, CW // GW, GW, GW), GW ** -0.5, 0.375, ((0, 16),))
    bn_mean = centred(arg_keys[2], (LAYERS, CW), 0.5, 3.0, ((0, 16),), jnp.float32)
    bn_var = jnp.clip(jnp.exp(math.log(2.0) - 2.0794415 * jax.random.uniform(arg_keys[3], (LAYERS, CW), jnp.float32) ** block_levels(arg_keys[3], (LAYERS, CW), ((0, 16),), -0.2, 0.2)), 0.25, 2.0)
    bn_gain = jnp.clip(1.0 + 0.18 * jax.random.normal(arg_keys[4], (LAYERS, CW), jnp.float32), 0.1, 1.9)
    bn_bias = centred(arg_keys[5], (LAYERS, CW), 0.5, 3.0, ((0, 16),), jnp.float32)
    return dict(images=images, weights=weights, bn_mean=bn_mean, bn_var=bn_var, bn_gain=bn_gain, bn_bias=bn_bias)


EPS = 1e-05
HIGHEST = lax.Precision.HIGHEST

def conv_forward(hidden, weight):
    row_total = hidden.shape[0]
    groups, in_width, out_width = weight.shape
    pieces = hidden.astype(jnp.float32).reshape(row_total, groups, in_width)
    result = jnp.einsum('rgi,gio->rgo', pieces, weight.astype(jnp.float32))
    return result.reshape(row_total, groups * out_width)

def conv_backward(upstream, weight):
    row_total = upstream.shape[0]
    groups, in_width, out_width = weight.shape
    pieces = upstream.astype(jnp.float32).reshape(row_total, groups, out_width)
    result = jnp.einsum('rgo,gio->rgi', pieces, weight.astype(jnp.float32))
    return result.reshape(row_total, groups * in_width)

def target_blocks(variance):
    blocks = variance.reshape(-1, BLOCK)
    return blocks[:, :, None] * jnp.eye(BLOCK, dtype=jnp.float32)[None]

def reference(images, weights, bn_mean, bn_var, bn_gain, bn_bias):
    channels = images.shape[2]
    hidden = images.reshape(-1, channels)
    row_total = hidden.shape[0]
    block_count = channels // BLOCK
    saved = []
    loss_total = jnp.zeros((), jnp.float32)
    for layer_index in range(LAYERS):
        bn_scale = bn_gain[layer_index] * lax.rsqrt(bn_var[layer_index] + EPS)
        pre_act = conv_forward(hidden, weights[layer_index])
        batch_mean = lax.optimization_barrier(jnp.sum(pre_act, axis=0)) / row_total
        centered = (pre_act - batch_mean).reshape(row_total, block_count, BLOCK)
        covariance = jnp.einsum('rbi,rbj->bij', centered, centered, precision=HIGHEST) / row_total
        deviation = covariance - target_blocks(bn_var[layer_index])
        loss_total = loss_total + jnp.sum((batch_mean - bn_mean[layer_index]) ** 2) + 0.25 * jnp.sum(deviation ** 2)
        saved.append((pre_act, batch_mean, deviation, bn_scale))
        active = (pre_act - bn_mean[layer_index]) * bn_scale + bn_bias[layer_index]
        hidden = jax.nn.silu(active).astype(jnp.bfloat16)
    upstream = jnp.zeros((row_total, channels), jnp.bfloat16)
    for layer_index in reversed(range(LAYERS)):
        pre_act, batch_mean, deviation, bn_scale = saved[layer_index]
        active = (pre_act - bn_mean[layer_index]) * bn_scale + bn_bias[layer_index]
        sig_value = jax.nn.sigmoid(active)
        silu_slope = sig_value * (1.0 + active * (1.0 - sig_value))
        centered = (pre_act - batch_mean).reshape(row_total, block_count, BLOCK)
        cov_pull = jnp.einsum('rbi,bij->rbj', centered, deviation, precision=HIGHEST).reshape(row_total, channels)
        pre_grad = upstream.astype(jnp.float32) * silu_slope * bn_scale + 2.0 * (batch_mean - bn_mean[layer_index]) + cov_pull
        pre_grad = pre_grad.astype(jnp.bfloat16)
        upstream = conv_backward(pre_grad, weights[layer_index]).astype(jnp.bfloat16)
    return (upstream.reshape(images.shape), loss_total / (LAYERS * channels))
```

```python
import jax
import jax.numpy as jnp
import numpy as np
from jax import lax
from jax.experimental import pallas as pl
from jax.experimental.pallas import tpu as pltpu
from jax.sharding import Mesh, PartitionSpec as P

EPS = 1e-05
HIGHEST = lax.Precision.HIGHEST
F32 = jnp.float32
BF16 = jnp.bfloat16

LAYERS = 16
GW = 256
BLOCKS = 3
CHIPS = 16
SLICE = GW // CHIPS
PROWS = 8
BROWS = 64
ROWS = 2 * BROWS
HOME = CHIPS * BROWS
PARTS = 8
PIECE = GW // PARTS
TAIL = 8
TOTAL = HOME * PARTS


def split2(value):
    high = lax.reduce_precision(value, 8, 7)
    return high.astype(BF16), (value - high).astype(BF16)


def split3(value):
    high = value.astype(BF16).astype(F32)
    rest = value - high
    middle = rest.astype(BF16).astype(F32)
    return high, middle, rest - middle


def forward_kernel(x_ref, w_ref, par_ref, xs_ref, slope_ref):
    x = x_ref[...]
    for layer in range(LAYERS):
        xs_ref[layer] = x
        weight = w_ref[:, layer].reshape(GW, GW)
        packed = par_ref[layer, SLICE:SLICE + PROWS].astype(F32)
        scale = packed[0:1] + packed[4:5]
        shift = packed[1:2] + packed[5:6]
        active = jnp.dot(x, weight, preferred_element_type=F32) * scale + shift
        gate = 1.0 / (1.0 + jnp.exp(-active))
        slope_ref[layer] = gate * (1.0 + active * (1.0 - gate)) * scale
        x = (active * gate).astype(BF16)


def gram_kernel(x_ref, wl_ref, out_ref, zc_ref):
    means = []
    for g in range(2):
        z = jnp.dot(x_ref[:, g].reshape(HOME, GW), wl_ref[g, 0:GW], preferred_element_type=F32)
        mean = jnp.sum(z, axis=0, keepdims=True) * (1.0 / HOME)
        zc_ref[g] = (z - mean).astype(BF16)
        means.append(mean)
    parts = [split3(mean) for mean in means]
    tail = [parts[g][term] for term in range(3) for g in range(2)]
    tail = jnp.concatenate(tail + [jnp.zeros((2, GW), F32)], axis=0).astype(BF16)
    for at, (a, b) in enumerate(((0, 0), (0, 1), (1, 1))):
        gram = lax.dot_general(
            zc_ref[a], zc_ref[b], (((0,), (0,)), ((), ())), preferred_element_type=F32
        ).astype(BF16)
        for j in range(PARTS):
            out_ref[j, at * PIECE:(at + 1) * PIECE] = gram[j * PIECE:(j + 1) * PIECE]
    for j in range(PARTS):
        out_ref[j, 3 * PIECE:3 * PIECE + TAIL] = tail


def all_means(r_ref):
    rows = r_ref[:, 3 * PIECE:3 * PIECE + TAIL].astype(F32)
    return [rows[:, g] + rows[:, 2 + g] + rows[:, 4 + g] for g in range(2)]


def deviation_kernel(j_ref, r_ref, wl_ref, e_ref, scratch_ref):
    row_at = j_ref[0] * PIECE
    means = all_means(r_ref)
    shifted = [m - jnp.mean(m, axis=0, keepdims=True) for m in means]
    total = jnp.sum(r_ref[:, 0:3 * PIECE].astype(F32), axis=0) * (1.0 / TOTAL)
    diagonal = (
        lax.broadcasted_iota(jnp.int32, (PIECE, GW), 0) + row_at
        == lax.broadcasted_iota(jnp.int32, (PIECE, GW), 1)
    )
    for at, (a, b) in enumerate(((0, 0), (0, 1), (1, 1))):
        scratch_ref[...] = lax.dot_general(
            shifted[a], shifted[b], (((0,), (0,)), ((), ())), precision=HIGHEST, preferred_element_type=F32
        )
        part = total[at * PIECE:(at + 1) * PIECE] + scratch_ref[pl.ds(row_at, PIECE), :] * (1.0 / PARTS)
        if a == b:
            packed = wl_ref[a, GW:GW + PROWS].astype(F32)
            part = part - jnp.where(diagonal, packed[3:4] + packed[7:8], 0.0)
        e_ref[at * PIECE:(at + 1) * PIECE] = part.astype(BF16)


def pull_kernel(j_ref, e_ref, r_ref, wl_ref, zc_ref, out_ref):
    means = all_means(r_ref)
    mine = r_ref[j_ref[0], 3 * PIECE:3 * PIECE + TAIL].astype(F32)
    mats = [e_ref[:, at * PIECE:(at + 1) * PIECE].reshape(GW, GW) for at in range(3)]
    whole = [m.astype(F32) for m in mats]
    loss = 0.25 * (
        jnp.sum(whole[0] * whole[0], keepdims=True)
        + 2.0 * jnp.sum(whole[1] * whole[1], keepdims=True)
        + jnp.sum(whole[2] * whole[2], keepdims=True)
    )
    away, offset = [], []
    for g in range(2):
        packed = wl_ref[g, GW:GW + PROWS].astype(F32)
        mean = jnp.mean(means[g], axis=0, keepdims=True)
        gap = mean - (packed[2:3] + packed[6:7])
        loss = loss + jnp.sum(gap * gap, keepdims=True)
        away.append(2.0 * gap)
        own = mine[g:g + 1] + mine[2 + g:3 + g] + mine[4 + g:5 + g]
        offset.append(jnp.broadcast_to(own - mean, (8, GW)))
    tail = [jnp.broadcast_to(part, (1, GW)) for part in split3(loss)]
    tail = jnp.concatenate(tail + [jnp.zeros((TAIL - 3, GW), F32)], axis=0).astype(BF16)
    tail = jnp.broadcast_to(tail[None], (CHIPS, TAIL, GW))
    plain, crossed = (((1,), (0,)), ((), ())), (((1,), (1,)), ((), ()))

    def product(lhs, rhs, dims, precision=None):
        return lax.dot_general(lhs, rhs, dims, precision=precision, preferred_element_type=F32)

    for g in range(2):
        first, second = (plain, crossed) if g == 0 else (plain, plain)
        at, bt = (0, 1) if g == 0 else (1, 2)
        row = (
            product(offset[0], whole[at], first, HIGHEST) + product(offset[1], whole[bt], second, HIGHEST)
        )[0:1] + away[g]
        pull = product(zc_ref[0], mats[at], first) + product(zc_ref[1], mats[bt], second) + row
        out_ref[:, g, 0:BROWS] = pull.astype(BF16).reshape(CHIPS, BROWS, GW)
        out_ref[:, g, BROWS:BROWS + TAIL] = tail


def backward_kernel(q_ref, slope_ref, w_ref, out_ref):
    loss = jnp.zeros((1, GW), F32)
    grad = None
    for layer in reversed(range(LAYERS)):
        rows = q_ref[layer, 0, BROWS:BROWS + TAIL].astype(F32)
        loss = loss + (rows[0:1] + rows[1:2] + rows[2:3])
        pull = q_ref[layer, :, 0:BROWS].reshape(ROWS, GW)
        if grad is not None:
            pull = (grad * slope_ref[layer] + pull.astype(F32)).astype(BF16)
        weight = w_ref[:, layer].reshape(GW, GW)
        grad = lax.dot_general(
            pull, weight, (((1,), (1,)), ((), ())), preferred_element_type=F32
        ).astype(BF16).astype(F32)
    tail = jnp.concatenate(list(split3(loss)) + [jnp.zeros((TAIL - 3, GW), F32)], axis=0).astype(BF16)
    grad = grad.astype(BF16)
    for b in range(2):
        for strip in range(4):
            at = b * BROWS + strip * 16
            out_ref[strip, b, 0:16] = grad[at:at + 16]
            out_ref[strip, b, 16:16 + TAIL] = tail


VMEM = pl.BlockSpec(memory_space=pltpu.VMEM)
SMEM = pl.BlockSpec(memory_space=pltpu.SMEM)


def kernel_call(kernel, outs, count, name, scalars=0, scratch=()):
    return pl.pallas_call(
        kernel,
        out_shape=[jax.ShapeDtypeStruct(shape, dtype) for shape, dtype in outs],
        in_specs=[SMEM] * scalars + [VMEM] * (count - scalars),
        out_specs=[VMEM] * len(outs),
        scratch_shapes=list(scratch),
        name=name,
    )


def shards(images, weights, bn_mean, bn_var, bn_gain, bn_bias):
    k, q, c = lax.axis_index("k"), lax.axis_index("q"), lax.axis_index("c")
    block = jnp.minimum(k, BLOCKS - 1)
    chip = lax.axis_index(("x", "y"))
    part = (q * 2 + c).astype(jnp.int32).reshape(1)

    scale = bn_gain[0] * lax.rsqrt(bn_var[0] + EPS)
    shift = bn_bias[0] - bn_mean[0] * scale
    packed = jnp.stack(split2(jnp.stack([scale, shift, bn_mean[0], bn_var[0]])))
    packed = packed.reshape(PROWS, BLOCKS, 2, GW)
    packed = lax.dynamic_index_in_dim(packed, c, 2, keepdims=False).transpose(1, 0, 2)
    slab = weights[0].reshape(BLOCKS, 2, GW, GW)
    slab = lax.dynamic_slice(slab, (0, c, chip * SLICE, 0), (BLOCKS, 1, SLICE, GW))[:, 0]
    message = jnp.concatenate([slab, packed], axis=1)
    message = jnp.concatenate([message, message[BLOCKS - 1:]], axis=0)
    message = jnp.broadcast_to(message[:, None], (4, 4, SLICE + PROWS, GW)).reshape(LAYERS, SLICE + PROWS, GW)
    layer_parts = lax.all_to_all(message, ("k", "q"), 0, 0, tiled=True)

    own = layer_parts[:, 0:SLICE]
    chain_weights = lax.all_to_all(
        jnp.broadcast_to(own[None], (CHIPS, LAYERS, SLICE, GW)), ("x", "y"), 0, 0, tiled=True
    )

    rows = lax.dynamic_index_in_dim(images[0].reshape(4, 4, 16, BLOCKS * 2 * GW), q, 1, keepdims=False)
    rows = lax.dynamic_index_in_dim(rows.reshape(BROWS, BLOCKS, 2, GW), block, 1, keepdims=False)
    rows = lax.all_to_all(rows.transpose(1, 0, 2), "c", 0, 0, tiled=True).reshape(ROWS, GW)

    xs, slope = kernel_call(
        forward_kernel, [((LAYERS, ROWS, GW), BF16), ((LAYERS, ROWS, GW), F32)], 3, "fwd"
    )(rows, chain_weights, layer_parts)

    home = lax.all_to_all(xs.reshape(2 * CHIPS, BROWS, GW), ("x", "y", "c"), 0, 0, tiled=True)
    mine = jnp.concatenate(
        [
            lax.dynamic_index_in_dim(chain_weights, chip, 1, keepdims=False).reshape(GW, GW),
            lax.dynamic_index_in_dim(layer_parts, chip, 0, keepdims=False)[SLICE:],
        ],
        axis=0,
    )
    both = lax.all_gather(mine, "c", axis=0)
    pieces, centered = kernel_call(
        gram_kernel, [((PARTS, 3 * PIECE + TAIL, GW), BF16), ((2, HOME, GW), BF16)], 2, "gram"
    )(home.reshape(CHIPS, 2, BROWS, GW), both)
    pieces = lax.all_to_all(pieces, ("q", "c"), 0, 0, tiled=True)
    (deviation,) = kernel_call(
        deviation_kernel, [((3 * PIECE, GW), BF16)], 3, "deviation", 1, [pltpu.VMEM((GW, GW), F32)]
    )(part, pieces, both)
    deviation = lax.all_gather(deviation, ("q", "c"), axis=0)
    (pulls,) = kernel_call(pull_kernel, [((CHIPS, 2, BROWS + TAIL, GW), BF16)], 5, "pull", 1)(
        part, deviation, pieces, both, centered
    )
    pulls = lax.all_to_all(pulls.reshape(2 * CHIPS, BROWS + TAIL, GW), ("x", "y", "c"), 0, 0, tiled=True)

    (grads,) = kernel_call(backward_kernel, [((4, 2, 16 + TAIL, GW), BF16)], 3, "bwd")(
        pulls.reshape(LAYERS, 2, BROWS + TAIL, GW), slope, chain_weights
    )
    grads = lax.all_to_all(grads.reshape(8, 16 + TAIL, GW), ("k", "c"), 0, 0, tiled=True)
    grads = grads.reshape(4, 2, 16 + TAIL, GW)[:BLOCKS]
    terms = grads[:, 0, 16:19, 0].astype(F32)
    loss = jnp.sum(terms) / (LAYERS * BLOCKS * 2 * GW)
    image_grad = grads[:, :, 0:16].transpose(2, 0, 1, 3).reshape(1, 16, BLOCKS * 2 * GW)
    return image_grad, loss


def solution(mesh):
    fine = Mesh(np.asarray(mesh.devices).reshape(4, 4, 4, 4, 2), ("k", "q", "x", "y", "c"))
    batch, section = ("x", "y", "c"), ("k", "q")
    return jax.shard_map(
        shards,
        mesh=fine,
        in_specs=(
            P(batch, None, None),
            P(section, None, None, None),
            P(section, None),
            P(section, None),
            P(section, None),
            P(section, None),
        ),
        out_specs=(P(batch, section, None), P()),
        check_vma=False,
    )
```

```python
import math

import jax
import jax.numpy as jnp
import numpy as np
from jax import lax
from jax.experimental import pallas as pl
from jax.experimental.pallas import tpu as pltpu
from jax.sharding import Mesh, PartitionSpec as P

EPS = 1e-05
HIGHEST = lax.Precision.HIGHEST
F32 = jnp.float32
BF16 = jnp.bfloat16

LAYERS = 16
GW = 256
BLOCKS = 3
CHIPS = 16
SLICE = GW // (2 * CHIPS)
PROWS = 8
ROWS = 128
HALF = ROWS // 2
HOME = CHIPS * HALF
LANES = 128
PARTS = 8
PIECE = GW // PARTS
TAIL = 8
TOTAL = HOME * PARTS


def split3(value):
    high = value.astype(BF16).astype(F32)
    rest = value - high
    middle = rest.astype(BF16).astype(F32)
    return high, middle, rest - middle


def pack_kernel(w_ref, images_ref, mean_ref, var_ref, gain_ref, bias_ref, out_ref, x_ref, slab_ref, sems):
    chip = lax.axis_index("x") * 4 + lax.axis_index("y")
    row = (lax.axis_index("c") * CHIPS + chip) * SLICE
    half = lax.axis_index("h")
    group = 2 * jnp.minimum(lax.axis_index("k"), BLOCKS - 1) + lax.axis_index("g")
    slab = pltpu.make_async_copy(w_ref.at[0, :, pl.ds(pl.multiple_of(row, SLICE), SLICE), :], slab_ref, sems.at[0])
    slab.start()
    copies = []
    for strip in range(4):
        source = images_ref.at[
            0, pl.ds(pl.multiple_of(strip * 64 + half * 32, 32), 32), pl.ds(pl.multiple_of(group * GW, GW), GW)
        ]
        copies.append(pltpu.make_async_copy(source, x_ref.at[strip * 32:strip * 32 + 32], sems.at[1 + strip]))
        copies[-1].start()
    scale = gain_ref[...] * lax.rsqrt(var_ref[...] + EPS)
    packed = [scale, bias_ref[...] - mean_ref[...] * scale, mean_ref[...], var_ref[...]]
    high = [value.astype(BF16).astype(F32) for value in packed]
    packed = jnp.concatenate(high + [value - top for value, top in zip(packed, high)], axis=0).astype(BF16)
    slab.wait()
    for k in range(4):
        for g in range(2):
            at = 2 * min(k, BLOCKS - 1) + g
            for h in range(2):
                out_ref[k, h, g, 0:SLICE] = slab_ref[at]
                out_ref[k, h, g, SLICE:] = packed[:, at * GW:(at + 1) * GW]
    for copy in copies:
        copy.wait()


def in_order(own, other, core):
    return jnp.concatenate([lax.select(core == 0, own, other), lax.select(core == 0, other, own)], axis=0)


def layer_weight(own_ref, other_ref, core, layer):
    return in_order(own_ref[:, layer].reshape(GW // 2, GW), other_ref[:, layer].reshape(GW // 2, GW), core)


def forward_kernel(j_ref, x_ref, par_ref, own_ref, other_ref, xs_ref, slope_ref):
    core = j_ref[0] % 2
    x = x_ref[...]
    for layer in range(LAYERS):
        xs_ref[layer] = x
        weight = layer_weight(own_ref, other_ref, core, layer)
        packed = par_ref[layer, SLICE:SLICE + PROWS].astype(F32)
        scale = packed[0:1] + packed[4:5]
        shift = packed[1:2] + packed[5:6]
        active = jnp.dot(x, weight, preferred_element_type=F32) * scale + shift
        gate = 1.0 / (1.0 + jnp.exp(-active))
        x = (active * gate).astype(BF16)
        slope_ref[layer] = (gate * (1.0 + active * (1.0 - gate)) * scale).astype(BF16)


def gram_kernel(j_ref, x_ref, mine_ref, theirs_ref, keep_ref, send_ref, tail_ref, par_ref, zc_ref):
    core, side = j_ref[0] % 2, j_ref[0] // 2 % 2
    means = []
    for g in range(2):
        layer = lax.select(side == g, mine_ref[...], theirs_ref[...])
        packed = layer[GW:].astype(F32)
        par_ref[g] = packed[0:4] + packed[4:8]
        weight = in_order(layer[0:GW // 2], layer[GW // 2:GW], core)
        z = jnp.dot(x_ref[:, g].reshape(HOME, GW), weight, preferred_element_type=F32)
        mean = jnp.sum(z, axis=0, keepdims=True) * (1.0 / HOME)
        zc_ref[g] = (z - mean).astype(BF16)
        means.append(mean)
    parts = [split3(mean) for mean in means]
    tail = [parts[g][term] for term in range(3) for g in range(2)]
    tail = jnp.concatenate(tail + [jnp.zeros((2, GW), F32)], axis=0).astype(BF16)
    tail_ref[...] = tail
    send_ref[4 * 3 * PIECE:] = tail
    for at, (a, b) in enumerate(((0, 0), (0, 1), (1, 1))):
        gram = lax.dot_general(zc_ref[a], zc_ref[b], (((0,), (0,)), ((), ())), preferred_element_type=F32)
        low, high = gram[0:GW // 2], gram[GW // 2:]
        keep, send = lax.select(core == 0, low, high), lax.select(core == 0, high, low).astype(BF16)
        for j in range(4):
            rows = pl.ds((3 * j + at) * PIECE, PIECE)
            keep_ref[rows] = keep[j * PIECE:(j + 1) * PIECE]
            send_ref[rows] = send[j * PIECE:(j + 1) * PIECE]


def chip_kernel(j_ref, keep_ref, tail_ref, got_ref, out_ref):
    core = j_ref[0] % 2
    tails = in_order(tail_ref[...], got_ref[4 * 3 * PIECE:], core)
    for j in range(4):
        rows = pl.ds(3 * j * PIECE, 3 * PIECE)
        out_ref[j, 0:3 * PIECE] = (keep_ref[rows] + got_ref[rows].astype(F32)).astype(BF16)
        out_ref[j, 3 * PIECE:] = tails


def mean_of(rows, g):
    return rows[..., g, :] + rows[..., 2 + g, :] + rows[..., 4 + g, :]


def all_means(r_ref):
    rows = r_ref[:, 3 * PIECE:].astype(F32)
    cores = rows[:, 0:TAIL], rows[:, TAIL:]
    return [jnp.concatenate([mean_of(core, g) for core in cores], axis=0) for g in range(2)]


def deviation_kernel(j_ref, r_ref, par_ref, e_ref, scratch_ref):
    row_at = (j_ref[0] % 2 * 4 + j_ref[0] // 2) * PIECE
    means = all_means(r_ref)
    shifted = [m - jnp.mean(m, axis=0, keepdims=True) for m in means]
    total = jnp.sum(r_ref[:, 0:3 * PIECE].astype(F32), axis=0) * (1.0 / TOTAL)
    diagonal = (
        lax.broadcasted_iota(jnp.int32, (PIECE, GW), 0) + row_at
        == lax.broadcasted_iota(jnp.int32, (PIECE, GW), 1)
    )
    for at, (a, b) in enumerate(((0, 0), (0, 1), (1, 1))):
        scratch_ref[...] = lax.dot_general(
            shifted[a], shifted[b], (((0,), (0,)), ((), ())), precision=HIGHEST, preferred_element_type=F32
        )
        part = total[at * PIECE:(at + 1) * PIECE] + scratch_ref[pl.ds(row_at, PIECE), :] * (1.0 / PARTS)
        if a == b:
            part = part - jnp.where(diagonal, par_ref[a, 3:4], 0.0)
        for j in range(4):
            e_ref[j, at * PIECE:(at + 1) * PIECE] = part.astype(BF16)


def pull_kernel(e_ref, r_ref, tail_ref, par_ref, zc_ref, out_ref):
    means = all_means(r_ref)
    mine = tail_ref[...].astype(F32)
    mats = [e_ref[:, :, at * PIECE:(at + 1) * PIECE].reshape(GW, GW) for at in range(3)]
    whole = [m.astype(F32) for m in mats]
    loss = 0.25 * (
        jnp.sum(whole[0] * whole[0], keepdims=True)
        + 2.0 * jnp.sum(whole[1] * whole[1], keepdims=True)
        + jnp.sum(whole[2] * whole[2], keepdims=True)
    )
    away, offset = [], []
    for g in range(2):
        mean = jnp.mean(means[g], axis=0, keepdims=True)
        gap = mean - par_ref[g, 2:3]
        loss = loss + jnp.sum(gap * gap, keepdims=True)
        away.append(2.0 * gap)
        own = mine[g:g + 1] + mine[2 + g:3 + g] + mine[4 + g:5 + g]
        offset.append(jnp.concatenate(list(split3(own - mean)) + [jnp.zeros((13, GW), F32)], axis=0).astype(BF16))
    tail = [jnp.broadcast_to(part, (1, LANES)) for part in split3(loss)]
    tail = jnp.concatenate(tail + [jnp.zeros((TAIL - 3, LANES), F32)], axis=0).astype(BF16)
    tail = jnp.broadcast_to(tail[None], (CHIPS, TAIL, LANES))
    plain, crossed = (((1,), (0,)), ((), ())), (((1,), (1,)), ((), ()))

    def product(side, at, dims):
        lhs = jnp.concatenate([zc_ref[side], offset[side]], axis=0)
        return lax.dot_general(lhs, mats[at], dims, preferred_element_type=F32)

    for g in range(2):
        pull = product(0, 0, plain) + product(1, 1, crossed) if g == 0 else product(0, 1, plain) + product(1, 2, plain)
        row = pull[HOME:HOME + 1] + pull[HOME + 1:HOME + 2] + pull[HOME + 2:HOME + 3] + away[g]
        pull = pull[0:HOME] + row
        pull = pull.astype(BF16).reshape(CHIPS, HALF, GW)
        out_ref[:, g, 0:HALF] = pull[:, :, 0:LANES]
        out_ref[:, g, HALF:2 * HALF] = pull[:, :, LANES:]
        out_ref[:, g, 2 * HALF:] = tail


def backward_kernel(j_ref, q_ref, slope_ref, own_ref, other_ref, out_ref):
    core = j_ref[0] % 2
    loss = jnp.zeros((1, LANES), F32)
    grad = None
    for layer in reversed(range(LAYERS)):
        rows = q_ref[layer, 0, 2 * HALF:].astype(F32)
        loss = loss + (rows[0:1] + rows[1:2] + rows[2:3])
        pull = jnp.concatenate(
            [q_ref[layer, :, 0:HALF].reshape(ROWS, LANES), q_ref[layer, :, HALF:2 * HALF].reshape(ROWS, LANES)], axis=1
        )
        if grad is not None:
            pull = (grad * slope_ref[layer].astype(F32) + pull.astype(F32)).astype(BF16)
        grad = lax.dot_general(
            pull, layer_weight(own_ref, other_ref, core, layer), (((1,), (1,)), ((), ())), preferred_element_type=F32
        ).astype(BF16).astype(F32)
    loss = jnp.concatenate([loss, loss], axis=1)
    tail = jnp.concatenate(list(split3(loss)) + [jnp.zeros((TAIL - 3, GW), F32)], axis=0).astype(BF16)
    grad = grad.astype(BF16)
    for strip in range(8):
        out_ref[strip, 0:16] = grad[strip * 16:strip * 16 + 16]
        out_ref[strip, 16:16 + TAIL] = tail


def output_kernel(r_ref, grad_ref, loss_ref):
    loss = jnp.zeros((1, 1), F32)
    for k in range(BLOCKS):
        for g in range(2):
            at = 2 * k + g
            grad_ref[0, :, at * GW:(at + 1) * GW] = r_ref[at, 0:16]
        loss = loss + jnp.sum(r_ref[2 * k, 16:16 + TAIL].astype(F32)[0:3, 0:1], axis=0, keepdims=True)
    loss_ref[...] = loss * (1.0 / (LAYERS * BLOCKS * 2 * GW))


LARGE = 1100000


def is_large(shape, dtype):
    return math.prod(shape) * jnp.dtype(dtype).itemsize > LARGE


def kernel_call(kernel, outs, name, *args, scalars=(), scratch=(), far=(), loose=()):
    vmem = pl.BlockSpec(memory_space=pltpu.VMEM)
    smem = pl.BlockSpec(memory_space=pltpu.SMEM)
    placed = [arg if is_large(arg.shape, arg.dtype) else pltpu.with_memory_space_constraint(arg, pltpu.VMEM) for arg in args]
    placed += [pltpu.with_memory_space_constraint(arg, pltpu.HBM) for arg in far]
    return pl.pallas_call(
        kernel,
        out_shape=[jax.ShapeDtypeStruct(*out) if is_large(*out) else pltpu.VMEM(*out) for out in outs] + list(loose),
        in_specs=[smem] * len(scalars) + [vmem] * len(placed),
        out_specs=[vmem] * (len(outs) + len(loose)),
        scratch_shapes=list(scratch),
        name=name,
    )(*scalars, *placed)


def shards(images, weights, bn_mean, bn_var, bn_gain, bn_bias):
    chip = lax.axis_index(("x", "y"))
    part = lax.axis_index(("h", "g", "c")).astype(jnp.int32).reshape(1)

    hbm, vmem = pl.BlockSpec(memory_space=pl.ANY), pl.BlockSpec(memory_space=pltpu.VMEM)
    message, rows = pl.pallas_call(
        pack_kernel,
        out_shape=[pltpu.VMEM((4, 2, 2, SLICE + PROWS, GW), BF16), pltpu.VMEM((ROWS, GW), BF16)],
        in_specs=[hbm, hbm] + [vmem] * 4,
        out_specs=[vmem, vmem],
        scratch_shapes=[pltpu.VMEM((2 * BLOCKS, SLICE, GW), BF16), pltpu.SemaphoreType.DMA((5,))],
        name="pack",
    )(weights, images, bn_mean, bn_var, bn_gain, bn_bias)
    message = message.reshape(LAYERS, SLICE + PROWS, GW)
    layer_parts = lax.all_to_all(message, ("k", "h", "g"), 0, 0, tiled=True)

    own = layer_parts[:, 0:SLICE]
    own = lax.all_to_all(jnp.broadcast_to(own[None], (CHIPS, LAYERS, SLICE, GW)), ("x", "y"), 0, 0, tiled=True)
    other = lax.ppermute(own, "c", [(0, 1), (1, 0)])

    xs, slope = kernel_call(
        forward_kernel,
        [],
        "fwd",
        rows,
        layer_parts,
        scalars=[part],
        far=[own, other],
        loose=[jax.ShapeDtypeStruct((LAYERS, ROWS, GW), BF16)] * 2,
    )

    home = lax.all_to_all(xs.reshape(2 * CHIPS, HALF, GW), ("x", "y", "g"), 0, 0, tiled=True)
    mine = jnp.concatenate(
        [
            lax.dynamic_index_in_dim(own, chip, 1, keepdims=False).reshape(GW // 2, GW),
            lax.dynamic_index_in_dim(other, chip, 1, keepdims=False).reshape(GW // 2, GW),
            lax.dynamic_index_in_dim(layer_parts, chip, 0, keepdims=False)[SLICE:],
        ],
        axis=0,
    )
    mine = lax.optimization_barrier((mine, xs))[0]
    theirs = lax.ppermute(mine, "g", [(0, 1), (1, 0)])
    keep, send, tail, params, centered = kernel_call(
        gram_kernel,
        [
            ((4 * 3 * PIECE, GW), F32),
            ((4 * 3 * PIECE + TAIL, GW), BF16),
            ((TAIL, GW), BF16),
            ((2, 4, GW), F32),
        ],
        "gram",
        home.reshape(CHIPS, 2, HALF, GW),
        mine,
        theirs,
        scalars=[part],
        loose=[jax.ShapeDtypeStruct((2, HOME, GW), BF16)],
    )
    got = lax.ppermute(send, "c", [(0, 1), (1, 0)])
    (pieces,) = kernel_call(
        chip_kernel, [((4, 3 * PIECE + 2 * TAIL, GW), BF16)], "chip", keep, tail, got, scalars=[part]
    )
    pieces = lax.all_to_all(pieces, ("h", "g"), 0, 0, tiled=True)
    (deviation,) = kernel_call(
        deviation_kernel,
        [((4, 3 * PIECE, GW), BF16)],
        "deviation",
        pieces,
        params,
        scalars=[part],
        scratch=[pltpu.VMEM((GW, GW), F32)],
    )
    deviation = lax.all_gather(lax.all_to_all(deviation, ("h", "g"), 0, 0, tiled=True), "c", axis=0)
    (pulls,) = kernel_call(
        pull_kernel,
        [((CHIPS, 2, 2 * HALF + TAIL, LANES), BF16)],
        "pull",
        deviation,
        pieces,
        tail,
        params,
        far=[centered],
    )
    pulls = lax.all_to_all(pulls.reshape(2 * CHIPS, 2 * HALF + TAIL, LANES), ("x", "y", "g"), 0, 0, tiled=True)

    (grads,) = kernel_call(
        backward_kernel,
        [((8, 16 + TAIL, GW), BF16)],
        "bwd",
        pulls.reshape(LAYERS, 2, 2 * HALF + TAIL, LANES),
        scalars=[part],
        far=[slope, own, other],
    )
    grads = lax.all_to_all(grads, ("k", "g"), 0, 0, tiled=True)
    image_grad, loss = pl.pallas_call(
        output_kernel,
        out_shape=[jax.ShapeDtypeStruct((1, 16, BLOCKS * 2 * GW), BF16), jax.ShapeDtypeStruct((1, 1), F32)],
        in_specs=[vmem],
        out_specs=[vmem, vmem],
        name="outputs",
    )(pltpu.with_memory_space_constraint(grads, pltpu.VMEM))
    return image_grad, loss.reshape(())


def solution(mesh):
    fine = Mesh(np.asarray(mesh.devices).reshape(4, 2, 2, 4, 4, 2), ("k", "h", "g", "x", "y", "c"))
    batch, section = ("x", "y", "c"), ("k", "h", "g")
    return jax.shard_map(
        shards,
        mesh=fine,
        in_specs=(
            P(batch, None, None),
            P(section, None, None, None),
            P(section, None),
            P(section, None),
            P(section, None),
            P(section, None),
        ),
        out_specs=(P(batch, section, None), P()),
        check_vma=False,
    )
```

```python
import math

import jax
import jax.numpy as jnp
import numpy as np
from jax import lax
from jax.experimental import pallas as pl
from jax.experimental.pallas import tpu as pltpu
from jax.sharding import Mesh, PartitionSpec as P

EPS = 1e-05
LOG2E = math.log2(math.e)
HIGHEST = lax.Precision.HIGHEST
F32 = jnp.float32
BF16 = jnp.bfloat16

LAYERS = 16
GW = 256
BLOCKS = 3
CHIPS = 16
SLICE = GW // (2 * CHIPS)
PROWS = 8
ROWS = 128
HALF = ROWS // 2
HOME = CHIPS * HALF
LANES = 128
PARTS = 8
PIECE = GW // PARTS
TAIL = 8
TOTAL = HOME * PARTS


def split3(value):
    high = value.astype(BF16).astype(F32)
    rest = value - high
    middle = rest.astype(BF16).astype(F32)
    return high, middle, rest - middle


def pack_kernel(w_ref, images_ref, *refs):
    inputs, (out_ref, x_ref, slab_ref), held, sems = refs[:4], refs[4:7], refs[7:11], refs[11]
    reads = [pltpu.make_async_copy(source, target, sems.at[5 + at]) for at, (source, target) in enumerate(zip(inputs, held))]
    for copy in reads:
        copy.start()
    mean_ref, var_ref, gain_ref, bias_ref = held
    chip = lax.axis_index("y") * 4 + lax.axis_index("x")
    row = (lax.axis_index("c") * CHIPS + chip) * SLICE
    half = lax.axis_index("h")
    group = 2 * jnp.minimum(lax.axis_index("k"), BLOCKS - 1) + lax.axis_index("g")
    slab = pltpu.make_async_copy(w_ref.at[0, :, pl.ds(pl.multiple_of(row, SLICE), SLICE), :], slab_ref, sems.at[0])
    slab.start()
    copies = []
    for strip in range(4):
        source = images_ref.at[
            0, pl.ds(pl.multiple_of(strip * 64 + half * 32, 32), 32), pl.ds(pl.multiple_of(group * GW, GW), GW)
        ]
        copies.append(pltpu.make_async_copy(source, x_ref.at[strip * 32:strip * 32 + 32], sems.at[1 + strip]))
        copies[-1].start()
    for copy in reads:
        copy.wait()
    scale = gain_ref[...] * lax.rsqrt(var_ref[...] + EPS)
    packed = [scale, bias_ref[...] - mean_ref[...] * scale, mean_ref[...], var_ref[...]]
    high = [value.astype(BF16).astype(F32) for value in packed]
    packed = jnp.concatenate(high + [value - top for value, top in zip(packed, high)], axis=0).astype(BF16)
    slab.wait()
    for k in range(4):
        for g in range(2):
            at = 2 * min(k, BLOCKS - 1) + g
            for h in range(2):
                out_ref[k, h, g, 0:SLICE] = slab_ref[at]
                out_ref[k, h, g, SLICE:] = packed[:, at * GW:(at + 1) * GW]
    for copy in copies:
        copy.wait()


def in_order(own, other, core):
    return jnp.concatenate([lax.select(core == 0, own, other), lax.select(core == 0, other, own)], axis=0)


def forward_kernel(
    x_ref, par_ref, own_in, other_in, out_ref, w_out, slope_out, w_ref, slope_ref, rows_ref, sems
):
    core = lax.axis_index("c")
    chip = lax.axis_index("y") * 4 + lax.axis_index("x")
    arrivals = []
    for layer in range(LAYERS):
        arrivals.append(
            [
                pltpu.make_async_copy(own_in.at[:, layer], w_ref.at[layer, core], sems.at[0, layer]),
                pltpu.make_async_copy(other_in.at[:, layer], w_ref.at[layer, 1 - core], sems.at[1, layer]),
            ]
        )
        for copy in arrivals[layer]:
            copy.start()
    for layer in range(LAYERS):
        rows_ref[layer] = par_ref[layer, SLICE:SLICE + PROWS].astype(F32)
    at_row = lax.broadcasted_iota(jnp.int32, (TAIL, LANES), 0)
    copies = []
    x = x_ref[...]
    for layer in range(LAYERS):
        for copy in arrivals[layer]:
            copy.wait()
        copies.append(pltpu.make_async_copy(w_ref.at[layer], w_out.at[layer], sems.at[2, layer]))
        copies[-1].start()
        scale = rows_ref[layer, 0:1] + rows_ref[layer, 4:5]
        shift = rows_ref[layer, 1:2] + rows_ref[layer, 5:6]
        z = jnp.dot(x, w_ref[layer].reshape(GW, GW), preferred_element_type=F32)
        active = z * scale + shift
        gate = 1.0 / (1.0 + jnp.exp2(active * -LOG2E))
        after = active * gate
        x = after.astype(BF16)
        slope_ref[layer] = (gate * ((active - after) + 1.0) * scale).astype(BF16)
        copies.append(pltpu.make_async_copy(slope_ref.at[layer], slope_out.at[layer], sems.at[3, layer]))
        copies[-1].start()
        row = rows_ref[layer, pl.ds(chip // 2, 1), :]
        row = jnp.broadcast_to(lax.select(chip % 2 == 0, row[:, 0:LANES], row[:, LANES:]), (TAIL, LANES))
        for half in range(2):
            rows = z[half * HALF:(half + 1) * HALF]
            mean = jnp.sum(rows, axis=0, keepdims=True) * (1.0 / HALF)
            rows = (rows - mean).astype(BF16)
            out_ref[half, layer, 0:HALF] = rows[:, 0:LANES]
            out_ref[half, layer, HALF:2 * HALF] = rows[:, LANES:]
            high = mean.astype(BF16).astype(F32)
            terms = [part[:, at:at + LANES] for part in (high, mean - high) for at in (0, LANES)]
            tail = row
            for at, term in enumerate(terms):
                tail = jnp.where(at_row == at, term, tail)
            out_ref[half, layer, 2 * HALF:] = tail.astype(BF16)
    for copy in copies:
        copy.wait()


def gram_kernel(j_ref, x_ref, keep_ref, send_ref, tail_ref, par_ref, zc_ref):
    core = j_ref[0] % 2
    means = []
    for g in range(2):
        tails = x_ref[g, :, 2 * HALF:].astype(F32)
        mean = sum(jnp.concatenate([tails[:, at:at + 1], tails[:, at + 1:at + 2]], axis=2) for at in (0, 2))
        means.append(jnp.mean(mean, axis=0))
        rows = jnp.concatenate([x_ref[g, :, 0:HALF], x_ref[g, :, HALF:2 * HALF]], axis=2).astype(F32)
        zc_ref[g] = (rows + (mean - means[g][None])).astype(BF16).reshape(HOME, GW)
        packed = [jnp.concatenate([tails[2 * r, 6:7], tails[2 * r + 1, 6:7]], axis=1) for r in range(PROWS)]
        par_ref[g] = jnp.concatenate([packed[r] + packed[r + 4] for r in range(4)], axis=0)
    parts = [split3(mean) for mean in means]
    tail = [parts[g][term] for term in range(3) for g in range(2)]
    tail = jnp.concatenate(tail + [jnp.zeros((2, GW), F32)], axis=0).astype(BF16)
    tail_ref[...] = tail
    send_ref[4 * 3 * PIECE:] = tail
    for at, (a, b) in enumerate(((0, 0), (0, 1), (1, 1))):
        gram = lax.dot_general(zc_ref[a], zc_ref[b], (((0,), (0,)), ((), ())), preferred_element_type=F32)
        low, high = gram[0:GW // 2], gram[GW // 2:]
        keep, send = lax.select(core == 0, low, high), lax.select(core == 0, high, low).astype(BF16)
        for j in range(4):
            rows = pl.ds((3 * j + at) * PIECE, PIECE)
            keep_ref[rows] = keep[j * PIECE:(j + 1) * PIECE]
            send_ref[rows] = send[j * PIECE:(j + 1) * PIECE]


def chip_kernel(j_ref, keep_ref, tail_ref, got_ref, out_ref):
    core = j_ref[0] % 2
    tails = in_order(tail_ref[...], got_ref[4 * 3 * PIECE:], core)
    for j in range(4):
        rows = pl.ds(3 * j * PIECE, 3 * PIECE)
        out_ref[j, 0:3 * PIECE] = (keep_ref[rows] + got_ref[rows].astype(F32)).astype(BF16)
        out_ref[j, 3 * PIECE:] = tails


def mean_of(rows, g):
    return rows[..., g, :] + rows[..., 2 + g, :] + rows[..., 4 + g, :]


def all_means(r_ref):
    rows = r_ref[:, 3 * PIECE:].astype(F32)
    cores = rows[:, 0:TAIL], rows[:, TAIL:]
    return [jnp.concatenate([mean_of(core, g) for core in cores], axis=0) for g in range(2)]


def deviation_kernel(j_ref, r_ref, par_ref, e_ref, scratch_ref):
    row_at = (j_ref[0] % 2 * 4 + j_ref[0] // 2) * PIECE
    means = all_means(r_ref)
    shifted = [m - jnp.mean(m, axis=0, keepdims=True) for m in means]
    total = jnp.sum(r_ref[:, 0:3 * PIECE].astype(F32), axis=0) * (1.0 / TOTAL)
    diagonal = (
        lax.broadcasted_iota(jnp.int32, (PIECE, GW), 0) + row_at
        == lax.broadcasted_iota(jnp.int32, (PIECE, GW), 1)
    )
    for at, (a, b) in enumerate(((0, 0), (0, 1), (1, 1))):
        scratch_ref[...] = lax.dot_general(
            shifted[a], shifted[b], (((0,), (0,)), ((), ())), precision=HIGHEST, preferred_element_type=F32
        )
        part = total[at * PIECE:(at + 1) * PIECE] + scratch_ref[pl.ds(row_at, PIECE), :] * (1.0 / PARTS)
        if a == b:
            part = part - jnp.where(diagonal, par_ref[a, 3:4], 0.0)
        for j in range(4):
            e_ref[j, at * PIECE:(at + 1) * PIECE] = part.astype(BF16)


def pull_kernel(e_ref, r_ref, tail_ref, par_ref, zc_ref, out_ref):
    means = all_means(r_ref)
    mine = tail_ref[...].astype(F32)
    mats = [e_ref[:, :, at * PIECE:(at + 1) * PIECE].reshape(GW, GW) for at in range(3)]
    whole = [m.astype(F32) for m in mats]
    loss = 0.25 * (
        jnp.sum(whole[0] * whole[0], keepdims=True)
        + 2.0 * jnp.sum(whole[1] * whole[1], keepdims=True)
        + jnp.sum(whole[2] * whole[2], keepdims=True)
    )
    away, offset = [], []
    for g in range(2):
        mean = jnp.mean(means[g], axis=0, keepdims=True)
        gap = mean - par_ref[g, 2:3]
        loss = loss + jnp.sum(gap * gap, keepdims=True)
        away.append(2.0 * gap)
        own = mine[g:g + 1] + mine[2 + g:3 + g] + mine[4 + g:5 + g]
        offset.append(jnp.concatenate(list(split3(own - mean)) + [jnp.zeros((13, GW), F32)], axis=0).astype(BF16))
    tail = [jnp.broadcast_to(part, (1, LANES)) for part in split3(loss)]
    tail = jnp.concatenate(tail + [jnp.zeros((TAIL - 3, LANES), F32)], axis=0).astype(BF16)
    tail = jnp.broadcast_to(tail[None], (CHIPS, TAIL, LANES))
    plain, crossed = (((1,), (0,)), ((), ())), (((1,), (1,)), ((), ()))

    def product(side, at, dims):
        lhs = jnp.concatenate([zc_ref[side], offset[side]], axis=0)
        return lax.dot_general(lhs, mats[at], dims, preferred_element_type=F32)

    for g in range(2):
        pull = product(0, 0, plain) + product(1, 1, crossed) if g == 0 else product(0, 1, plain) + product(1, 2, plain)
        row = pull[HOME:HOME + 1] + pull[HOME + 1:HOME + 2] + pull[HOME + 2:HOME + 3] + away[g]
        pull = pull[0:HOME] + row
        pull = pull.astype(BF16).reshape(CHIPS, HALF, GW)
        out_ref[g, :, 0:HALF] = pull[:, :, 0:LANES]
        out_ref[g, :, HALF:2 * HALF] = pull[:, :, LANES:]
        out_ref[g, :, 2 * HALF:] = tail


def backward_kernel(q_ref, w_in, slope_in, out_ref, w_ref, slope_ref, sems):
    copies = [None] * LAYERS
    for layer in reversed(range(LAYERS)):
        copies[layer] = [pltpu.make_async_copy(w_in.at[layer], w_ref.at[layer], sems.at[0, layer])]
        if layer < LAYERS - 1:
            copies[layer].append(pltpu.make_async_copy(slope_in.at[layer], slope_ref.at[layer], sems.at[1, layer]))
        for copy in copies[layer]:
            copy.start()
    loss = jnp.zeros((1, LANES), F32)
    grad = None
    for layer in reversed(range(LAYERS)):
        rows = q_ref[0, layer, 2 * HALF:].astype(F32)
        loss = loss + (rows[0:1] + rows[1:2] + rows[2:3])
        pull = jnp.concatenate(
            [q_ref[:, layer, 0:HALF].reshape(ROWS, LANES), q_ref[:, layer, HALF:2 * HALF].reshape(ROWS, LANES)], axis=1
        )
        for copy in copies[layer]:
            copy.wait()
        if grad is not None:
            pull = (grad * slope_ref[layer].astype(F32) + pull.astype(F32)).astype(BF16)
        grad = lax.dot_general(
            pull, w_ref[layer].reshape(GW, GW), (((1,), (1,)), ((), ())), preferred_element_type=F32
        ).astype(BF16).astype(F32)
    loss = jnp.concatenate([loss, loss], axis=1)
    tail = jnp.concatenate(list(split3(loss)) + [jnp.zeros((TAIL - 3, GW), F32)], axis=0).astype(BF16)
    grad = grad.astype(BF16)
    for strip in range(8):
        slot = strip % 2 * 4 + strip // 2
        out_ref[slot, 0:16] = grad[strip * 16:strip * 16 + 16]
        out_ref[slot, 16:16 + TAIL] = tail


def output_kernel(r_ref, grad_ref, loss_ref):
    loss = jnp.zeros((1, 1), F32)
    for k in range(BLOCKS):
        for g in range(2):
            at = 2 * k + g
            grad_ref[0, :, at * GW:(at + 1) * GW] = r_ref[4 * g + k, 0:16]
        loss = loss + jnp.sum(r_ref[k, 16:16 + TAIL].astype(F32)[0:3, 0:1], axis=0, keepdims=True)
    loss_ref[...] = loss * (1.0 / (LAYERS * BLOCKS * 2 * GW))


LARGE = 1200000


def is_large(shape, dtype):
    return math.prod(shape) * jnp.dtype(dtype).itemsize > LARGE


def kernel_call(kernel, outs, name, *args, scalars=(), scratch=(), far=(), loose=()):
    vmem = pl.BlockSpec(memory_space=pltpu.VMEM)
    smem = pl.BlockSpec(memory_space=pltpu.SMEM)
    placed = [arg if is_large(arg.shape, arg.dtype) else pltpu.with_memory_space_constraint(arg, pltpu.VMEM) for arg in args]
    placed += [pltpu.with_memory_space_constraint(arg, pltpu.HBM) for arg in far]
    return pl.pallas_call(
        kernel,
        out_shape=[jax.ShapeDtypeStruct(*out) if is_large(*out) else pltpu.VMEM(*out) for out in outs] + list(loose),
        in_specs=[smem] * len(scalars) + [vmem] * len(placed),
        out_specs=[vmem] * (len(outs) + len(loose)),
        scratch_shapes=list(scratch),
        name=name,
    )(*scalars, *placed)


def shards(images, weights, bn_mean, bn_var, bn_gain, bn_bias):
    part = lax.axis_index(("g", "h", "c")).astype(jnp.int32).reshape(1)

    hbm, vmem = pl.BlockSpec(memory_space=pl.ANY), pl.BlockSpec(memory_space=pltpu.VMEM)
    message, rows = pl.pallas_call(
        pack_kernel,
        out_shape=[pltpu.VMEM((4, 2, 2, SLICE + PROWS, GW), BF16), pltpu.VMEM((ROWS, GW), BF16)],
        in_specs=[hbm] * 6,
        out_specs=[vmem, vmem],
        scratch_shapes=[pltpu.VMEM((2 * BLOCKS, SLICE, GW), BF16)]
        + [pltpu.VMEM((1, 2 * BLOCKS * GW), F32)] * 4
        + [pltpu.SemaphoreType.DMA((9,))],
        name="pack",
    )(weights, images, bn_mean, bn_var, bn_gain, bn_bias)
    message = message.reshape(LAYERS, SLICE + PROWS, GW)
    layer_parts = lax.all_to_all(message, ("k", "h", "g"), 0, 0, tiled=True)

    own = layer_parts[:, 0:SLICE]
    own = lax.all_to_all(jnp.broadcast_to(own[None], (CHIPS, LAYERS, SLICE, GW)), ("y", "x"), 0, 0, tiled=True)
    other = lax.ppermute(own, "c", [(0, 1), (1, 0)])

    def near(array):
        return pltpu.with_memory_space_constraint(array, pltpu.VMEM)

    layers = [pltpu.VMEM((LAYERS, 2, CHIPS, SLICE, GW), BF16), pltpu.VMEM((LAYERS, ROWS, GW), BF16)]
    xs, chain_weights, slope = pl.pallas_call(
        forward_kernel,
        out_shape=[
            pltpu.VMEM((2, LAYERS, 2 * HALF + TAIL, LANES), BF16),
            jax.ShapeDtypeStruct((LAYERS, 2, CHIPS, SLICE, GW), BF16),
            jax.ShapeDtypeStruct((LAYERS, ROWS, GW), BF16),
        ],
        in_specs=[vmem, vmem, hbm, vmem],
        out_specs=[vmem, hbm, hbm],
        scratch_shapes=layers + [pltpu.VMEM((LAYERS, PROWS, GW), F32), pltpu.SemaphoreType.DMA((4, LAYERS))],
        name="fwd",
    )(near(rows), near(layer_parts), own, near(other))

    home = lax.all_to_all(xs.reshape(2 * CHIPS, 2 * HALF + TAIL, LANES), ("g", "y", "x"), 0, 0, tiled=True)
    keep, send, tail, params, centered = kernel_call(
        gram_kernel,
        [
            ((4 * 3 * PIECE, GW), F32),
            ((4 * 3 * PIECE + TAIL, GW), BF16),
            ((TAIL, GW), BF16),
            ((2, 4, GW), F32),
        ],
        "gram",
        home.reshape(2, CHIPS, 2 * HALF + TAIL, LANES),
        scalars=[part],
        loose=[jax.ShapeDtypeStruct((2, HOME, GW), BF16)],
    )
    got = lax.ppermute(send, "c", [(0, 1), (1, 0)])
    (pieces,) = kernel_call(
        chip_kernel, [((4, 3 * PIECE + 2 * TAIL, GW), BF16)], "chip", keep, tail, got, scalars=[part]
    )
    pieces = lax.all_to_all(pieces, ("g", "h"), 0, 0, tiled=True)
    (deviation,) = kernel_call(
        deviation_kernel,
        [((4, 3 * PIECE, GW), BF16)],
        "deviation",
        pieces,
        params,
        scalars=[part],
        scratch=[pltpu.VMEM((GW, GW), F32)],
    )
    deviation = lax.all_gather(lax.all_to_all(deviation, ("g", "h"), 0, 0, tiled=True), "c", axis=0)
    (pulls,) = kernel_call(
        pull_kernel,
        [((2, CHIPS, 2 * HALF + TAIL, LANES), BF16)],
        "pull",
        deviation,
        pieces,
        tail,
        params,
        far=[centered],
    )
    pulls = lax.all_to_all(pulls.reshape(2 * CHIPS, 2 * HALF + TAIL, LANES), ("g", "y", "x"), 0, 0, tiled=True)

    grads = pl.pallas_call(
        backward_kernel,
        out_shape=pltpu.VMEM((8, 16 + TAIL, GW), BF16),
        in_specs=[vmem, hbm, hbm],
        out_specs=vmem,
        scratch_shapes=layers + [pltpu.SemaphoreType.DMA((2, LAYERS))],
        name="bwd",
    )(near(pulls.reshape(2, LAYERS, 2 * HALF + TAIL, LANES)), chain_weights, slope)
    grads = lax.all_to_all(grads, ("g", "k"), 0, 0, tiled=True)
    image_grad, loss = pl.pallas_call(
        output_kernel,
        out_shape=[jax.ShapeDtypeStruct((1, 16, BLOCKS * 2 * GW), BF16), jax.ShapeDtypeStruct((1, 1), F32)],
        in_specs=[vmem],
        out_specs=[vmem, vmem],
        name="outputs",
    )(near(grads))
    return image_grad, loss.reshape(())


def solution(mesh):
    fine = Mesh(np.asarray(mesh.devices).reshape(4, 2, 2, 4, 4, 2), ("k", "h", "g", "x", "y", "c"))
    batch, section = ("x", "y", "c"), ("k", "h", "g")
    return jax.shard_map(
        shards,
        mesh=fine,
        in_specs=(
            P(batch, None, None),
            P(section, None, None, None),
            P(section, None),
            P(section, None),
            P(section, None),
            P(section, None),
        ),
        out_specs=(P(batch, section, None), P()),
        check_vma=False,
    )
```

```python
import math

import jax
import jax.numpy as jnp
import numpy as np
from jax import lax
from jax.experimental import pallas as pl
from jax.experimental.pallas import tpu as pltpu
from jax.sharding import Mesh, PartitionSpec as P

EPS = 1e-05
LOG2E = math.log2(math.e)
F32 = jnp.float32
BF16 = jnp.bfloat16

LAYERS = 16
GW = 256
BLOCKS = 3
CHIPS = 16
SLICE = GW // (2 * CHIPS)
PROWS = 8
ROWS = 128
HALF = ROWS // 2
HOME = CHIPS * HALF
LANES = 128
PARTS = 8
PIECE = GW // PARTS
TAIL = 8
TOTAL = HOME * PARTS


def split3(value):
    high = value.astype(BF16).astype(F32)
    rest = value - high
    middle = rest.astype(BF16).astype(F32)
    return high, middle, rest - middle


def pack_kernel(w_ref, images_ref, *refs):
    inputs, (out_ref, x_ref, slab_ref), held, sems = refs[:4], refs[4:7], refs[7:11], refs[11]
    reads = [pltpu.make_async_copy(source, target, sems.at[5 + at]) for at, (source, target) in enumerate(zip(inputs, held))]
    for copy in reads:
        copy.start()
    mean_ref, var_ref, gain_ref, bias_ref = held
    chip = lax.axis_index("y") * 4 + lax.axis_index("x")
    row = (lax.axis_index("c") * CHIPS + chip) * SLICE
    half = lax.axis_index("h")
    group = 2 * jnp.minimum(lax.axis_index("k"), BLOCKS - 1) + lax.axis_index("g")
    slab = pltpu.make_async_copy(w_ref.at[0, :, pl.ds(pl.multiple_of(row, SLICE), SLICE), :], slab_ref, sems.at[0])
    slab.start()
    copies = []
    for strip in range(4):
        source = images_ref.at[
            0, pl.ds(pl.multiple_of(strip * 64 + half * 32, 32), 32), pl.ds(pl.multiple_of(group * GW, GW), GW)
        ]
        copies.append(pltpu.make_async_copy(source, x_ref.at[strip * 32:strip * 32 + 32], sems.at[1 + strip]))
        copies[-1].start()
    for copy in reads:
        copy.wait()
    scale = gain_ref[...] * lax.rsqrt(var_ref[...] + EPS)
    packed = [scale, bias_ref[...] - mean_ref[...] * scale, mean_ref[...], var_ref[...]]
    high = [value.astype(BF16).astype(F32) for value in packed]
    packed = jnp.concatenate(high + [value - top for value, top in zip(packed, high)], axis=0).astype(BF16)
    slab.wait()
    for k in range(4):
        for g in range(2):
            at = 2 * min(k, BLOCKS - 1) + g
            for h in range(2):
                out_ref[k, h, g, 0:SLICE] = slab_ref[at]
                out_ref[k, h, g, SLICE:] = packed[:, at * GW:(at + 1) * GW]
    for copy in copies:
        copy.wait()


def in_order(own, other, core):
    return jnp.concatenate([lax.select(core == 0, own, other), lax.select(core == 0, other, own)], axis=0)


FIRST = 4


def weight_reads(own_in, other_in, w_ref, core, sems, layer):
    return [
        pltpu.make_async_copy(own_in.at[:, layer], w_ref.at[layer, core], sems.at[0, layer]),
        pltpu.make_async_copy(other_in.at[:, layer], w_ref.at[layer, 1 - core], sems.at[1, layer]),
    ]


def forward_kernel(
    x_ref, par_ref, own_in, other_in, xs_out, slope_out, w_ref, slope_ref, rows_ref, z_ref, xs_ref, sems, out_sems
):
    core = lax.axis_index("c")
    chip = lax.axis_index("y") * 4 + lax.axis_index("x")
    arrivals = [weight_reads(own_in, other_in, w_ref, core, sems, layer) for layer in range(LAYERS)]
    for copy in sum(arrivals, []):
        copy.start()
    for layer in range(LAYERS):
        rows_ref[layer] = par_ref[layer, SLICE:SLICE + PROWS].astype(F32)
    at_row = lax.broadcasted_iota(jnp.int32, (TAIL, LANES), 0)

    def pack_layer(layer):
        row = rows_ref[layer, pl.ds(chip // 2, 1), :]
        row = jnp.broadcast_to(lax.select(chip % 2 == 0, row[:, 0:LANES], row[:, LANES:]), (TAIL, LANES))
        for half in range(2):
            rows = z_ref[layer, half * HALF:(half + 1) * HALF]
            mean = jnp.sum(rows, axis=0, keepdims=True) * (1.0 / HALF)
            rows = (rows - mean).astype(BF16)
            xs_ref[half, layer, 0:HALF] = rows[:, 0:LANES]
            xs_ref[half, layer, HALF:2 * HALF] = rows[:, LANES:]
            high = mean.astype(BF16).astype(F32)
            terms = [part[:, at:at + LANES] for part in (high, mean - high) for at in (0, LANES)]
            tail = row
            for at, term in enumerate(terms):
                tail = jnp.where(at_row == at, term, tail)
            xs_ref[half, layer, 2 * HALF:] = tail.astype(BF16)

    writes = []

    def write(first, last):
        span = pl.ds(first, last - first)
        at = len(writes)
        writes.append(pltpu.make_async_copy(xs_ref.at[:, span], xs_out.at[:, span], out_sems.at[at]))
        writes.append(pltpu.make_async_copy(slope_ref.at[span], slope_out.at[span], out_sems.at[at + 1]))
        for copy in writes[-2:]:
            copy.start()

    x = x_ref[...]
    for layer in range(LAYERS):
        if layer in (0, FIRST):
            for copy in sum(arrivals[0:FIRST] if layer == 0 else arrivals[FIRST:], []):
                copy.wait()
        z = jnp.dot(x, w_ref[layer].reshape(GW, GW), preferred_element_type=F32)
        z_ref[layer] = z
        if layer > 0:
            pack_layer(layer - 1)
        scale = rows_ref[layer, 0:1] + rows_ref[layer, 4:5]
        shift = rows_ref[layer, 1:2] + rows_ref[layer, 5:6]
        active = z * scale + shift
        gate = 1.0 / (1.0 + jnp.exp2(active * -LOG2E))
        after = active * gate
        x = after.astype(BF16)
        slope_ref[layer] = (gate * ((active - after) + 1.0) * scale).astype(BF16)
        if layer == LAYERS // 2:
            write(0, LAYERS // 2)
    pack_layer(LAYERS - 1)
    write(LAYERS // 2, LAYERS)
    for copy in writes:
        copy.wait()


def gram_kernel(j_ref, x_ref, keep_ref, send_ref, tail_ref, par_ref, zc_ref):
    core = j_ref[0] % 2
    means = []
    for g in range(2):
        tails = x_ref[g, :, 2 * HALF:].astype(F32)
        mean = sum(jnp.concatenate([tails[:, at:at + 1], tails[:, at + 1:at + 2]], axis=2) for at in (0, 2))
        means.append(jnp.mean(mean, axis=0))
        rows = jnp.concatenate([x_ref[g, :, 0:HALF], x_ref[g, :, HALF:2 * HALF]], axis=2).astype(F32)
        zc_ref[g] = (rows + (mean - means[g][None])).astype(BF16).reshape(HOME, GW)
        packed = [jnp.concatenate([tails[2 * r, 6:7], tails[2 * r + 1, 6:7]], axis=1) for r in range(PROWS)]
        par_ref[g] = jnp.concatenate([packed[r] + packed[r + 4] for r in range(4)], axis=0)
    parts = [split3(mean) for mean in means]
    tail = [parts[g][term] for term in range(3) for g in range(2)]
    tail = jnp.concatenate(tail + [jnp.zeros((2, GW), F32)], axis=0).astype(BF16)
    tail_ref[...] = tail
    send_ref[4 * 3 * PIECE:] = tail
    for at, (a, b) in enumerate(((0, 0), (0, 1), (1, 1))):
        gram = lax.dot_general(zc_ref[a], zc_ref[b], (((0,), (0,)), ((), ())), preferred_element_type=F32)
        low, high = gram[0:GW // 2], gram[GW // 2:]
        keep, send = lax.select(core == 0, low, high), lax.select(core == 0, high, low).astype(BF16)
        for j in range(4):
            rows = pl.ds((3 * j + at) * PIECE, PIECE)
            keep_ref[rows] = keep[j * PIECE:(j + 1) * PIECE]
            send_ref[rows] = send[j * PIECE:(j + 1) * PIECE]


def chip_kernel(j_ref, keep_ref, tail_ref, got_ref, out_ref):
    core = j_ref[0] % 2
    tails = in_order(tail_ref[...], got_ref[4 * 3 * PIECE:], core)
    for j in range(4):
        rows = pl.ds(3 * j * PIECE, 3 * PIECE)
        out_ref[j, 0:3 * PIECE] = (keep_ref[rows] + got_ref[rows].astype(F32)).astype(BF16)
        out_ref[j, 3 * PIECE:] = tails


def mean_of(rows, g):
    return rows[..., g, :] + rows[..., 2 + g, :] + rows[..., 4 + g, :]


def all_means(r_ref):
    rows = r_ref[:, 3 * PIECE:].astype(F32)
    cores = rows[:, 0:TAIL], rows[:, TAIL:]
    return [jnp.concatenate([mean_of(core, g) for core in cores], axis=0) for g in range(2)]


def deviation_kernel(j_ref, r_ref, par_ref, e_ref, scratch_ref):
    row_at = (j_ref[0] % 2 * 4 + j_ref[0] // 2) * PIECE
    means = all_means(r_ref)
    shifted = [m - jnp.mean(m, axis=0, keepdims=True) for m in means]
    highs = [m.astype(BF16).astype(F32) for m in shifted]
    lows = [m - high for m, high in zip(shifted, highs)]
    spare = jnp.zeros((PARTS, GW), F32)
    firsts = [jnp.concatenate([high, high, low, spare], axis=0).astype(BF16) for high, low in zip(highs, lows)]
    seconds = [jnp.concatenate([high, low, high, spare], axis=0).astype(BF16) for high, low in zip(highs, lows)]
    total = jnp.sum(r_ref[:, 0:3 * PIECE].astype(F32), axis=0) * (1.0 / TOTAL)
    diagonal = (
        lax.broadcasted_iota(jnp.int32, (PIECE, GW), 0) + row_at
        == lax.broadcasted_iota(jnp.int32, (PIECE, GW), 1)
    )
    for at, (a, b) in enumerate(((0, 0), (0, 1), (1, 1))):
        scratch_ref[...] = lax.dot_general(
            firsts[a], seconds[b], (((0,), (0,)), ((), ())), preferred_element_type=F32
        )
        part = total[at * PIECE:(at + 1) * PIECE] + scratch_ref[pl.ds(row_at, PIECE), :] * (1.0 / PARTS)
        if a == b:
            part = part - jnp.where(diagonal, par_ref[a, 3:4], 0.0)
        for j in range(4):
            e_ref[j, at * PIECE:(at + 1) * PIECE] = part.astype(BF16)


def pull_kernel(e_ref, r_ref, tail_ref, par_ref, zc_ref, out_ref):
    means = all_means(r_ref)
    mine = tail_ref[...].astype(F32)
    mats = [e_ref[:, :, at * PIECE:(at + 1) * PIECE].reshape(GW, GW) for at in range(3)]
    whole = [m.astype(F32) for m in mats]
    loss = 0.25 * (
        jnp.sum(whole[0] * whole[0], keepdims=True)
        + 2.0 * jnp.sum(whole[1] * whole[1], keepdims=True)
        + jnp.sum(whole[2] * whole[2], keepdims=True)
    )
    away, offset = [], []
    for g in range(2):
        mean = jnp.mean(means[g], axis=0, keepdims=True)
        gap = mean - par_ref[g, 2:3]
        loss = loss + jnp.sum(gap * gap, keepdims=True)
        away.append(2.0 * gap)
        own = mine[g:g + 1] + mine[2 + g:3 + g] + mine[4 + g:5 + g]
        offset.append(jnp.concatenate(list(split3(own - mean)) + [jnp.zeros((13, GW), F32)], axis=0).astype(BF16))
    tail = [jnp.broadcast_to(part, (1, LANES)) for part in split3(loss)]
    tail = jnp.concatenate(tail + [jnp.zeros((TAIL - 3, LANES), F32)], axis=0).astype(BF16)
    tail = jnp.broadcast_to(tail[None], (CHIPS, TAIL, LANES))
    plain, crossed = (((1,), (0,)), ((), ())), (((1,), (1,)), ((), ()))

    def product(side, at, dims):
        lhs = jnp.concatenate([zc_ref[side], offset[side]], axis=0)
        return lax.dot_general(lhs, mats[at], dims, preferred_element_type=F32)

    for g in range(2):
        pull = product(0, 0, plain) + product(1, 1, crossed) if g == 0 else product(0, 1, plain) + product(1, 2, plain)
        row = pull[HOME:HOME + 1] + pull[HOME + 1:HOME + 2] + pull[HOME + 2:HOME + 3] + away[g]
        pull = pull[0:HOME] + row
        pull = pull.astype(BF16).reshape(CHIPS, HALF, GW)
        out_ref[g, :, 0:HALF] = pull[:, :, 0:LANES]
        out_ref[g, :, HALF:2 * HALF] = pull[:, :, LANES:]
        out_ref[g, :, 2 * HALF:] = tail


def backward_kernel(q_ref, own_in, other_in, slope_in, out_ref, w_ref, slope_ref, sems, slope_sem):
    core = lax.axis_index("c")
    arrivals = [weight_reads(own_in, other_in, w_ref, core, sems, layer) for layer in range(LAYERS)]
    parts = [pl.ds(LAYERS - FIRST, FIRST), pl.ds(0, LAYERS - FIRST)]
    slopes = [pltpu.make_async_copy(slope_in.at[at], slope_ref.at[at], slope_sem.at[n]) for n, at in enumerate(parts)]
    arrivals = [sum(arrivals[LAYERS - FIRST:], []) + slopes[:1], sum(arrivals[:LAYERS - FIRST], []) + slopes[1:]]
    for copy in arrivals[0] + arrivals[1]:
        copy.start()
    loss = jnp.zeros((1, LANES), F32)
    grad = None
    for layer in reversed(range(LAYERS)):
        rows = q_ref[0, layer, 2 * HALF:].astype(F32)
        loss = loss + (rows[0:1] + rows[1:2] + rows[2:3])
        pull = jnp.concatenate(
            [q_ref[:, layer, 0:HALF].reshape(ROWS, LANES), q_ref[:, layer, HALF:2 * HALF].reshape(ROWS, LANES)], axis=1
        )
        if layer in (LAYERS - 1, LAYERS - 1 - FIRST):
            for copy in arrivals[0 if layer == LAYERS - 1 else 1]:
                copy.wait()
        if grad is not None:
            pull = (grad * slope_ref[layer].astype(F32) + pull.astype(F32)).astype(BF16)
        grad = lax.dot_general(
            pull, w_ref[layer].reshape(GW, GW), (((1,), (1,)), ((), ())), preferred_element_type=F32
        ).astype(BF16).astype(F32)
    loss = jnp.concatenate([loss, loss], axis=1)
    tail = jnp.concatenate(list(split3(loss)) + [jnp.zeros((TAIL - 3, GW), F32)], axis=0).astype(BF16)
    grad = grad.astype(BF16)
    for strip in range(8):
        slot = strip % 2 * 4 + strip // 2
        out_ref[slot, 0:16] = grad[strip * 16:strip * 16 + 16]
        out_ref[slot, 16:16 + TAIL] = tail


def output_kernel(r_ref, grad_ref, loss_ref):
    loss = jnp.zeros((1, 1), F32)
    for k in range(BLOCKS):
        for g in range(2):
            at = 2 * k + g
            grad_ref[0, :, at * GW:(at + 1) * GW] = r_ref[4 * g + k, 0:16]
        loss = loss + jnp.sum(r_ref[k, 16:16 + TAIL].astype(F32)[0:3, 0:1], axis=0, keepdims=True)
    loss_ref[...] = loss * (1.0 / (LAYERS * BLOCKS * 2 * GW))


LARGE = 1200000


def is_large(shape, dtype):
    return math.prod(shape) * jnp.dtype(dtype).itemsize > LARGE


def kernel_call(kernel, outs, name, *args, scalars=(), scratch=(), far=(), loose=()):
    vmem = pl.BlockSpec(memory_space=pltpu.VMEM)
    smem = pl.BlockSpec(memory_space=pltpu.SMEM)
    placed = [arg if is_large(arg.shape, arg.dtype) else pltpu.with_memory_space_constraint(arg, pltpu.VMEM) for arg in args]
    placed += [pltpu.with_memory_space_constraint(arg, pltpu.HBM) for arg in far]
    return pl.pallas_call(
        kernel,
        out_shape=[jax.ShapeDtypeStruct(*out) if is_large(*out) else pltpu.VMEM(*out) for out in outs] + list(loose),
        in_specs=[smem] * len(scalars) + [vmem] * len(placed),
        out_specs=[vmem] * (len(outs) + len(loose)),
        scratch_shapes=list(scratch),
        name=name,
    )(*scalars, *placed)


def shards(images, weights, bn_mean, bn_var, bn_gain, bn_bias):
    part = lax.axis_index(("g", "h", "c")).astype(jnp.int32).reshape(1)

    hbm, vmem = pl.BlockSpec(memory_space=pl.ANY), pl.BlockSpec(memory_space=pltpu.VMEM)
    message, rows = pl.pallas_call(
        pack_kernel,
        out_shape=[pltpu.VMEM((4, 2, 2, SLICE + PROWS, GW), BF16), pltpu.VMEM((ROWS, GW), BF16)],
        in_specs=[hbm] * 6,
        out_specs=[vmem, vmem],
        scratch_shapes=[pltpu.VMEM((2 * BLOCKS, SLICE, GW), BF16)]
        + [pltpu.VMEM((1, 2 * BLOCKS * GW), F32)] * 4
        + [pltpu.SemaphoreType.DMA((9,))],
        name="pack",
    )(weights, images, bn_mean, bn_var, bn_gain, bn_bias)
    message = message.reshape(LAYERS, SLICE + PROWS, GW)
    layer_parts = lax.all_to_all(message, ("k", "h", "g"), 0, 0, tiled=True)

    own = layer_parts[:, 0:SLICE]
    own = lax.all_to_all(jnp.broadcast_to(own[None], (CHIPS, LAYERS, SLICE, GW)), ("y", "x"), 0, 0, tiled=True)
    other = lax.ppermute(own, "c", [(0, 1), (1, 0)])

    def near(array):
        return pltpu.with_memory_space_constraint(array, pltpu.VMEM)

    layers = [pltpu.VMEM((LAYERS, 2, CHIPS, SLICE, GW), BF16), pltpu.VMEM((LAYERS, ROWS, GW), BF16)]
    sems = pltpu.SemaphoreType.DMA((2, LAYERS))
    pieces_shape = (2, LAYERS, 2 * HALF + TAIL, LANES)
    xs, slope = pl.pallas_call(
        forward_kernel,
        out_shape=[jax.ShapeDtypeStruct(pieces_shape, BF16), jax.ShapeDtypeStruct((LAYERS, ROWS, GW), BF16)],
        in_specs=[vmem, vmem, hbm, vmem],
        out_specs=[hbm, hbm],
        scratch_shapes=layers
        + [pltpu.VMEM((LAYERS, PROWS, GW), F32), pltpu.VMEM((LAYERS, ROWS, GW), F32), pltpu.VMEM(pieces_shape, BF16)]
        + [sems, pltpu.SemaphoreType.DMA((4,))],
        name="fwd",
    )(near(rows), near(layer_parts), own, near(other))

    home = lax.all_to_all(xs.reshape(2 * CHIPS, 2 * HALF + TAIL, LANES), ("g", "y", "x"), 0, 0, tiled=True)
    keep, send, tail, params, centered = kernel_call(
        gram_kernel,
        [
            ((4 * 3 * PIECE, GW), F32),
            ((4 * 3 * PIECE + TAIL, GW), BF16),
            ((TAIL, GW), BF16),
            ((2, 4, GW), F32),
        ],
        "gram",
        home.reshape(2, CHIPS, 2 * HALF + TAIL, LANES),
        scalars=[part],
        loose=[jax.ShapeDtypeStruct((2, HOME, GW), BF16)],
    )
    got = lax.ppermute(send, "c", [(0, 1), (1, 0)])
    (pieces,) = kernel_call(
        chip_kernel, [((4, 3 * PIECE + 2 * TAIL, GW), BF16)], "chip", keep, tail, got, scalars=[part]
    )
    pieces = lax.all_to_all(pieces, ("g", "h"), 0, 0, tiled=True)
    (deviation,) = kernel_call(
        deviation_kernel,
        [((4, 3 * PIECE, GW), BF16)],
        "deviation",
        pieces,
        params,
        scalars=[part],
        scratch=[pltpu.VMEM((GW, GW), F32)],
    )
    deviation = lax.all_gather(lax.all_to_all(deviation, ("g", "h"), 0, 0, tiled=True), "c", axis=0)
    (pulls,) = kernel_call(
        pull_kernel,
        [((2, CHIPS, 2 * HALF + TAIL, LANES), BF16)],
        "pull",
        deviation,
        pieces,
        tail,
        params,
        far=[centered],
    )
    pulls = lax.all_to_all(pulls.reshape(2 * CHIPS, 2 * HALF + TAIL, LANES), ("g", "y", "x"), 0, 0, tiled=True)

    grads = pl.pallas_call(
        backward_kernel,
        out_shape=pltpu.VMEM((8, 16 + TAIL, GW), BF16),
        in_specs=[vmem, hbm, hbm, hbm],
        out_specs=vmem,
        scratch_shapes=layers + [sems, pltpu.SemaphoreType.DMA((2,))],
        name="bwd",
    )(near(pulls.reshape(2, LAYERS, 2 * HALF + TAIL, LANES)), own, other, slope)
    grads = lax.all_to_all(grads, ("g", "k"), 0, 0, tiled=True)
    image_grad, loss = pl.pallas_call(
        output_kernel,
        out_shape=[jax.ShapeDtypeStruct((1, 16, BLOCKS * 2 * GW), BF16), jax.ShapeDtypeStruct((1, 1), F32)],
        in_specs=[vmem],
        out_specs=[vmem, vmem],
        name="outputs",
    )(near(grads))
    return image_grad, loss.reshape(())


def solution(mesh):
    fine = Mesh(np.asarray(mesh.devices).reshape(4, 2, 2, 4, 4, 2), ("k", "h", "g", "x", "y", "c"))
    batch, section = ("x", "y", "c"), ("k", "h", "g")
    return jax.shard_map(
        shards,
        mesh=fine,
        in_specs=(
            P(batch, None, None),
            P(section, None, None, None),
            P(section, None),
            P(section, None),
            P(section, None),
            P(section, None),
        ),
        out_specs=(P(batch, section, None), P()),
        check_vma=False,
    )
```

```python
import math

import jax
import jax.numpy as jnp
import numpy as np
from jax import lax
from jax.experimental import pallas as pl
from jax.experimental.pallas import tpu as pltpu
from jax.sharding import Mesh, PartitionSpec as P

EPS = 1e-05
LOG2E = math.log2(math.e)
F32 = jnp.float32
BF16 = jnp.bfloat16

LAYERS = 16
GW = 256
BLOCKS = 3
CHIPS = 16
SLICE = GW // (2 * CHIPS)
PROWS = 8
ROWS = 128
HALF = ROWS // 2
HOME = CHIPS * HALF
LANES = 128
PARTS = 8
PIECE = GW // PARTS
TAIL = 8
TOTAL = HOME * PARTS


def split3(value):
    high = value.astype(BF16).astype(F32)
    rest = value - high
    middle = rest.astype(BF16).astype(F32)
    return high, middle, rest - middle


def pack_kernel(w_ref, images_ref, *refs):
    inputs, (out_ref, x_ref, slab_ref), held, sems = refs[:4], refs[4:7], refs[7:11], refs[11]
    reads = [pltpu.make_async_copy(source, target, sems.at[5 + at]) for at, (source, target) in enumerate(zip(inputs, held))]
    for copy in reads:
        copy.start()
    mean_ref, var_ref, gain_ref, bias_ref = held
    chip = lax.axis_index("y") * 4 + lax.axis_index("x")
    row = (lax.axis_index("c") * CHIPS + chip) * SLICE
    half = lax.axis_index("h")
    group = 2 * jnp.minimum(lax.axis_index("k"), BLOCKS - 1) + lax.axis_index("g")
    slab = pltpu.make_async_copy(w_ref.at[0, :, pl.ds(pl.multiple_of(row, SLICE), SLICE), :], slab_ref, sems.at[0])
    slab.start()
    copies = []
    for strip in range(4):
        source = images_ref.at[
            0, pl.ds(pl.multiple_of(strip * 64 + half * 32, 32), 32), pl.ds(pl.multiple_of(group * GW, GW), GW)
        ]
        copies.append(pltpu.make_async_copy(source, x_ref.at[strip * 32:strip * 32 + 32], sems.at[1 + strip]))
        copies[-1].start()
    for copy in reads:
        copy.wait()
    scale = gain_ref[...] * lax.rsqrt(var_ref[...] + EPS)
    packed = [scale, bias_ref[...] - mean_ref[...] * scale, mean_ref[...], var_ref[...]]
    high = [value.astype(BF16).astype(F32) for value in packed]
    packed = jnp.concatenate(high + [value - top for value, top in zip(packed, high)], axis=0).astype(BF16)
    slab.wait()
    for k in range(4):
        for g in range(2):
            at = 2 * min(k, BLOCKS - 1) + g
            for h in range(2):
                out_ref[k, h, g, 0:SLICE] = slab_ref[at]
                out_ref[k, h, g, SLICE:] = packed[:, at * GW:(at + 1) * GW]
    for copy in copies:
        copy.wait()


def in_order(own, other, core):
    return jnp.concatenate([lax.select(core == 0, own, other), lax.select(core == 0, other, own)], axis=0)


FIRST = 4


def weight_reads(own_in, other_in, w_ref, core, sems, layer):
    return [
        pltpu.make_async_copy(own_in.at[:, layer], w_ref.at[layer, core], sems.at[0, layer]),
        pltpu.make_async_copy(other_in.at[:, layer], w_ref.at[layer, 1 - core], sems.at[1, layer]),
    ]


def forward_kernel(
    x_ref, par_ref, own_in, other_in, xs_out, slope_out, w_ref, slope_ref, rows_ref, z_ref, xs_ref, sems, out_sems
):
    core = lax.axis_index("c")
    chip = lax.axis_index("y") * 4 + lax.axis_index("x")
    arrivals = [weight_reads(own_in, other_in, w_ref, core, sems, layer) for layer in range(LAYERS)]
    for copy in sum(arrivals, []):
        copy.start()
    for layer in range(LAYERS):
        rows_ref[layer] = par_ref[layer, SLICE:SLICE + PROWS].astype(F32)
    at_row = lax.broadcasted_iota(jnp.int32, (TAIL, LANES), 0)

    def pack_layer(layer):
        row = rows_ref[layer, pl.ds(chip // 2, 1), :]
        row = jnp.broadcast_to(lax.select(chip % 2 == 0, row[:, 0:LANES], row[:, LANES:]), (TAIL, LANES))
        for half in range(2):
            rows = z_ref[layer, half * HALF:(half + 1) * HALF]
            mean = jnp.sum(rows, axis=0, keepdims=True) * (1.0 / HALF)
            rows = (rows - mean).astype(BF16)
            xs_ref[half, layer, 0:HALF] = rows[:, 0:LANES]
            xs_ref[half, layer, HALF:2 * HALF] = rows[:, LANES:]
            high = mean.astype(BF16).astype(F32)
            terms = [part[:, at:at + LANES] for part in (high, mean - high) for at in (0, LANES)]
            tail = row
            for at, term in enumerate(terms):
                tail = jnp.where(at_row == at, term, tail)
            xs_ref[half, layer, 2 * HALF:] = tail.astype(BF16)

    writes = []

    def write(first, last):
        span = pl.ds(first, last - first)
        at = len(writes)
        writes.append(pltpu.make_async_copy(xs_ref.at[:, span], xs_out.at[:, span], out_sems.at[at]))
        writes.append(pltpu.make_async_copy(slope_ref.at[span], slope_out.at[span], out_sems.at[at + 1]))
        for copy in writes[-2:]:
            copy.start()

    x = x_ref[...]
    for layer in range(LAYERS):
        if layer in (0, FIRST):
            for copy in sum(arrivals[0:FIRST] if layer == 0 else arrivals[FIRST:], []):
                copy.wait()
        z = jnp.dot(x, w_ref[layer].reshape(GW, GW), preferred_element_type=F32)
        z_ref[layer] = z
        if layer > 0:
            pack_layer(layer - 1)
        scale = rows_ref[layer, 0:1] + rows_ref[layer, 4:5]
        shift = rows_ref[layer, 1:2] + rows_ref[layer, 5:6]
        active = z * scale + shift
        gate = 1.0 / (1.0 + jnp.exp2(z * (scale * -LOG2E) + shift * -LOG2E))
        after = active * gate
        x = after.astype(BF16)
        slope_ref[layer] = (gate * ((active - after) + 1.0) * scale).astype(BF16)
        if layer == LAYERS // 2:
            write(0, LAYERS // 2)
    pack_layer(LAYERS - 1)
    write(LAYERS // 2, LAYERS)
    for copy in writes:
        copy.wait()


def gram_kernel(x_ref, keep_ref, send_ref, tail_ref, par_ref, zc_out, zc_ref, sems):
    core = lax.axis_index("c")
    means, writes = [], []
    for g in range(2):
        tails = x_ref[g, :, 2 * HALF:].astype(F32)
        mean = sum(jnp.concatenate([tails[:, at:at + 1], tails[:, at + 1:at + 2]], axis=2) for at in (0, 2))
        means.append(jnp.mean(mean, axis=0))
        rows = jnp.concatenate([x_ref[g, :, 0:HALF], x_ref[g, :, HALF:2 * HALF]], axis=2).astype(F32)
        zc_ref[g] = (rows + (mean - means[g][None])).astype(BF16).reshape(HOME, GW)
        writes.append(pltpu.make_async_copy(zc_ref.at[g], zc_out.at[g], sems.at[g]))
        writes[g].start()
        packed = [jnp.concatenate([tails[2 * r, 6:7], tails[2 * r + 1, 6:7]], axis=1) for r in range(PROWS)]
        par_ref[g] = jnp.concatenate([packed[r] + packed[r + 4] for r in range(4)], axis=0)
    parts = [split3(mean) for mean in means]
    tail = [parts[g][term] for term in range(3) for g in range(2)]
    tail = jnp.concatenate(tail + [jnp.zeros((2, GW), F32)], axis=0).astype(BF16)
    tail_ref[...] = tail
    send_ref[4 * 3 * PIECE:] = tail
    for at, (a, b) in enumerate(((0, 0), (0, 1), (1, 1))):
        gram = lax.dot_general(zc_ref[a], zc_ref[b], (((0,), (0,)), ((), ())), preferred_element_type=F32)
        low, high = gram[0:GW // 2], gram[GW // 2:]
        keep, send = lax.select(core == 0, low, high), lax.select(core == 0, high, low).astype(BF16)
        for j in range(4):
            rows = pl.ds((3 * j + at) * PIECE, PIECE)
            keep_ref[rows] = keep[j * PIECE:(j + 1) * PIECE]
            send_ref[rows] = send[j * PIECE:(j + 1) * PIECE]
    for copy in writes:
        copy.wait()


def chip_kernel(j_ref, keep_ref, tail_ref, got_ref, out_ref):
    core = j_ref[0] % 2
    tails = in_order(tail_ref[...], got_ref[4 * 3 * PIECE:], core)
    for j in range(4):
        rows = pl.ds(3 * j * PIECE, 3 * PIECE)
        out_ref[j, 0:3 * PIECE] = (keep_ref[rows] + got_ref[rows].astype(F32)).astype(BF16)
        out_ref[j, 3 * PIECE:] = tails


def mean_of(rows, g):
    return rows[..., g, :] + rows[..., 2 + g, :] + rows[..., 4 + g, :]


def all_means(r_ref):
    rows = r_ref[:, 3 * PIECE:].astype(F32)
    cores = rows[:, 0:TAIL], rows[:, TAIL:]
    return [jnp.concatenate([mean_of(core, g) for core in cores], axis=0) for g in range(2)]


def deviation_kernel(j_ref, r_ref, par_ref, e_ref, scratch_ref):
    row_at = (j_ref[0] % 2 * 4 + j_ref[0] // 2) * PIECE
    means = all_means(r_ref)
    shifted = [m - jnp.mean(m, axis=0, keepdims=True) for m in means]
    highs = [m.astype(BF16).astype(F32) for m in shifted]
    lows = [m - high for m, high in zip(shifted, highs)]
    spare = jnp.zeros((PARTS, GW), F32)
    firsts = [jnp.concatenate([high, high, low, spare], axis=0).astype(BF16) for high, low in zip(highs, lows)]
    seconds = [jnp.concatenate([high, low, high, spare], axis=0).astype(BF16) for high, low in zip(highs, lows)]
    total = jnp.sum(r_ref[:, 0:3 * PIECE].astype(F32), axis=0) * (1.0 / TOTAL)
    diagonal = (
        lax.broadcasted_iota(jnp.int32, (PIECE, GW), 0) + row_at
        == lax.broadcasted_iota(jnp.int32, (PIECE, GW), 1)
    )
    for at, (a, b) in enumerate(((0, 0), (0, 1), (1, 1))):
        scratch_ref[...] = lax.dot_general(
            firsts[a], seconds[b], (((0,), (0,)), ((), ())), preferred_element_type=F32
        )
        part = total[at * PIECE:(at + 1) * PIECE] + scratch_ref[pl.ds(row_at, PIECE), :] * (1.0 / PARTS)
        if a == b:
            part = part - jnp.where(diagonal, par_ref[a, 3:4], 0.0)
        for j in range(4):
            e_ref[j, at * PIECE:(at + 1) * PIECE] = part.astype(BF16)


CHUNKS = 1


def pull_kernel(e_ref, r_ref, tail_ref, par_ref, zc_in, out_ref, zc_ref, sems):
    reads = []
    for n in range(CHUNKS):
        rows = pl.ds(n * (HOME // CHUNKS), HOME // CHUNKS)
        reads.append(pltpu.make_async_copy(zc_in.at[:, rows], zc_ref.at[:, rows], sems.at[n]))
        reads[n].start()
    means = all_means(r_ref)
    mine = tail_ref[...].astype(F32)
    mats = [e_ref[:, :, at * PIECE:(at + 1) * PIECE].reshape(GW, GW) for at in range(3)]
    whole = [m.astype(F32) for m in mats]
    loss = 0.25 * (
        jnp.sum(whole[0] * whole[0], keepdims=True)
        + 2.0 * jnp.sum(whole[1] * whole[1], keepdims=True)
        + jnp.sum(whole[2] * whole[2], keepdims=True)
    )
    away, offset = [], []
    for g in range(2):
        mean = jnp.mean(means[g], axis=0, keepdims=True)
        gap = mean - par_ref[g, 2:3]
        loss = loss + jnp.sum(gap * gap, keepdims=True)
        away.append(2.0 * gap)
        own = mine[g:g + 1] + mine[2 + g:3 + g] + mine[4 + g:5 + g]
        offset.append(jnp.concatenate(list(split3(own - mean)) + [jnp.zeros((13, GW), F32)], axis=0).astype(BF16))
    tail = [jnp.broadcast_to(part, (1, LANES)) for part in split3(loss)]
    tail = jnp.concatenate(tail + [jnp.zeros((TAIL - 3, LANES), F32)], axis=0).astype(BF16)
    tail = jnp.broadcast_to(tail[None], (CHIPS, TAIL, LANES))
    plain, crossed = (((1,), (0,)), ((), ())), (((1,), (1,)), ((), ()))

    def both(lhs, g):
        (at, first), (bt, second) = ((0, plain), (1, crossed)) if g == 0 else ((1, plain), (2, plain))
        return lax.dot_general(lhs[0], mats[at], first, preferred_element_type=F32) + lax.dot_general(
            lhs[1], mats[bt], second, preferred_element_type=F32
        )

    rows = []
    for g in range(2):
        row = both(offset, g)
        rows.append(row[0:1] + row[1:2] + row[2:3] + away[g])
    size = HOME // CHUNKS
    chips = CHIPS // CHUNKS
    for copy in reads:
        copy.wait()
    for n in range(CHUNKS):
        for g in range(2):
            pull = both([zc_ref[side, n * size:(n + 1) * size] for side in range(2)], g) + rows[g]
            pull = pull.astype(BF16).reshape(chips, HALF, GW)
            out_ref[g, n * chips:(n + 1) * chips, 0:HALF] = pull[:, :, 0:LANES]
            out_ref[g, n * chips:(n + 1) * chips, HALF:2 * HALF] = pull[:, :, LANES:]
    for g in range(2):
        out_ref[g, :, 2 * HALF:] = tail


def backward_kernel(q_ref, own_in, other_in, slope_in, out_ref, w_ref, slope_ref, sems, slope_sem):
    core = lax.axis_index("c")
    arrivals = [weight_reads(own_in, other_in, w_ref, core, sems, layer) for layer in range(LAYERS)]
    parts = [pl.ds(LAYERS - FIRST, FIRST), pl.ds(0, LAYERS - FIRST)]
    slopes = [pltpu.make_async_copy(slope_in.at[at], slope_ref.at[at], slope_sem.at[n]) for n, at in enumerate(parts)]
    arrivals = [sum(arrivals[LAYERS - FIRST:], []) + slopes[:1], sum(arrivals[:LAYERS - FIRST], []) + slopes[1:]]
    for copy in arrivals[0] + arrivals[1]:
        copy.start()
    loss = jnp.zeros((1, LANES), F32)
    grad = None
    for layer in reversed(range(LAYERS)):
        rows = q_ref[0, layer, 2 * HALF:].astype(F32)
        loss = loss + (rows[0:1] + rows[1:2] + rows[2:3])
        pull = jnp.concatenate(
            [q_ref[:, layer, 0:HALF].reshape(ROWS, LANES), q_ref[:, layer, HALF:2 * HALF].reshape(ROWS, LANES)], axis=1
        )
        if layer in (LAYERS - 1, LAYERS - 1 - FIRST):
            for copy in arrivals[0 if layer == LAYERS - 1 else 1]:
                copy.wait()
        if grad is not None:
            pull = (grad * slope_ref[layer].astype(F32) + pull.astype(F32)).astype(BF16)
        grad = lax.dot_general(
            pull, w_ref[layer].reshape(GW, GW), (((1,), (1,)), ((), ())), preferred_element_type=F32
        )
    loss = jnp.concatenate([loss, loss], axis=1)
    tail = jnp.concatenate(list(split3(loss)) + [jnp.zeros((TAIL - 3, GW), F32)], axis=0).astype(BF16)
    grad = grad.astype(BF16)
    for strip in range(8):
        slot = strip % 2 * 4 + strip // 2
        out_ref[slot, 0:16] = grad[strip * 16:strip * 16 + 16]
        out_ref[slot, 16:16 + TAIL] = tail


def output_kernel(r_ref, grad_ref, loss_ref):
    loss = jnp.zeros((1, 1), F32)
    for k in range(BLOCKS):
        for g in range(2):
            at = 2 * k + g
            grad_ref[0, :, at * GW:(at + 1) * GW] = r_ref[4 * g + k, 0:16]
        loss = loss + jnp.sum(r_ref[k, 16:16 + TAIL].astype(F32)[0:3, 0:1], axis=0, keepdims=True)
    loss_ref[...] = loss * (1.0 / (LAYERS * BLOCKS * 2 * GW))


def near(array):
    return pltpu.with_memory_space_constraint(array, pltpu.VMEM)


def kernel_call(kernel, outs, name, *args, scalars=(), scratch=()):
    vmem = pl.BlockSpec(memory_space=pltpu.VMEM)
    smem = pl.BlockSpec(memory_space=pltpu.SMEM)
    return pl.pallas_call(
        kernel,
        out_shape=[pltpu.VMEM(*out) for out in outs],
        in_specs=[smem] * len(scalars) + [vmem] * len(args),
        out_specs=[vmem] * len(outs),
        scratch_shapes=list(scratch),
        name=name,
    )(*scalars, *[near(arg) for arg in args])


def shards(images, weights, bn_mean, bn_var, bn_gain, bn_bias):
    part = lax.axis_index(("g", "h", "c")).astype(jnp.int32).reshape(1)

    hbm, vmem = pl.BlockSpec(memory_space=pl.ANY), pl.BlockSpec(memory_space=pltpu.VMEM)
    message, rows = pl.pallas_call(
        pack_kernel,
        out_shape=[pltpu.VMEM((4, 2, 2, SLICE + PROWS, GW), BF16), pltpu.VMEM((ROWS, GW), BF16)],
        in_specs=[hbm] * 6,
        out_specs=[vmem, vmem],
        scratch_shapes=[pltpu.VMEM((2 * BLOCKS, SLICE, GW), BF16)]
        + [pltpu.VMEM((1, 2 * BLOCKS * GW), F32)] * 4
        + [pltpu.SemaphoreType.DMA((9,))],
        name="pack",
    )(weights, images, bn_mean, bn_var, bn_gain, bn_bias)
    message = message.reshape(LAYERS, SLICE + PROWS, GW)
    layer_parts = lax.all_to_all(message, ("k", "h", "g"), 0, 0, tiled=True)

    own = layer_parts[:, 0:SLICE]
    own = lax.all_to_all(jnp.broadcast_to(own[None], (CHIPS, LAYERS, SLICE, GW)), ("y", "x"), 0, 0, tiled=True)
    other = lax.ppermute(own, "c", [(0, 1), (1, 0)])

    layers = [pltpu.VMEM((LAYERS, 2, CHIPS, SLICE, GW), BF16), pltpu.VMEM((LAYERS, ROWS, GW), BF16)]
    sems = pltpu.SemaphoreType.DMA((2, LAYERS))
    pieces_shape = (2, LAYERS, 2 * HALF + TAIL, LANES)
    xs, slope = pl.pallas_call(
        forward_kernel,
        out_shape=[jax.ShapeDtypeStruct(pieces_shape, BF16), jax.ShapeDtypeStruct((LAYERS, ROWS, GW), BF16)],
        in_specs=[vmem, vmem, hbm, vmem],
        out_specs=[hbm, hbm],
        scratch_shapes=layers
        + [pltpu.VMEM((LAYERS, PROWS, GW), F32), pltpu.VMEM((LAYERS, ROWS, GW), F32), pltpu.VMEM(pieces_shape, BF16)]
        + [sems, pltpu.SemaphoreType.DMA((4,))],
        name="fwd",
    )(near(rows), near(layer_parts), own, near(other))

    home = lax.all_to_all(xs.reshape(2 * CHIPS, 2 * HALF + TAIL, LANES), ("g", "y", "x"), 0, 0, tiled=True)
    held = pltpu.VMEM((2, HOME, GW), BF16)
    keep, send, tail, params, centered = pl.pallas_call(
        gram_kernel,
        out_shape=[
            pltpu.VMEM((4 * 3 * PIECE, GW), F32),
            pltpu.VMEM((4 * 3 * PIECE + TAIL, GW), BF16),
            pltpu.VMEM((TAIL, GW), BF16),
            pltpu.VMEM((2, 4, GW), F32),
            jax.ShapeDtypeStruct((2, HOME, GW), BF16),
        ],
        in_specs=[vmem],
        out_specs=[vmem] * 4 + [hbm],
        scratch_shapes=[held, pltpu.SemaphoreType.DMA((2,))],
        name="gram",
    )(near(home.reshape(2, CHIPS, 2 * HALF + TAIL, LANES)))
    got = lax.ppermute(send, "c", [(0, 1), (1, 0)])
    (pieces,) = kernel_call(
        chip_kernel, [((4, 3 * PIECE + 2 * TAIL, GW), BF16)], "chip", keep, tail, got, scalars=[part]
    )
    pieces = lax.all_to_all(pieces, ("g", "h"), 0, 0, tiled=True)
    (deviation,) = kernel_call(
        deviation_kernel,
        [((4, 3 * PIECE, GW), BF16)],
        "deviation",
        pieces,
        params,
        scalars=[part],
        scratch=[pltpu.VMEM((GW, GW), F32)],
    )
    deviation = lax.all_gather(lax.all_to_all(deviation, ("g", "h"), 0, 0, tiled=True), "c", axis=0)
    pulls = pl.pallas_call(
        pull_kernel,
        out_shape=pltpu.VMEM((2, CHIPS, 2 * HALF + TAIL, LANES), BF16),
        in_specs=[vmem] * 4 + [hbm],
        out_specs=vmem,
        scratch_shapes=[held, pltpu.SemaphoreType.DMA((CHUNKS,))],
        name="pull",
    )(near(deviation), near(pieces), near(tail), near(params), centered)
    pulls = lax.all_to_all(pulls.reshape(2 * CHIPS, 2 * HALF + TAIL, LANES), ("g", "y", "x"), 0, 0, tiled=True)

    grads = pl.pallas_call(
        backward_kernel,
        out_shape=pltpu.VMEM((8, 16 + TAIL, GW), BF16),
        in_specs=[vmem, hbm, hbm, hbm],
        out_specs=vmem,
        scratch_shapes=layers + [sems, pltpu.SemaphoreType.DMA((2,))],
        name="bwd",
    )(near(pulls.reshape(2, LAYERS, 2 * HALF + TAIL, LANES)), own, other, slope)
    grads = lax.all_to_all(grads, ("g", "k"), 0, 0, tiled=True)
    image_grad, loss = pl.pallas_call(
        output_kernel,
        out_shape=[jax.ShapeDtypeStruct((1, 16, BLOCKS * 2 * GW), BF16), jax.ShapeDtypeStruct((1, 1), F32)],
        in_specs=[vmem],
        out_specs=[vmem, vmem],
        name="outputs",
    )(near(grads))
    return image_grad, loss.reshape(())


def solution(mesh):
    fine = Mesh(np.asarray(mesh.devices).reshape(4, 2, 2, 4, 4, 2), ("k", "h", "g", "x", "y", "c"))
    batch, section = ("x", "y", "c"), ("k", "h", "g")
    return jax.shard_map(
        shards,
        mesh=fine,
        in_specs=(
            P(batch, None, None),
            P(section, None, None, None),
            P(section, None),
            P(section, None),
            P(section, None),
            P(section, None),
        ),
        out_specs=(P(batch, section, None), P()),
        check_vma=False,
    )
```

```python
import math

import jax
import jax.numpy as jnp
import numpy as np
from jax import lax
from jax.experimental import pallas as pl
from jax.experimental.pallas import tpu as pltpu
from jax.sharding import Mesh, PartitionSpec as P

EPS = 1e-05
LOG2E = math.log2(math.e)
F32 = jnp.float32
BF16 = jnp.bfloat16

LAYERS = 16
GW = 256
BLOCKS = 3
CHIPS = 16
SLICE = GW // (2 * CHIPS)
PROWS = 8
ROWS = 128
HALF = ROWS // 2
HOME = CHIPS * HALF
LANES = 128
PARTS = 8
PIECE = GW // PARTS
TAIL = 8
TOTAL = HOME * PARTS


def split3(value):
    high = value.astype(BF16).astype(F32)
    rest = value - high
    middle = rest.astype(BF16).astype(F32)
    return high, middle, rest - middle


def pack_kernel(w_ref, images_ref, *refs):
    inputs, (out_ref, x_ref, slab_ref), held, sems = refs[:4], refs[4:7], refs[7:11], refs[11]
    reads = [pltpu.make_async_copy(source, target, sems.at[5 + at]) for at, (source, target) in enumerate(zip(inputs, held))]
    for copy in reads:
        copy.start()
    mean_ref, var_ref, gain_ref, bias_ref = held
    chip = lax.axis_index("y") * 4 + lax.axis_index("x")
    row = (lax.axis_index("c") * CHIPS + chip) * SLICE
    half = lax.axis_index("h")
    group = 2 * jnp.minimum(lax.axis_index("k"), BLOCKS - 1) + lax.axis_index("g")
    slab = pltpu.make_async_copy(w_ref.at[0, :, pl.ds(pl.multiple_of(row, SLICE), SLICE), :], slab_ref, sems.at[0])
    slab.start()
    copies = []
    for strip in range(4):
        source = images_ref.at[
            0, pl.ds(pl.multiple_of(strip * 64 + half * 32, 32), 32), pl.ds(pl.multiple_of(group * GW, GW), GW)
        ]
        copies.append(pltpu.make_async_copy(source, x_ref.at[strip * 32:strip * 32 + 32], sems.at[1 + strip]))
        copies[-1].start()
    for copy in reads:
        copy.wait()
    scale = gain_ref[...] * lax.rsqrt(var_ref[...] + EPS)
    packed = [scale, bias_ref[...] - mean_ref[...] * scale, mean_ref[...], var_ref[...]]
    high = [value.astype(BF16).astype(F32) for value in packed]
    packed = jnp.concatenate(high + [value - top for value, top in zip(packed, high)], axis=0).astype(BF16)
    slab.wait()
    for k in range(4):
        for g in range(2):
            at = 2 * min(k, BLOCKS - 1) + g
            for h in range(2):
                out_ref[k, h, g, 0:SLICE] = slab_ref[at]
                out_ref[k, h, g, SLICE:] = packed[:, at * GW:(at + 1) * GW]
    for copy in copies:
        copy.wait()


def in_order(own, other, core):
    return jnp.concatenate([lax.select(core == 0, own, other), lax.select(core == 0, other, own)], axis=0)


GROUPS = (0, 2, 4, 8, LAYERS)


def weight_reads(own_in, other_in, w_ref, core, sems, layer):
    return [
        pltpu.make_async_copy(own_in.at[:, layer], w_ref.at[layer, core], sems.at[0, layer]),
        pltpu.make_async_copy(other_in.at[:, layer], w_ref.at[layer, 1 - core], sems.at[1, layer]),
    ]


def forward_kernel(
    x_ref, par_ref, own_in, other_in, xs_out, slope_out, w_ref, slope_ref, rows_ref, z_ref, xs_ref, sems, out_sems
):
    core = lax.axis_index("c")
    chip = lax.axis_index("y") * 4 + lax.axis_index("x")
    arrivals = [weight_reads(own_in, other_in, w_ref, core, sems, layer) for layer in range(LAYERS)]
    for copy in sum(arrivals, []):
        copy.start()
    for layer in range(LAYERS):
        rows_ref[layer] = par_ref[layer, SLICE:SLICE + PROWS].astype(F32)
    at_row = lax.broadcasted_iota(jnp.int32, (TAIL, LANES), 0)

    def pack_layer(layer):
        row = rows_ref[layer, pl.ds(chip // 2, 1), :]
        row = jnp.broadcast_to(lax.select(chip % 2 == 0, row[:, 0:LANES], row[:, LANES:]), (TAIL, LANES))
        for half in range(2):
            rows = z_ref[layer, half * HALF:(half + 1) * HALF]
            mean = jnp.sum(rows, axis=0, keepdims=True) * (1.0 / HALF)
            rows = (rows - mean).astype(BF16)
            xs_ref[half, layer, 0:HALF] = rows[:, 0:LANES]
            xs_ref[half, layer, HALF:2 * HALF] = rows[:, LANES:]
            high = mean.astype(BF16).astype(F32)
            terms = [part[:, at:at + LANES] for part in (high, mean - high) for at in (0, LANES)]
            tail = row
            for at, term in enumerate(terms):
                tail = jnp.where(at_row == at, term, tail)
            xs_ref[half, layer, 2 * HALF:] = tail.astype(BF16)

    writes = []

    def write(first, last):
        span = pl.ds(first, last - first)
        at = len(writes)
        writes.append(pltpu.make_async_copy(xs_ref.at[:, span], xs_out.at[:, span], out_sems.at[at]))
        writes.append(pltpu.make_async_copy(slope_ref.at[span], slope_out.at[span], out_sems.at[at + 1]))
        for copy in writes[-2:]:
            copy.start()

    x = x_ref[...]
    for layer in range(LAYERS):
        if layer in GROUPS:
            for copy in sum(arrivals[layer:GROUPS[GROUPS.index(layer) + 1]], []):
                copy.wait()
        z = jnp.dot(x, w_ref[layer].reshape(GW, GW), preferred_element_type=F32)
        z_ref[layer] = z
        if layer > 0:
            pack_layer(layer - 1)
        scale = rows_ref[layer, 0:1] + rows_ref[layer, 4:5]
        shift = rows_ref[layer, 1:2] + rows_ref[layer, 5:6]
        active = z * scale + shift
        gate = 1.0 / (1.0 + jnp.exp2(z * (scale * -LOG2E) + shift * -LOG2E))
        after = active * gate
        x = after.astype(BF16)
        slope_ref[layer] = (gate * ((active - after) + 1.0) * scale).astype(BF16)
        if layer == LAYERS // 2:
            write(0, LAYERS // 2)
    pack_layer(LAYERS - 1)
    write(LAYERS // 2, LAYERS)
    for copy in writes:
        copy.wait()


def gram_kernel(x_ref, keep_ref, send_ref, tail_ref, par_ref, zc_out, zc_ref, sems):
    core = lax.axis_index("c")
    means, writes = [], []
    for g in range(2):
        tails = x_ref[g, :, 2 * HALF:].astype(F32)
        mean = sum(jnp.concatenate([tails[:, at:at + 1], tails[:, at + 1:at + 2]], axis=2) for at in (0, 2))
        means.append(jnp.mean(mean, axis=0))
        rows = jnp.concatenate([x_ref[g, :, 0:HALF], x_ref[g, :, HALF:2 * HALF]], axis=2).astype(F32)
        zc_ref[g] = (rows + (mean - means[g][None])).astype(BF16).reshape(HOME, GW)
        writes.append(pltpu.make_async_copy(zc_ref.at[g], zc_out.at[g], sems.at[g]))
        writes[g].start()
        packed = [jnp.concatenate([tails[2 * r, 6:7], tails[2 * r + 1, 6:7]], axis=1) for r in range(PROWS)]
        par_ref[g] = jnp.concatenate([packed[r] + packed[r + 4] for r in range(4)], axis=0)
    parts = [split3(mean) for mean in means]
    tail = [parts[g][term] for term in range(3) for g in range(2)]
    tail = jnp.concatenate(tail + [jnp.zeros((2, GW), F32)], axis=0).astype(BF16)
    tail_ref[...] = tail
    send_ref[4 * 3 * PIECE:] = tail
    for at, (a, b) in enumerate(((0, 0), (0, 1), (1, 1))):
        gram = lax.dot_general(zc_ref[a], zc_ref[b], (((0,), (0,)), ((), ())), preferred_element_type=F32)
        low, high = gram[0:GW // 2], gram[GW // 2:]
        keep, send = lax.select(core == 0, low, high), lax.select(core == 0, high, low).astype(BF16)
        for j in range(4):
            rows = pl.ds((3 * j + at) * PIECE, PIECE)
            keep_ref[rows] = keep[j * PIECE:(j + 1) * PIECE]
            send_ref[rows] = send[j * PIECE:(j + 1) * PIECE]
    for copy in writes:
        copy.wait()


def chip_kernel(j_ref, keep_ref, tail_ref, got_ref, out_ref):
    core = j_ref[0] % 2
    tails = in_order(tail_ref[...], got_ref[4 * 3 * PIECE:], core)
    for j in range(4):
        rows = pl.ds(3 * j * PIECE, 3 * PIECE)
        out_ref[j, 0:3 * PIECE] = (keep_ref[rows] + got_ref[rows].astype(F32)).astype(BF16)
        out_ref[j, 3 * PIECE:] = tails


def mean_of(rows, g):
    return rows[..., g, :] + rows[..., 2 + g, :] + rows[..., 4 + g, :]


def all_means(r_ref):
    rows = r_ref[:, 3 * PIECE:].astype(F32)
    cores = rows[:, 0:TAIL], rows[:, TAIL:]
    return [jnp.concatenate([mean_of(core, g) for core in cores], axis=0) for g in range(2)]


def deviation_kernel(j_ref, r_ref, par_ref, e_ref, scratch_ref):
    row_at = (j_ref[0] % 2 * 4 + j_ref[0] // 2) * PIECE
    means = all_means(r_ref)
    shifted = [m - jnp.mean(m, axis=0, keepdims=True) for m in means]
    highs = [m.astype(BF16).astype(F32) for m in shifted]
    lows = [m - high for m, high in zip(shifted, highs)]
    spare = jnp.zeros((PARTS, GW), F32)
    firsts = [jnp.concatenate([high, high, low, spare], axis=0).astype(BF16) for high, low in zip(highs, lows)]
    seconds = [jnp.concatenate([high, low, high, spare], axis=0).astype(BF16) for high, low in zip(highs, lows)]
    total = jnp.sum(r_ref[:, 0:3 * PIECE].astype(F32), axis=0) * (1.0 / TOTAL)
    diagonal = (
        lax.broadcasted_iota(jnp.int32, (PIECE, GW), 0) + row_at
        == lax.broadcasted_iota(jnp.int32, (PIECE, GW), 1)
    )
    for at, (a, b) in enumerate(((0, 0), (0, 1), (1, 1))):
        scratch_ref[...] = lax.dot_general(
            firsts[a], seconds[b], (((0,), (0,)), ((), ())), preferred_element_type=F32
        )
        part = total[at * PIECE:(at + 1) * PIECE] + scratch_ref[pl.ds(row_at, PIECE), :] * (1.0 / PARTS)
        if a == b:
            part = part - jnp.where(diagonal, par_ref[a, 3:4], 0.0)
        for j in range(4):
            e_ref[j, at * PIECE:(at + 1) * PIECE] = part.astype(BF16)


CHUNKS = 1


def pull_kernel(e_ref, r_ref, tail_ref, par_ref, zc_in, out_ref, zc_ref, sems):
    reads = []
    for n in range(CHUNKS):
        rows = pl.ds(n * (HOME // CHUNKS), HOME // CHUNKS)
        reads.append(pltpu.make_async_copy(zc_in.at[:, rows], zc_ref.at[:, rows], sems.at[n]))
        reads[n].start()
    means = all_means(r_ref)
    mine = tail_ref[...].astype(F32)
    mats = [e_ref[:, :, at * PIECE:(at + 1) * PIECE].reshape(GW, GW) for at in range(3)]
    whole = [m.astype(F32) for m in mats]
    loss = 0.25 * (
        jnp.sum(whole[0] * whole[0], keepdims=True)
        + 2.0 * jnp.sum(whole[1] * whole[1], keepdims=True)
        + jnp.sum(whole[2] * whole[2], keepdims=True)
    )
    away, offset = [], []
    for g in range(2):
        mean = jnp.mean(means[g], axis=0, keepdims=True)
        gap = mean - par_ref[g, 2:3]
        loss = loss + jnp.sum(gap * gap, keepdims=True)
        away.append(2.0 * gap)
        own = mine[g:g + 1] + mine[2 + g:3 + g] + mine[4 + g:5 + g]
        offset.append(jnp.concatenate(list(split3(own - mean)) + [jnp.zeros((13, GW), F32)], axis=0).astype(BF16))
    tail = [jnp.broadcast_to(part, (1, LANES)) for part in split3(loss)]
    tail = jnp.concatenate(tail + [jnp.zeros((TAIL - 3, LANES), F32)], axis=0).astype(BF16)
    tail = jnp.broadcast_to(tail[None], (CHIPS, TAIL, LANES))
    plain, crossed = (((1,), (0,)), ((), ())), (((1,), (1,)), ((), ()))

    def both(lhs, g):
        (at, first), (bt, second) = ((0, plain), (1, crossed)) if g == 0 else ((1, plain), (2, plain))
        return lax.dot_general(lhs[0], mats[at], first, preferred_element_type=F32) + lax.dot_general(
            lhs[1], mats[bt], second, preferred_element_type=F32
        )

    rows = []
    for g in range(2):
        row = both(offset, g)
        rows.append(row[0:1] + row[1:2] + row[2:3] + away[g])
    size = HOME // CHUNKS
    chips = CHIPS // CHUNKS
    for copy in reads:
        copy.wait()
    for n in range(CHUNKS):
        for g in range(2):
            pull = both([zc_ref[side, n * size:(n + 1) * size] for side in range(2)], g) + rows[g]
            pull = pull.astype(BF16).reshape(chips, HALF, GW)
            out_ref[g, n * chips:(n + 1) * chips, 0:HALF] = pull[:, :, 0:LANES]
            out_ref[g, n * chips:(n + 1) * chips, HALF:2 * HALF] = pull[:, :, LANES:]
    for g in range(2):
        out_ref[g, :, 2 * HALF:] = tail


def backward_kernel(q_ref, own_in, other_in, slope_in, out_ref, w_ref, slope_ref, sems, slope_sem):
    core = lax.axis_index("c")
    arrivals = []
    for n, (first, last) in enumerate(zip(GROUPS, GROUPS[1:])):
        span = pl.ds(LAYERS - last, last - first)
        group = [pltpu.make_async_copy(slope_in.at[span], slope_ref.at[span], slope_sem.at[n])]
        for layer in range(LAYERS - last, LAYERS - first):
            group += weight_reads(own_in, other_in, w_ref, core, sems, layer)
        for copy in group:
            copy.start()
        arrivals.append(group)
    loss = jnp.zeros((1, LANES), F32)
    grad = None
    for layer in reversed(range(LAYERS)):
        rows = q_ref[0, layer, 2 * HALF:].astype(F32)
        loss = loss + (rows[0:1] + rows[1:2] + rows[2:3])
        pull = jnp.concatenate(
            [q_ref[:, layer, 0:HALF].reshape(ROWS, LANES), q_ref[:, layer, HALF:2 * HALF].reshape(ROWS, LANES)], axis=1
        )
        if LAYERS - 1 - layer in GROUPS:
            for copy in arrivals[GROUPS.index(LAYERS - 1 - layer)]:
                copy.wait()
        if grad is not None:
            pull = (grad * slope_ref[layer].astype(F32) + pull.astype(F32)).astype(BF16)
        grad = lax.dot_general(
            pull, w_ref[layer].reshape(GW, GW), (((1,), (1,)), ((), ())), preferred_element_type=F32
        )
    loss = jnp.concatenate([loss, loss], axis=1)
    tail = jnp.concatenate(list(split3(loss)) + [jnp.zeros((TAIL - 3, GW), F32)], axis=0).astype(BF16)
    grad = grad.astype(BF16)
    for strip in range(8):
        slot = strip % 2 * 4 + strip // 2
        out_ref[slot, 0:16] = grad[strip * 16:strip * 16 + 16]
        out_ref[slot, 16:16 + TAIL] = tail


def output_kernel(r_ref, grad_ref, loss_ref):
    loss = jnp.zeros((1, 1), F32)
    for k in range(BLOCKS):
        for g in range(2):
            at = 2 * k + g
            grad_ref[0, :, at * GW:(at + 1) * GW] = r_ref[4 * g + k, 0:16]
        loss = loss + jnp.sum(r_ref[k, 16:16 + TAIL].astype(F32)[0:3, 0:1], axis=0, keepdims=True)
    loss_ref[...] = loss * (1.0 / (LAYERS * BLOCKS * 2 * GW))


def near(array):
    return pltpu.with_memory_space_constraint(array, pltpu.VMEM)


def kernel_call(kernel, outs, name, *args, scalars=(), scratch=()):
    vmem = pl.BlockSpec(memory_space=pltpu.VMEM)
    smem = pl.BlockSpec(memory_space=pltpu.SMEM)
    return pl.pallas_call(
        kernel,
        out_shape=[pltpu.VMEM(*out) for out in outs],
        in_specs=[smem] * len(scalars) + [vmem] * len(args),
        out_specs=[vmem] * len(outs),
        scratch_shapes=list(scratch),
        name=name,
    )(*scalars, *[near(arg) for arg in args])


def shards(images, weights, bn_mean, bn_var, bn_gain, bn_bias):
    part = lax.axis_index(("g", "h", "c")).astype(jnp.int32).reshape(1)

    hbm, vmem = pl.BlockSpec(memory_space=pl.ANY), pl.BlockSpec(memory_space=pltpu.VMEM)
    message, rows = pl.pallas_call(
        pack_kernel,
        out_shape=[pltpu.VMEM((4, 2, 2, SLICE + PROWS, GW), BF16), pltpu.VMEM((ROWS, GW), BF16)],
        in_specs=[hbm] * 6,
        out_specs=[vmem, vmem],
        scratch_shapes=[pltpu.VMEM((2 * BLOCKS, SLICE, GW), BF16)]
        + [pltpu.VMEM((1, 2 * BLOCKS * GW), F32)] * 4
        + [pltpu.SemaphoreType.DMA((9,))],
        name="pack",
    )(weights, images, bn_mean, bn_var, bn_gain, bn_bias)
    message = message.reshape(LAYERS, SLICE + PROWS, GW)
    layer_parts = lax.all_to_all(message, ("k", "h", "g"), 0, 0, tiled=True)

    own = layer_parts[:, 0:SLICE]
    own = lax.all_to_all(jnp.broadcast_to(own[None], (CHIPS, LAYERS, SLICE, GW)), ("y", "x"), 0, 0, tiled=True)
    other = lax.ppermute(own, "c", [(0, 1), (1, 0)])

    layers = [pltpu.VMEM((LAYERS, 2, CHIPS, SLICE, GW), BF16), pltpu.VMEM((LAYERS, ROWS, GW), BF16)]
    sems = pltpu.SemaphoreType.DMA((2, LAYERS))
    pieces_shape = (2, LAYERS, 2 * HALF + TAIL, LANES)
    xs, slope = pl.pallas_call(
        forward_kernel,
        out_shape=[jax.ShapeDtypeStruct(pieces_shape, BF16), jax.ShapeDtypeStruct((LAYERS, ROWS, GW), BF16)],
        in_specs=[vmem, vmem, hbm, vmem],
        out_specs=[hbm, hbm],
        scratch_shapes=layers
        + [pltpu.VMEM((LAYERS, PROWS, GW), F32), pltpu.VMEM((LAYERS, ROWS, GW), F32), pltpu.VMEM(pieces_shape, BF16)]
        + [sems, pltpu.SemaphoreType.DMA((4,))],
        name="fwd",
    )(near(rows), near(layer_parts), own, near(other))

    home = lax.all_to_all(xs.reshape(2 * CHIPS, 2 * HALF + TAIL, LANES), ("g", "y", "x"), 0, 0, tiled=True)
    held = pltpu.VMEM((2, HOME, GW), BF16)
    keep, send, tail, params, centered = pl.pallas_call(
        gram_kernel,
        out_shape=[
            pltpu.VMEM((4 * 3 * PIECE, GW), F32),
            pltpu.VMEM((4 * 3 * PIECE + TAIL, GW), BF16),
            pltpu.VMEM((TAIL, GW), BF16),
            pltpu.VMEM((2, 4, GW), F32),
            jax.ShapeDtypeStruct((2, HOME, GW), BF16),
        ],
        in_specs=[vmem],
        out_specs=[vmem] * 4 + [hbm],
        scratch_shapes=[held, pltpu.SemaphoreType.DMA((2,))],
        name="gram",
    )(near(home.reshape(2, CHIPS, 2 * HALF + TAIL, LANES)))
    got = lax.ppermute(send, "c", [(0, 1), (1, 0)])
    (pieces,) = kernel_call(
        chip_kernel, [((4, 3 * PIECE + 2 * TAIL, GW), BF16)], "chip", keep, tail, got, scalars=[part]
    )
    pieces = lax.all_to_all(pieces, ("g", "h"), 0, 0, tiled=True)
    (deviation,) = kernel_call(
        deviation_kernel,
        [((4, 3 * PIECE, GW), BF16)],
        "deviation",
        pieces,
        params,
        scalars=[part],
        scratch=[pltpu.VMEM((GW, GW), F32)],
    )
    deviation = lax.all_gather(lax.all_to_all(deviation, ("g", "h"), 0, 0, tiled=True), "c", axis=0)
    pulls = pl.pallas_call(
        pull_kernel,
        out_shape=pltpu.VMEM((2, CHIPS, 2 * HALF + TAIL, LANES), BF16),
        in_specs=[vmem] * 4 + [hbm],
        out_specs=vmem,
        scratch_shapes=[held, pltpu.SemaphoreType.DMA((CHUNKS,))],
        name="pull",
    )(near(deviation), near(pieces), near(tail), near(params), centered)
    pulls = lax.all_to_all(pulls.reshape(2 * CHIPS, 2 * HALF + TAIL, LANES), ("g", "y", "x"), 0, 0, tiled=True)

    grads = pl.pallas_call(
        backward_kernel,
        out_shape=pltpu.VMEM((8, 16 + TAIL, GW), BF16),
        in_specs=[vmem, hbm, hbm, hbm],
        out_specs=vmem,
        scratch_shapes=layers + [sems, pltpu.SemaphoreType.DMA((4,))],
        name="bwd",
    )(near(pulls.reshape(2, LAYERS, 2 * HALF + TAIL, LANES)), own, other, slope)
    grads = lax.all_to_all(grads, ("g", "k"), 0, 0, tiled=True)
    image_grad, loss = pl.pallas_call(
        output_kernel,
        out_shape=[jax.ShapeDtypeStruct((1, 16, BLOCKS * 2 * GW), BF16), jax.ShapeDtypeStruct((1, 1), F32)],
        in_specs=[vmem],
        out_specs=[vmem, vmem],
        name="outputs",
    )(near(grads))
    return image_grad, loss.reshape(())


def solution(mesh):
    fine = Mesh(np.asarray(mesh.devices).reshape(4, 2, 2, 4, 4, 2), ("k", "h", "g", "x", "y", "c"))
    batch, section = ("x", "y", "c"), ("k", "h", "g")
    return jax.shard_map(
        shards,
        mesh=fine,
        in_specs=(
            P(batch, None, None),
            P(section, None, None, None),
            P(section, None),
            P(section, None),
            P(section, None),
            P(section, None),
        ),
        out_specs=(P(batch, section, None), P()),
        check_vma=False,
    )
```

```python
import math

import jax
import jax.numpy as jnp
import numpy as np
from jax import lax
from jax.experimental import pallas as pl
from jax.experimental.pallas import tpu as pltpu
from jax.sharding import Mesh, PartitionSpec as P

EPS = 1e-05
LOG2E = math.log2(math.e)
F32 = jnp.float32
BF16 = jnp.bfloat16

LAYERS = 16
GW = 256
BLOCKS = 3
CHIPS = 16
SLICE = GW // (2 * CHIPS)
PROWS = 8
ROWS = 128
HALF = ROWS // 2
HOME = CHIPS * HALF
LANES = 128
PARTS = 8
PIECE = GW // PARTS
TAIL = 8
TOTAL = HOME * PARTS


def split3(value):
    high = value.astype(BF16).astype(F32)
    rest = value - high
    middle = rest.astype(BF16).astype(F32)
    return high, middle, rest - middle


def pack_kernel(w_ref, images_ref, *refs):
    inputs, (out_ref, x_ref, slab_ref), held, sems = refs[:4], refs[4:7], refs[7:11], refs[11]
    reads = [pltpu.make_async_copy(source, target, sems.at[5 + at]) for at, (source, target) in enumerate(zip(inputs, held))]
    for copy in reads:
        copy.start()
    mean_ref, var_ref, gain_ref, bias_ref = held
    chip = lax.axis_index("y") * 4 + lax.axis_index("x")
    row = (lax.axis_index("c") * CHIPS + chip) * SLICE
    half = lax.axis_index("h")
    group = 2 * jnp.minimum(lax.axis_index("k"), BLOCKS - 1) + lax.axis_index("g")
    slab = pltpu.make_async_copy(w_ref.at[0, :, pl.ds(pl.multiple_of(row, SLICE), SLICE), :], slab_ref, sems.at[0])
    slab.start()
    copies = []
    for strip in range(4):
        source = images_ref.at[
            0, pl.ds(pl.multiple_of(strip * 64 + half * 32, 32), 32), pl.ds(pl.multiple_of(group * GW, GW), GW)
        ]
        copies.append(pltpu.make_async_copy(source, x_ref.at[strip * 32:strip * 32 + 32], sems.at[1 + strip]))
        copies[-1].start()
    for copy in reads:
        copy.wait()
    scale = gain_ref[...] * lax.rsqrt(var_ref[...] + EPS)
    packed = [scale, bias_ref[...] - mean_ref[...] * scale, mean_ref[...], var_ref[...]]
    high = [value.astype(BF16).astype(F32) for value in packed]
    packed = jnp.concatenate(high + [value - top for value, top in zip(packed, high)], axis=0).astype(BF16)
    slab.wait()
    for k in range(4):
        for g in range(2):
            at = 2 * min(k, BLOCKS - 1) + g
            for h in range(2):
                out_ref[k, h, g, 0:SLICE] = slab_ref[at]
                out_ref[k, h, g, SLICE:] = packed[:, at * GW:(at + 1) * GW]
    for copy in copies:
        copy.wait()


def in_order(own, other, core):
    return jnp.concatenate([lax.select(core == 0, own, other), lax.select(core == 0, other, own)], axis=0)


FIRST = 4


def weight_reads(own_in, other_in, w_ref, core, sems, layer):
    return [
        pltpu.make_async_copy(own_in.at[:, layer], w_ref.at[layer, core], sems.at[0, layer]),
        pltpu.make_async_copy(other_in.at[:, layer], w_ref.at[layer, 1 - core], sems.at[1, layer]),
    ]


def forward_kernel(
    x_ref, par_ref, own_in, other_in, xs_out, slope_out, w_ref, slope_ref, rows_ref, xs_ref, sems, out_sems
):
    core = lax.axis_index("c")
    arrivals = [weight_reads(own_in, other_in, w_ref, core, sems, layer) for layer in range(LAYERS)]
    for copy in sum(arrivals, []):
        copy.start()
    for layer in range(LAYERS):
        packed = par_ref[layer, SLICE:SLICE + PROWS].astype(F32)
        rows_ref[layer] = packed[0:4] + packed[4:8]
    writes = []

    def write(first, last):
        span = pl.ds(first, last - first)
        at = len(writes)
        writes.append(pltpu.make_async_copy(xs_ref.at[:, span], xs_out.at[:, span], out_sems.at[at]))
        writes.append(pltpu.make_async_copy(slope_ref.at[span], slope_out.at[span], out_sems.at[at + 1]))
        for copy in writes[-2:]:
            copy.start()

    x = x_ref[...]
    for layer in range(LAYERS):
        if layer in (0, FIRST):
            for copy in sum(arrivals[0:FIRST] if layer == 0 else arrivals[FIRST:], []):
                copy.wait()
        z = jnp.dot(x, w_ref[layer].reshape(GW, GW), preferred_element_type=F32)
        scale, shift = rows_ref[layer, 0:1], rows_ref[layer, 1:2]
        active = z * scale + shift
        gate = 1.0 / (1.0 + jnp.exp2(z * (scale * -LOG2E) + shift * -LOG2E))
        after = active * gate
        x = after.astype(BF16)
        slope_ref[layer] = (gate * ((active - after) + 1.0) * scale).astype(BF16)
        away = (z - rows_ref[layer, 2:3]).astype(BF16)
        for half in range(2):
            xs_ref[half, layer] = away[half * HALF:(half + 1) * HALF]
        if layer == LAYERS // 2:
            write(0, LAYERS // 2)
    write(LAYERS // 2, LAYERS)
    for copy in writes:
        copy.wait()


def gram_kernel(x_ref, mine_ref, theirs_ref, keep_ref, send_ref, tail_ref, par_ref, zc_out, zc_ref, sems):
    core, side = lax.axis_index("c"), lax.axis_index("g")
    means, writes = [], []
    for g in range(2):
        rows = x_ref[g].reshape(HOME, GW).astype(F32)
        means.append(jnp.sum(rows, axis=0, keepdims=True) * (1.0 / HOME))
        zc_ref[g] = (rows - means[g]).astype(BF16)
        writes.append(pltpu.make_async_copy(zc_ref.at[g], zc_out.at[g], sems.at[g]))
        writes[g].start()
        packed = lax.select(side == g, mine_ref[...], theirs_ref[...]).astype(F32)
        par_ref[g] = packed[0:4] + packed[4:8]
    parts = [split3(mean) for mean in means]
    tail = [parts[g][term] for term in range(3) for g in range(2)]
    tail = jnp.concatenate(tail + [jnp.zeros((2, GW), F32)], axis=0).astype(BF16)
    tail_ref[...] = tail
    send_ref[4 * 3 * PIECE:] = tail
    for at, (a, b) in enumerate(((0, 0), (0, 1), (1, 1))):
        gram = lax.dot_general(zc_ref[a], zc_ref[b], (((0,), (0,)), ((), ())), preferred_element_type=F32)
        low, high = gram[0:GW // 2], gram[GW // 2:]
        keep, send = lax.select(core == 0, low, high), lax.select(core == 0, high, low).astype(BF16)
        for j in range(4):
            rows = pl.ds((3 * j + at) * PIECE, PIECE)
            keep_ref[rows] = keep[j * PIECE:(j + 1) * PIECE]
            send_ref[rows] = send[j * PIECE:(j + 1) * PIECE]
    for copy in writes:
        copy.wait()


def chip_kernel(j_ref, keep_ref, tail_ref, got_ref, out_ref):
    core = j_ref[0] % 2
    tails = in_order(tail_ref[...], got_ref[4 * 3 * PIECE:], core)
    for j in range(4):
        rows = pl.ds(3 * j * PIECE, 3 * PIECE)
        out_ref[j, 0:3 * PIECE] = (keep_ref[rows] + got_ref[rows].astype(F32)).astype(BF16)
        out_ref[j, 3 * PIECE:] = tails


def mean_of(rows, g):
    return rows[..., g, :] + rows[..., 2 + g, :] + rows[..., 4 + g, :]


def all_means(r_ref):
    rows = r_ref[:, 3 * PIECE:].astype(F32)
    cores = rows[:, 0:TAIL], rows[:, TAIL:]
    return [jnp.concatenate([mean_of(core, g) for core in cores], axis=0) for g in range(2)]


def deviation_kernel(j_ref, r_ref, par_ref, e_ref, scratch_ref):
    row_at = (j_ref[0] % 2 * 4 + j_ref[0] // 2) * PIECE
    means = all_means(r_ref)
    shifted = [m - jnp.mean(m, axis=0, keepdims=True) for m in means]
    highs = [m.astype(BF16).astype(F32) for m in shifted]
    lows = [m - high for m, high in zip(shifted, highs)]
    spare = jnp.zeros((PARTS, GW), F32)
    firsts = [jnp.concatenate([high, high, low, spare], axis=0).astype(BF16) for high, low in zip(highs, lows)]
    seconds = [jnp.concatenate([high, low, high, spare], axis=0).astype(BF16) for high, low in zip(highs, lows)]
    total = jnp.sum(r_ref[:, 0:3 * PIECE].astype(F32), axis=0) * (1.0 / TOTAL)
    diagonal = (
        lax.broadcasted_iota(jnp.int32, (PIECE, GW), 0) + row_at
        == lax.broadcasted_iota(jnp.int32, (PIECE, GW), 1)
    )
    for at, (a, b) in enumerate(((0, 0), (0, 1), (1, 1))):
        scratch_ref[...] = lax.dot_general(
            firsts[a], seconds[b], (((0,), (0,)), ((), ())), preferred_element_type=F32
        )
        part = total[at * PIECE:(at + 1) * PIECE] + scratch_ref[pl.ds(row_at, PIECE), :] * (1.0 / PARTS)
        if a == b:
            part = part - jnp.where(diagonal, par_ref[a, 3:4], 0.0)
        for j in range(4):
            e_ref[j, at * PIECE:(at + 1) * PIECE] = part.astype(BF16)


CHUNKS = 1


def pull_kernel(e_ref, r_ref, tail_ref, zc_in, out_ref, zc_ref, sems):
    reads = []
    for n in range(CHUNKS):
        rows = pl.ds(n * (HOME // CHUNKS), HOME // CHUNKS)
        reads.append(pltpu.make_async_copy(zc_in.at[:, rows], zc_ref.at[:, rows], sems.at[n]))
        reads[n].start()
    means = all_means(r_ref)
    mine = tail_ref[...].astype(F32)
    mats = [e_ref[:, :, at * PIECE:(at + 1) * PIECE].reshape(GW, GW) for at in range(3)]
    whole = [m.astype(F32) for m in mats]
    loss = 0.25 * (
        jnp.sum(whole[0] * whole[0], keepdims=True)
        + 2.0 * jnp.sum(whole[1] * whole[1], keepdims=True)
        + jnp.sum(whole[2] * whole[2], keepdims=True)
    )
    away, offset = [], []
    for g in range(2):
        mean = jnp.mean(means[g], axis=0, keepdims=True)
        loss = loss + jnp.sum(mean * mean, keepdims=True)
        away.append(2.0 * mean)
        own = mine[g:g + 1] + mine[2 + g:3 + g] + mine[4 + g:5 + g]
        offset.append(jnp.concatenate(list(split3(own - mean)) + [jnp.zeros((13, GW), F32)], axis=0).astype(BF16))
    tail = [jnp.broadcast_to(part, (1, LANES)) for part in split3(loss)]
    tail = jnp.concatenate(tail + [jnp.zeros((TAIL - 3, LANES), F32)], axis=0).astype(BF16)
    tail = jnp.broadcast_to(tail[None], (CHIPS, TAIL, LANES))
    plain, crossed = (((1,), (0,)), ((), ())), (((1,), (1,)), ((), ()))

    def both(lhs, g):
        (at, first), (bt, second) = ((0, plain), (1, crossed)) if g == 0 else ((1, plain), (2, plain))
        return lax.dot_general(lhs[0], mats[at], first, preferred_element_type=F32) + lax.dot_general(
            lhs[1], mats[bt], second, preferred_element_type=F32
        )

    rows = []
    for g in range(2):
        row = both(offset, g)
        rows.append(row[0:1] + row[1:2] + row[2:3] + away[g])
    size = HOME // CHUNKS
    chips = CHIPS // CHUNKS
    for copy in reads:
        copy.wait()
    for n in range(CHUNKS):
        for g in range(2):
            pull = both([zc_ref[side, n * size:(n + 1) * size] for side in range(2)], g) + rows[g]
            pull = pull.astype(BF16).reshape(chips, HALF, GW)
            out_ref[g, n * chips:(n + 1) * chips, 0:HALF] = pull[:, :, 0:LANES]
            out_ref[g, n * chips:(n + 1) * chips, HALF:2 * HALF] = pull[:, :, LANES:]
    for g in range(2):
        out_ref[g, :, 2 * HALF:] = tail


def backward_kernel(q_ref, own_in, other_in, slope_in, out_ref, w_ref, slope_ref, sems, slope_sem):
    core = lax.axis_index("c")
    arrivals = [weight_reads(own_in, other_in, w_ref, core, sems, layer) for layer in range(LAYERS)]
    parts = [pl.ds(LAYERS - FIRST, FIRST), pl.ds(0, LAYERS - FIRST)]
    slopes = [pltpu.make_async_copy(slope_in.at[at], slope_ref.at[at], slope_sem.at[n]) for n, at in enumerate(parts)]
    arrivals = [sum(arrivals[LAYERS - FIRST:], []) + slopes[:1], sum(arrivals[:LAYERS - FIRST], []) + slopes[1:]]
    for copy in arrivals[0] + arrivals[1]:
        copy.start()
    loss = jnp.zeros((1, LANES), F32)
    grad = None
    for layer in reversed(range(LAYERS)):
        rows = q_ref[0, layer, 2 * HALF:].astype(F32)
        loss = loss + (rows[0:1] + rows[1:2] + rows[2:3])
        pull = jnp.concatenate(
            [q_ref[:, layer, 0:HALF].reshape(ROWS, LANES), q_ref[:, layer, HALF:2 * HALF].reshape(ROWS, LANES)], axis=1
        )
        if layer in (LAYERS - 1, LAYERS - 1 - FIRST):
            for copy in arrivals[0 if layer == LAYERS - 1 else 1]:
                copy.wait()
        if grad is not None:
            pull = (grad * slope_ref[layer].astype(F32) + pull.astype(F32)).astype(BF16)
        grad = lax.dot_general(
            pull, w_ref[layer].reshape(GW, GW), (((1,), (1,)), ((), ())), preferred_element_type=F32
        )
    loss = jnp.concatenate([loss, loss], axis=1)
    tail = jnp.concatenate(list(split3(loss)) + [jnp.zeros((TAIL - 3, GW), F32)], axis=0).astype(BF16)
    grad = grad.astype(BF16)
    for strip in range(8):
        slot = strip % 2 * 4 + strip // 2
        out_ref[slot, 0:16] = grad[strip * 16:strip * 16 + 16]
        out_ref[slot, 16:16 + TAIL] = tail


def output_kernel(r_ref, grad_ref, loss_ref):
    loss = jnp.zeros((1, 1), F32)
    for k in range(BLOCKS):
        for g in range(2):
            at = 2 * k + g
            grad_ref[0, :, at * GW:(at + 1) * GW] = r_ref[4 * g + k, 0:16]
        loss = loss + jnp.sum(r_ref[k, 16:16 + TAIL].astype(F32)[0:3, 0:1], axis=0, keepdims=True)
    loss_ref[...] = loss * (1.0 / (LAYERS * BLOCKS * 2 * GW))


def near(array):
    return pltpu.with_memory_space_constraint(array, pltpu.VMEM)


def kernel_call(kernel, outs, name, *args, scalars=(), scratch=()):
    vmem = pl.BlockSpec(memory_space=pltpu.VMEM)
    smem = pl.BlockSpec(memory_space=pltpu.SMEM)
    return pl.pallas_call(
        kernel,
        out_shape=[pltpu.VMEM(*out) for out in outs],
        in_specs=[smem] * len(scalars) + [vmem] * len(args),
        out_specs=[vmem] * len(outs),
        scratch_shapes=list(scratch),
        name=name,
    )(*scalars, *[near(arg) for arg in args])


def shards(images, weights, bn_mean, bn_var, bn_gain, bn_bias):
    part = lax.axis_index(("g", "h", "c")).astype(jnp.int32).reshape(1)

    hbm, vmem = pl.BlockSpec(memory_space=pl.ANY), pl.BlockSpec(memory_space=pltpu.VMEM)
    message, rows = pl.pallas_call(
        pack_kernel,
        out_shape=[pltpu.VMEM((4, 2, 2, SLICE + PROWS, GW), BF16), pltpu.VMEM((ROWS, GW), BF16)],
        in_specs=[hbm] * 6,
        out_specs=[vmem, vmem],
        scratch_shapes=[pltpu.VMEM((2 * BLOCKS, SLICE, GW), BF16)]
        + [pltpu.VMEM((1, 2 * BLOCKS * GW), F32)] * 4
        + [pltpu.SemaphoreType.DMA((9,))],
        name="pack",
    )(weights, images, bn_mean, bn_var, bn_gain, bn_bias)
    message = message.reshape(LAYERS, SLICE + PROWS, GW)
    layer_parts = lax.all_to_all(message, ("k", "h", "g"), 0, 0, tiled=True)

    own = layer_parts[:, 0:SLICE]
    own = lax.all_to_all(jnp.broadcast_to(own[None], (CHIPS, LAYERS, SLICE, GW)), ("y", "x"), 0, 0, tiled=True)
    other = lax.ppermute(own, "c", [(0, 1), (1, 0)])

    layers = [pltpu.VMEM((LAYERS, 2, CHIPS, SLICE, GW), BF16), pltpu.VMEM((LAYERS, ROWS, GW), BF16)]
    sems = pltpu.SemaphoreType.DMA((2, LAYERS))
    pieces_shape = (2, LAYERS, HALF, GW)
    xs, slope = pl.pallas_call(
        forward_kernel,
        out_shape=[jax.ShapeDtypeStruct(pieces_shape, BF16), jax.ShapeDtypeStruct((LAYERS, ROWS, GW), BF16)],
        in_specs=[vmem, vmem, hbm, vmem],
        out_specs=[hbm, hbm],
        scratch_shapes=layers
        + [pltpu.VMEM((LAYERS, 4, GW), F32), pltpu.VMEM(pieces_shape, BF16)]
        + [sems, pltpu.SemaphoreType.DMA((4,))],
        name="fwd",
    )(near(rows), near(layer_parts), own, near(other))

    home = lax.all_to_all(xs.reshape(2 * CHIPS, HALF, GW), ("g", "x", "y"), 0, 0, tiled=True)
    mine = lax.dynamic_index_in_dim(layer_parts, lax.axis_index(("x", "y")), 0, keepdims=False)[SLICE:]
    mine = lax.optimization_barrier((mine, xs))[0]
    theirs = lax.ppermute(mine, "g", [(0, 1), (1, 0)])
    held = pltpu.VMEM((2, HOME, GW), BF16)
    keep, send, tail, params, centered = pl.pallas_call(
        gram_kernel,
        out_shape=[
            pltpu.VMEM((4 * 3 * PIECE, GW), F32),
            pltpu.VMEM((4 * 3 * PIECE + TAIL, GW), BF16),
            pltpu.VMEM((TAIL, GW), BF16),
            pltpu.VMEM((2, 4, GW), F32),
            jax.ShapeDtypeStruct((2, HOME, GW), BF16),
        ],
        in_specs=[vmem] * 3,
        out_specs=[vmem] * 4 + [hbm],
        scratch_shapes=[held, pltpu.SemaphoreType.DMA((2,))],
        name="gram",
    )(near(home.reshape(2, CHIPS, HALF, GW)), near(mine), near(theirs))
    got = lax.ppermute(send, "c", [(0, 1), (1, 0)])
    (pieces,) = kernel_call(
        chip_kernel, [((4, 3 * PIECE + 2 * TAIL, GW), BF16)], "chip", keep, tail, got, scalars=[part]
    )
    pieces = lax.all_to_all(pieces, ("g", "h"), 0, 0, tiled=True)
    (deviation,) = kernel_call(
        deviation_kernel,
        [((4, 3 * PIECE, GW), BF16)],
        "deviation",
        pieces,
        params,
        scalars=[part],
        scratch=[pltpu.VMEM((GW, GW), F32)],
    )
    deviation = lax.all_gather(lax.all_to_all(deviation, ("g", "h"), 0, 0, tiled=True), "c", axis=0)
    pulls = pl.pallas_call(
        pull_kernel,
        out_shape=pltpu.VMEM((2, CHIPS, 2 * HALF + TAIL, LANES), BF16),
        in_specs=[vmem] * 3 + [hbm],
        out_specs=vmem,
        scratch_shapes=[held, pltpu.SemaphoreType.DMA((CHUNKS,))],
        name="pull",
    )(near(deviation), near(pieces), near(tail), centered)
    pulls = lax.all_to_all(pulls.reshape(2 * CHIPS, 2 * HALF + TAIL, LANES), ("g", "x", "y"), 0, 0, tiled=True)

    grads = pl.pallas_call(
        backward_kernel,
        out_shape=pltpu.VMEM((8, 16 + TAIL, GW), BF16),
        in_specs=[vmem, hbm, hbm, hbm],
        out_specs=vmem,
        scratch_shapes=layers + [sems, pltpu.SemaphoreType.DMA((2,))],
        name="bwd",
    )(near(pulls.reshape(2, LAYERS, 2 * HALF + TAIL, LANES)), own, other, slope)
    grads = lax.all_to_all(grads, ("g", "k"), 0, 0, tiled=True)
    image_grad, loss = pl.pallas_call(
        output_kernel,
        out_shape=[jax.ShapeDtypeStruct((1, 16, BLOCKS * 2 * GW), BF16), jax.ShapeDtypeStruct((1, 1), F32)],
        in_specs=[vmem],
        out_specs=[vmem, vmem],
        name="outputs",
    )(near(grads))
    return image_grad, loss.reshape(())


def solution(mesh):
    fine = Mesh(np.asarray(mesh.devices).reshape(4, 2, 2, 4, 4, 2), ("k", "h", "g", "x", "y", "c"))
    batch, section = ("x", "y", "c"), ("k", "h", "g")
    return jax.shard_map(
        shards,
        mesh=fine,
        in_specs=(
            P(batch, None, None),
            P(section, None, None, None),
            P(section, None),
            P(section, None),
            P(section, None),
            P(section, None),
        ),
        out_specs=(P(batch, section, None), P()),
        check_vma=False,
    )
```

```python
import math

import jax
import jax.numpy as jnp
import numpy as np
from jax import lax
from jax.experimental import pallas as pl
from jax.experimental.pallas import tpu as pltpu
from jax.sharding import Mesh, PartitionSpec as P

EPS = 1e-05
LOG2E = math.log2(math.e)
F32 = jnp.float32
BF16 = jnp.bfloat16

LAYERS = 16
GW = 256
BLOCKS = 3
CHIPS = 16
SLICE = GW // (2 * CHIPS)
PROWS = 8
ROWS = 128
HALF = ROWS // 2
HOME = CHIPS * HALF
LANES = 128
PARTS = 8
PIECE = GW // PARTS
TAIL = 8
TOTAL = HOME * PARTS


def split3(value):
    high = value.astype(BF16).astype(F32)
    rest = value - high
    middle = rest.astype(BF16).astype(F32)
    return high, middle, rest - middle


def pack_kernel(w_ref, images_ref, *refs):
    inputs, (out_ref, x_ref, slab_ref), held, sems = refs[:4], refs[4:7], refs[7:11], refs[11]
    reads = [pltpu.make_async_copy(source, target, sems.at[5 + at]) for at, (source, target) in enumerate(zip(inputs, held))]
    for copy in reads:
        copy.start()
    mean_ref, var_ref, gain_ref, bias_ref = held
    chip = lax.axis_index("y") * 4 + lax.axis_index("x")
    row = (lax.axis_index("c") * CHIPS + chip) * SLICE
    half = lax.axis_index("h")
    group = 2 * jnp.minimum(lax.axis_index("k"), BLOCKS - 1) + lax.axis_index("g")
    slab = pltpu.make_async_copy(w_ref.at[0, :, pl.ds(pl.multiple_of(row, SLICE), SLICE), :], slab_ref, sems.at[0])
    slab.start()
    copies = []
    for strip in range(4):
        source = images_ref.at[
            0, pl.ds(pl.multiple_of(strip * 64 + half * 32, 32), 32), pl.ds(pl.multiple_of(group * GW, GW), GW)
        ]
        copies.append(pltpu.make_async_copy(source, x_ref.at[strip * 32:strip * 32 + 32], sems.at[1 + strip]))
        copies[-1].start()
    for copy in reads:
        copy.wait()
    scale = gain_ref[...] * lax.rsqrt(var_ref[...] + EPS)
    packed = [scale, bias_ref[...] - mean_ref[...] * scale, mean_ref[...], var_ref[...]]
    high = [value.astype(BF16).astype(F32) for value in packed]
    packed = jnp.concatenate(high + [value - top for value, top in zip(packed, high)], axis=0).astype(BF16)
    slab.wait()
    for k in range(4):
        for g in range(2):
            at = 2 * min(k, BLOCKS - 1) + g
            for h in range(2):
                out_ref[k, h, g, 0:SLICE] = slab_ref[at]
                out_ref[k, h, g, SLICE:SLICE + PROWS] = packed[:, at * GW:(at + 1) * GW]
                beside = at + 1 - 2 * g
                out_ref[k, h, g, SLICE + PROWS:] = packed[:, beside * GW:(beside + 1) * GW]
    for copy in copies:
        copy.wait()


def in_order(own, other, core):
    return jnp.concatenate([lax.select(core == 0, own, other), lax.select(core == 0, other, own)], axis=0)


FIRST = 4


def weight_reads(own_in, other_in, w_ref, core, sems, layer):
    return [
        pltpu.make_async_copy(own_in.at[:, layer], w_ref.at[layer, core], sems.at[0, layer]),
        pltpu.make_async_copy(other_in.at[:, layer], w_ref.at[layer, 1 - core], sems.at[1, layer]),
    ]


def forward_kernel(
    x_ref, par_ref, own_in, other_in, xs_ref, slope_out, w_ref, slope_ref, rows_ref, sems, out_sems
):
    core = lax.axis_index("c")
    arrivals = [weight_reads(own_in, other_in, w_ref, core, sems, layer) for layer in range(LAYERS)]
    for copy in sum(arrivals, []):
        copy.start()
    for layer in range(LAYERS):
        packed = par_ref[layer, SLICE:SLICE + PROWS].astype(F32)
        rows_ref[layer] = packed[0:4] + packed[4:8]
    writes = []

    def write(first, last):
        span = pl.ds(first, last - first)
        writes.append(pltpu.make_async_copy(slope_ref.at[span], slope_out.at[span], out_sems.at[len(writes)]))
        writes[-1].start()

    x = x_ref[...]
    for layer in range(LAYERS):
        if layer in (0, FIRST):
            for copy in sum(arrivals[0:FIRST] if layer == 0 else arrivals[FIRST:], []):
                copy.wait()
        z = jnp.dot(x, w_ref[layer].reshape(GW, GW), preferred_element_type=F32)
        scale, shift = rows_ref[layer, 0:1], rows_ref[layer, 1:2]
        active = z * scale + shift
        gate = 1.0 / (1.0 + jnp.exp2(z * (scale * -LOG2E) + shift * -LOG2E))
        after = active * gate
        x = after.astype(BF16)
        slope_ref[layer] = (gate * ((active - after) + 1.0) * scale).astype(BF16)
        away = (z - rows_ref[layer, 2:3]).astype(BF16)
        for half in range(2):
            xs_ref[half, layer] = away[half * HALF:(half + 1) * HALF]
        if layer == LAYERS // 2:
            write(0, LAYERS // 2)
    write(LAYERS // 2, LAYERS)
    for copy in writes:
        copy.wait()


def gram_kernel(x_ref, parts_ref, keep_ref, send_ref, tail_ref, par_ref, zc_out, zc_ref, sems):
    core, side = lax.axis_index("c"), lax.axis_index("g")
    layer = lax.axis_index("x") * 4 + lax.axis_index("y")
    own, beside = parts_ref[layer, SLICE:SLICE + PROWS], parts_ref[layer, SLICE + PROWS:]
    means, writes = [], []
    for g in range(2):
        rows = x_ref[g].reshape(HOME, GW).astype(F32)
        means.append(jnp.sum(rows, axis=0, keepdims=True) * (1.0 / HOME))
        zc_ref[g] = (rows - means[g]).astype(BF16)
        writes.append(pltpu.make_async_copy(zc_ref.at[g], zc_out.at[g], sems.at[g]))
        writes[g].start()
        packed = lax.select(side == g, own, beside).astype(F32)
        par_ref[g] = packed[0:4] + packed[4:8]
    parts = [split3(mean) for mean in means]
    tail = [parts[g][term] for term in range(3) for g in range(2)]
    tail = jnp.concatenate(tail + [jnp.zeros((2, GW), F32)], axis=0).astype(BF16)
    tail_ref[...] = tail
    send_ref[4 * 3 * PIECE:] = tail
    for at, (a, b) in enumerate(((0, 0), (0, 1), (1, 1))):
        gram = lax.dot_general(zc_ref[a], zc_ref[b], (((0,), (0,)), ((), ())), preferred_element_type=F32)
        low, high = gram[0:GW // 2], gram[GW // 2:]
        keep, send = lax.select(core == 0, low, high), lax.select(core == 0, high, low).astype(BF16)
        for j in range(4):
            rows = pl.ds((3 * j + at) * PIECE, PIECE)
            keep_ref[rows] = keep[j * PIECE:(j + 1) * PIECE]
            send_ref[rows] = send[j * PIECE:(j + 1) * PIECE]
    for copy in writes:
        copy.wait()


def chip_kernel(j_ref, keep_ref, tail_ref, got_ref, out_ref):
    core = j_ref[0] % 2
    tails = in_order(tail_ref[...], got_ref[4 * 3 * PIECE:], core)
    for j in range(4):
        rows = pl.ds(3 * j * PIECE, 3 * PIECE)
        out_ref[j, 0:3 * PIECE] = (keep_ref[rows] + got_ref[rows].astype(F32)).astype(BF16)
        out_ref[j, 3 * PIECE:] = tails


def mean_of(rows, g):
    return rows[..., g, :] + rows[..., 2 + g, :] + rows[..., 4 + g, :]


def all_means(r_ref):
    rows = r_ref[:, 3 * PIECE:].astype(F32)
    cores = rows[:, 0:TAIL], rows[:, TAIL:]
    return [jnp.concatenate([mean_of(core, g) for core in cores], axis=0) for g in range(2)]


def deviation_kernel(j_ref, r_ref, par_ref, e_ref, scratch_ref):
    row_at = (j_ref[0] % 2 * 4 + j_ref[0] // 2) * PIECE
    means = all_means(r_ref)
    shifted = [m - jnp.mean(m, axis=0, keepdims=True) for m in means]
    highs = [m.astype(BF16).astype(F32) for m in shifted]
    lows = [m - high for m, high in zip(shifted, highs)]
    spare = jnp.zeros((PARTS, GW), F32)
    firsts = [jnp.concatenate([high, high, low, spare], axis=0).astype(BF16) for high, low in zip(highs, lows)]
    seconds = [jnp.concatenate([high, low, high, spare], axis=0).astype(BF16) for high, low in zip(highs, lows)]
    total = jnp.sum(r_ref[:, 0:3 * PIECE].astype(F32), axis=0) * (1.0 / TOTAL)
    diagonal = (
        lax.broadcasted_iota(jnp.int32, (PIECE, GW), 0) + row_at
        == lax.broadcasted_iota(jnp.int32, (PIECE, GW), 1)
    )
    for at, (a, b) in enumerate(((0, 0), (0, 1), (1, 1))):
        scratch_ref[...] = lax.dot_general(
            firsts[a], seconds[b], (((0,), (0,)), ((), ())), preferred_element_type=F32
        )
        part = total[at * PIECE:(at + 1) * PIECE] + scratch_ref[pl.ds(row_at, PIECE), :] * (1.0 / PARTS)
        if a == b:
            part = part - jnp.where(diagonal, par_ref[a, 3:4], 0.0)
        for j in range(4):
            e_ref[j, at * PIECE:(at + 1) * PIECE] = part.astype(BF16)


CHUNKS = 1


def pull_kernel(e_ref, r_ref, tail_ref, zc_in, out_ref, zc_ref, sems):
    reads = []
    for n in range(CHUNKS):
        rows = pl.ds(n * (HOME // CHUNKS), HOME // CHUNKS)
        reads.append(pltpu.make_async_copy(zc_in.at[:, rows], zc_ref.at[:, rows], sems.at[n]))
        reads[n].start()
    means = all_means(r_ref)
    mine = tail_ref[...].astype(F32)
    mats = [e_ref[:, :, at * PIECE:(at + 1) * PIECE].reshape(GW, GW) for at in range(3)]
    whole = [m.astype(F32) for m in mats]
    loss = 0.25 * (
        jnp.sum(whole[0] * whole[0], keepdims=True)
        + 2.0 * jnp.sum(whole[1] * whole[1], keepdims=True)
        + jnp.sum(whole[2] * whole[2], keepdims=True)
    )
    away, offset = [], []
    for g in range(2):
        mean = jnp.mean(means[g], axis=0, keepdims=True)
        loss = loss + jnp.sum(mean * mean, keepdims=True)
        away.append(2.0 * mean)
        own = mine[g:g + 1] + mine[2 + g:3 + g] + mine[4 + g:5 + g]
        offset.append(jnp.concatenate(list(split3(own - mean)) + [jnp.zeros((13, GW), F32)], axis=0).astype(BF16))
    tail = [jnp.broadcast_to(part, (1, LANES)) for part in split3(loss)]
    tail = jnp.concatenate(tail + [jnp.zeros((TAIL - 3, LANES), F32)], axis=0).astype(BF16)
    tail = jnp.broadcast_to(tail[None], (CHIPS, TAIL, LANES))
    plain, crossed = (((1,), (0,)), ((), ())), (((1,), (1,)), ((), ()))

    def both(lhs, g):
        (at, first), (bt, second) = ((0, plain), (1, crossed)) if g == 0 else ((1, plain), (2, plain))
        return lax.dot_general(lhs[0], mats[at], first, preferred_element_type=F32) + lax.dot_general(
            lhs[1], mats[bt], second, preferred_element_type=F32
        )

    rows = []
    for g in range(2):
        row = both(offset, g)
        rows.append(row[0:1] + row[1:2] + row[2:3] + away[g])
    size = HOME // CHUNKS
    chips = CHIPS // CHUNKS
    for copy in reads:
        copy.wait()
    for n in range(CHUNKS):
        for g in range(2):
            pull = both([zc_ref[side, n * size:(n + 1) * size] for side in range(2)], g) + rows[g]
            pull = pull.astype(BF16).reshape(chips, HALF, GW)
            out_ref[g, n * chips:(n + 1) * chips, 0:HALF] = pull[:, :, 0:LANES]
            out_ref[g, n * chips:(n + 1) * chips, HALF:2 * HALF] = pull[:, :, LANES:]
    for g in range(2):
        out_ref[g, :, 2 * HALF:] = tail


def backward_kernel(q_ref, own_in, other_in, slope_in, out_ref, w_ref, slope_ref, sems, slope_sem):
    core = lax.axis_index("c")
    arrivals = [weight_reads(own_in, other_in, w_ref, core, sems, layer) for layer in range(LAYERS)]
    parts = [pl.ds(LAYERS - FIRST, FIRST), pl.ds(0, LAYERS - FIRST)]
    slopes = [pltpu.make_async_copy(slope_in.at[at], slope_ref.at[at], slope_sem.at[n]) for n, at in enumerate(parts)]
    arrivals = [sum(arrivals[LAYERS - FIRST:], []) + slopes[:1], sum(arrivals[:LAYERS - FIRST], []) + slopes[1:]]
    for copy in arrivals[0] + arrivals[1]:
        copy.start()
    loss = jnp.zeros((1, LANES), F32)
    grad = None
    for layer in reversed(range(LAYERS)):
        rows = q_ref[0, layer, 2 * HALF:].astype(F32)
        loss = loss + (rows[0:1] + rows[1:2] + rows[2:3])
        pull = jnp.concatenate(
            [q_ref[:, layer, 0:HALF].reshape(ROWS, LANES), q_ref[:, layer, HALF:2 * HALF].reshape(ROWS, LANES)], axis=1
        )
        if layer in (LAYERS - 1, LAYERS - 1 - FIRST):
            for copy in arrivals[0 if layer == LAYERS - 1 else 1]:
                copy.wait()
        if grad is not None:
            pull = (grad * slope_ref[layer].astype(F32) + pull.astype(F32)).astype(BF16)
        grad = lax.dot_general(
            pull, w_ref[layer].reshape(GW, GW), (((1,), (1,)), ((), ())), preferred_element_type=F32
        )
    loss = jnp.concatenate([loss, loss], axis=1)
    tail = jnp.concatenate(list(split3(loss)) + [jnp.zeros((TAIL - 3, GW), F32)], axis=0).astype(BF16)
    grad = grad.astype(BF16)
    for strip in range(8):
        slot = strip % 2 * 4 + strip // 2
        out_ref[slot, 0:16] = grad[strip * 16:strip * 16 + 16]
        out_ref[slot, 16:16 + TAIL] = tail


def output_kernel(r_ref, grad_ref, loss_ref):
    loss = jnp.zeros((1, 1), F32)
    for k in range(BLOCKS):
        for g in range(2):
            at = 2 * k + g
            grad_ref[0, :, at * GW:(at + 1) * GW] = r_ref[4 * g + k, 0:16]
        loss = loss + jnp.sum(r_ref[k, 16:16 + TAIL].astype(F32)[0:3, 0:1], axis=0, keepdims=True)
    loss_ref[...] = loss * (1.0 / (LAYERS * BLOCKS * 2 * GW))


def near(array):
    return pltpu.with_memory_space_constraint(array, pltpu.VMEM)


def kernel_call(kernel, outs, name, *args, scalars=(), scratch=()):
    vmem = pl.BlockSpec(memory_space=pltpu.VMEM)
    smem = pl.BlockSpec(memory_space=pltpu.SMEM)
    return pl.pallas_call(
        kernel,
        out_shape=[pltpu.VMEM(*out) for out in outs],
        in_specs=[smem] * len(scalars) + [vmem] * len(args),
        out_specs=[vmem] * len(outs),
        scratch_shapes=list(scratch),
        name=name,
    )(*scalars, *[near(arg) for arg in args])


def shards(images, weights, bn_mean, bn_var, bn_gain, bn_bias):
    part = lax.axis_index(("g", "h", "c")).astype(jnp.int32).reshape(1)

    hbm, vmem = pl.BlockSpec(memory_space=pl.ANY), pl.BlockSpec(memory_space=pltpu.VMEM)
    message, rows = pl.pallas_call(
        pack_kernel,
        out_shape=[pltpu.VMEM((4, 2, 2, SLICE + 2 * PROWS, GW), BF16), pltpu.VMEM((ROWS, GW), BF16)],
        in_specs=[hbm] * 6,
        out_specs=[vmem, vmem],
        scratch_shapes=[pltpu.VMEM((2 * BLOCKS, SLICE, GW), BF16)]
        + [pltpu.VMEM((1, 2 * BLOCKS * GW), F32)] * 4
        + [pltpu.SemaphoreType.DMA((9,))],
        name="pack",
    )(weights, images, bn_mean, bn_var, bn_gain, bn_bias)
    message = message.reshape(LAYERS, SLICE + 2 * PROWS, GW)
    layer_parts = lax.all_to_all(message, ("k", "h", "g"), 0, 0, tiled=True)

    own = layer_parts[:, 0:SLICE]
    own = lax.all_to_all(jnp.broadcast_to(own[None], (CHIPS, LAYERS, SLICE, GW)), ("y", "x"), 0, 0, tiled=True)
    other = lax.ppermute(own, "c", [(0, 1), (1, 0)])

    layers = [pltpu.VMEM((LAYERS, 2, CHIPS, SLICE, GW), BF16), pltpu.VMEM((LAYERS, ROWS, GW), BF16)]
    sems = pltpu.SemaphoreType.DMA((2, LAYERS))
    pieces_shape = (2, LAYERS, HALF, GW)
    xs, slope = pl.pallas_call(
        forward_kernel,
        out_shape=[pltpu.VMEM(pieces_shape, BF16), jax.ShapeDtypeStruct((LAYERS, ROWS, GW), BF16)],
        in_specs=[vmem, vmem, hbm, vmem],
        out_specs=[vmem, hbm],
        scratch_shapes=layers
        + [pltpu.VMEM((LAYERS, 4, GW), F32), sems, pltpu.SemaphoreType.DMA((2,))],
        name="fwd",
    )(near(rows), near(layer_parts), own, near(other))

    home = lax.all_to_all(xs.reshape(2 * CHIPS, HALF, GW), ("g", "x", "y"), 0, 0, tiled=True)
    held = pltpu.VMEM((2, HOME, GW), BF16)
    keep, send, tail, params, centered = pl.pallas_call(
        gram_kernel,
        out_shape=[
            pltpu.VMEM((4 * 3 * PIECE, GW), F32),
            pltpu.VMEM((4 * 3 * PIECE + TAIL, GW), BF16),
            pltpu.VMEM((TAIL, GW), BF16),
            pltpu.VMEM((2, 4, GW), F32),
            jax.ShapeDtypeStruct((2, HOME, GW), BF16),
        ],
        in_specs=[vmem] * 2,
        out_specs=[vmem] * 4 + [hbm],
        scratch_shapes=[held, pltpu.SemaphoreType.DMA((2,))],
        name="gram",
    )(near(home.reshape(2, CHIPS, HALF, GW)), near(layer_parts))
    got = lax.ppermute(send, "c", [(0, 1), (1, 0)])
    (pieces,) = kernel_call(
        chip_kernel, [((4, 3 * PIECE + 2 * TAIL, GW), BF16)], "chip", keep, tail, got, scalars=[part]
    )
    pieces = lax.all_to_all(pieces, ("g", "h"), 0, 0, tiled=True)
    (deviation,) = kernel_call(
        deviation_kernel,
        [((4, 3 * PIECE, GW), BF16)],
        "deviation",
        pieces,
        params,
        scalars=[part],
        scratch=[pltpu.VMEM((GW, GW), F32)],
    )
    deviation = lax.all_gather(lax.all_to_all(deviation, ("g", "h"), 0, 0, tiled=True), "c", axis=0)
    pulls = pl.pallas_call(
        pull_kernel,
        out_shape=pltpu.VMEM((2, CHIPS, 2 * HALF + TAIL, LANES), BF16),
        in_specs=[vmem] * 3 + [hbm],
        out_specs=vmem,
        scratch_shapes=[held, pltpu.SemaphoreType.DMA((CHUNKS,))],
        name="pull",
    )(near(deviation), near(pieces), near(tail), centered)
    pulls = lax.all_to_all(pulls.reshape(2 * CHIPS, 2 * HALF + TAIL, LANES), ("g", "x", "y"), 0, 0, tiled=True)

    grads = pl.pallas_call(
        backward_kernel,
        out_shape=pltpu.VMEM((8, 16 + TAIL, GW), BF16),
        in_specs=[vmem, hbm, hbm, hbm],
        out_specs=vmem,
        scratch_shapes=layers + [sems, pltpu.SemaphoreType.DMA((2,))],
        name="bwd",
    )(near(pulls.reshape(2, LAYERS, 2 * HALF + TAIL, LANES)), own, other, slope)
    grads = lax.all_to_all(grads, ("g", "k"), 0, 0, tiled=True)
    image_grad, loss = pl.pallas_call(
        output_kernel,
        out_shape=[jax.ShapeDtypeStruct((1, 16, BLOCKS * 2 * GW), BF16), jax.ShapeDtypeStruct((1, 1), F32)],
        in_specs=[vmem],
        out_specs=[vmem, vmem],
        name="outputs",
    )(near(grads))
    return image_grad, loss.reshape(())


def solution(mesh):
    fine = Mesh(np.asarray(mesh.devices).reshape(4, 2, 2, 4, 4, 2), ("k", "h", "g", "x", "y", "c"))
    batch, section = ("x", "y", "c"), ("k", "h", "g")
    return jax.shard_map(
        shards,
        mesh=fine,
        in_specs=(
            P(batch, None, None),
            P(section, None, None, None),
            P(section, None),
            P(section, None),
            P(section, None),
            P(section, None),
        ),
        out_specs=(P(batch, section, None), P()),
        check_vma=False,
    )
```

```python
import math

import jax
import jax.numpy as jnp
import numpy as np
from jax import lax
from jax.experimental import pallas as pl
from jax.experimental.pallas import tpu as pltpu
from jax.sharding import Mesh, PartitionSpec as P

EPS = 1e-05
LOG2E = math.log2(math.e)
F32 = jnp.float32
BF16 = jnp.bfloat16

LAYERS = 16
GW = 256
BLOCKS = 3
CHIPS = 16
SLICE = GW // (2 * CHIPS)
PROWS = 8
ROWS = 128
HALF = ROWS // 2
HOME = CHIPS * HALF
LANES = 128
PARTS = 8
PIECE = GW // PARTS
TAIL = 8
TOTAL = HOME * PARTS


def split3(value):
    high = value.astype(BF16).astype(F32)
    rest = value - high
    middle = rest.astype(BF16).astype(F32)
    return high, middle, rest - middle


def pack_kernel(w_ref, images_ref, *refs):
    inputs, (out_ref, x_ref, slab_ref), held, sems = refs[:4], refs[4:7], refs[7:11], refs[11]
    reads = [pltpu.make_async_copy(source, target, sems.at[5 + at]) for at, (source, target) in enumerate(zip(inputs, held))]
    for copy in reads:
        copy.start()
    mean_ref, var_ref, gain_ref, bias_ref = held
    chip = lax.axis_index("y") * 4 + lax.axis_index("x")
    row = (lax.axis_index("c") * CHIPS + chip) * SLICE
    half = lax.axis_index("h")
    group = 2 * jnp.minimum(lax.axis_index("k"), BLOCKS - 1) + lax.axis_index("g")
    slab = pltpu.make_async_copy(w_ref.at[0, :, pl.ds(pl.multiple_of(row, SLICE), SLICE), :], slab_ref, sems.at[0])
    slab.start()
    copies = []
    for strip in range(4):
        source = images_ref.at[
            0, pl.ds(pl.multiple_of(strip * 64 + half * 32, 32), 32), pl.ds(pl.multiple_of(group * GW, GW), GW)
        ]
        copies.append(pltpu.make_async_copy(source, x_ref.at[strip * 32:strip * 32 + 32], sems.at[1 + strip]))
        copies[-1].start()
    for copy in reads:
        copy.wait()
    scale = gain_ref[...] * lax.rsqrt(var_ref[...] + EPS)
    packed = [scale, bias_ref[...] - mean_ref[...] * scale, mean_ref[...], var_ref[...]]
    high = [value.astype(BF16).astype(F32) for value in packed]
    packed = jnp.concatenate(high + [value - top for value, top in zip(packed, high)], axis=0).astype(BF16)
    slab.wait()
    for k in range(4):
        for g in range(2):
            at = 2 * min(k, BLOCKS - 1) + g
            for h in range(2):
                out_ref[h, k, g, 0:SLICE] = slab_ref[at]
                out_ref[h, k, g, SLICE:] = packed[:, at * GW:(at + 1) * GW]
    for copy in copies:
        copy.wait()


def in_order(own, other, core):
    return jnp.concatenate([lax.select(core == 0, own, other), lax.select(core == 0, other, own)], axis=0)


FIRST = 4


def slot(layer):
    return layer // 2 % 2 * 8 + layer // 4 * 2 + layer % 2


def weight_reads(own_in, other_in, w_ref, core, sems, layer):
    return [
        pltpu.make_async_copy(own_in.at[:, slot(layer)], w_ref.at[layer, core], sems.at[0, layer]),
        pltpu.make_async_copy(other_in.at[:, slot(layer)], w_ref.at[layer, 1 - core], sems.at[1, layer]),
    ]


def forward_kernel(
    x_ref, par_ref, own_in, other_in, xs_out, slope_out, w_ref, slope_ref, rows_ref, xs_ref, sems, out_sems
):
    core = lax.axis_index("c")
    arrivals = [weight_reads(own_in, other_in, w_ref, core, sems, layer) for layer in range(LAYERS)]
    for copy in sum(arrivals, []):
        copy.start()
    for layer in range(LAYERS):
        packed = par_ref[slot(layer), SLICE:SLICE + PROWS].astype(F32)
        rows_ref[layer] = packed[0:4] + packed[4:8]
    writes = []

    def write(first, last):
        span = pl.ds(first, last - first)
        at = len(writes)
        writes.append(pltpu.make_async_copy(xs_ref.at[:, span], xs_out.at[:, span], out_sems.at[at]))
        writes.append(pltpu.make_async_copy(slope_ref.at[span], slope_out.at[span], out_sems.at[at + 1]))
        for copy in writes[-2:]:
            copy.start()

    x = x_ref[...]
    for layer in range(LAYERS):
        if layer in (0, FIRST):
            for copy in sum(arrivals[0:FIRST] if layer == 0 else arrivals[FIRST:], []):
                copy.wait()
        z = jnp.dot(x, w_ref[layer].reshape(GW, GW), preferred_element_type=F32)
        scale, shift = rows_ref[layer, 0:1], rows_ref[layer, 1:2]
        active = z * scale + shift
        gate = 1.0 / (1.0 + jnp.exp2(z * (scale * -LOG2E) + shift * -LOG2E))
        after = active * gate
        x = after.astype(BF16)
        slope_ref[layer] = (gate * ((active - after) + 1.0) * scale).astype(BF16)
        away = (z - rows_ref[layer, 2:3]).astype(BF16)
        for half in range(2):
            xs_ref[half, layer] = away[half * HALF:(half + 1) * HALF]
        if layer == LAYERS // 2:
            write(0, LAYERS // 2)
    write(LAYERS // 2, LAYERS)
    for copy in writes:
        copy.wait()


def gram_kernel(x_ref, mine_ref, theirs_ref, keep_ref, send_ref, tail_ref, par_ref, zc_out, zc_ref, sems):
    core, side = lax.axis_index("c"), lax.axis_index("g")
    means, writes = [], []
    for g in range(2):
        rows = x_ref[g].reshape(HOME, GW).astype(F32)
        means.append(jnp.sum(rows, axis=0, keepdims=True) * (1.0 / HOME))
        zc_ref[g] = (rows - means[g]).astype(BF16)
        writes.append(pltpu.make_async_copy(zc_ref.at[g], zc_out.at[g], sems.at[g]))
        writes[g].start()
        packed = lax.select(side == g, mine_ref[...], theirs_ref[...]).astype(F32)
        par_ref[g] = packed[0:4] + packed[4:8]
    parts = [split3(mean) for mean in means]
    tail = [parts[g][term] for term in range(3) for g in range(2)]
    tail = jnp.concatenate(tail + [jnp.zeros((2, GW), F32)], axis=0).astype(BF16)
    tail_ref[...] = tail
    send_ref[4 * 3 * PIECE:] = tail
    for at, (a, b) in enumerate(((0, 0), (0, 1), (1, 1))):
        gram = lax.dot_general(zc_ref[a], zc_ref[b], (((0,), (0,)), ((), ())), preferred_element_type=F32)
        low, high = gram[0:GW // 2], gram[GW // 2:]
        keep, send = lax.select(core == 0, low, high), lax.select(core == 0, high, low).astype(BF16)
        for j in range(4):
            rows = pl.ds((3 * j + at) * PIECE, PIECE)
            keep_ref[rows] = keep[j * PIECE:(j + 1) * PIECE]
            send_ref[rows] = send[j * PIECE:(j + 1) * PIECE]
    for copy in writes:
        copy.wait()


def chip_kernel(j_ref, keep_ref, tail_ref, got_ref, out_ref):
    core = j_ref[0] % 2
    tails = in_order(tail_ref[...], got_ref[4 * 3 * PIECE:], core)
    for j in range(4):
        rows = pl.ds(3 * j * PIECE, 3 * PIECE)
        out_ref[j, 0:3 * PIECE] = (keep_ref[rows] + got_ref[rows].astype(F32)).astype(BF16)
        out_ref[j, 3 * PIECE:] = tails


def mean_of(rows, g):
    return rows[..., g, :] + rows[..., 2 + g, :] + rows[..., 4 + g, :]


def all_means(r_ref):
    rows = r_ref[:, 3 * PIECE:].astype(F32)
    cores = rows[:, 0:TAIL], rows[:, TAIL:]
    return [jnp.concatenate([mean_of(core, g) for core in cores], axis=0) for g in range(2)]


def deviation_kernel(j_ref, r_ref, par_ref, e_ref, scratch_ref):
    row_at = (j_ref[0] % 2 * 4 + j_ref[0] // 2) * PIECE
    means = all_means(r_ref)
    shifted = [m - jnp.mean(m, axis=0, keepdims=True) for m in means]
    highs = [m.astype(BF16).astype(F32) for m in shifted]
    lows = [m - high for m, high in zip(shifted, highs)]
    spare = jnp.zeros((PARTS, GW), F32)
    firsts = [jnp.concatenate([high, high, low, spare], axis=0).astype(BF16) for high, low in zip(highs, lows)]
    seconds = [jnp.concatenate([high, low, high, spare], axis=0).astype(BF16) for high, low in zip(highs, lows)]
    total = jnp.sum(r_ref[:, 0:3 * PIECE].astype(F32), axis=0) * (1.0 / TOTAL)
    diagonal = (
        lax.broadcasted_iota(jnp.int32, (PIECE, GW), 0) + row_at
        == lax.broadcasted_iota(jnp.int32, (PIECE, GW), 1)
    )
    for at, (a, b) in enumerate(((0, 0), (0, 1), (1, 1))):
        scratch_ref[...] = lax.dot_general(
            firsts[a], seconds[b], (((0,), (0,)), ((), ())), preferred_element_type=F32
        )
        part = total[at * PIECE:(at + 1) * PIECE] + scratch_ref[pl.ds(row_at, PIECE), :] * (1.0 / PARTS)
        if a == b:
            part = part - jnp.where(diagonal, par_ref[a, 3:4], 0.0)
        for j in range(4):
            e_ref[j, at * PIECE:(at + 1) * PIECE] = part.astype(BF16)


CHUNKS = 1


def pull_kernel(e_ref, r_ref, tail_ref, zc_in, out_ref, zc_ref, sems):
    reads = []
    for n in range(CHUNKS):
        rows = pl.ds(n * (HOME // CHUNKS), HOME // CHUNKS)
        reads.append(pltpu.make_async_copy(zc_in.at[:, rows], zc_ref.at[:, rows], sems.at[n]))
        reads[n].start()
    means = all_means(r_ref)
    mine = tail_ref[...].astype(F32)
    mats = [e_ref[:, :, at * PIECE:(at + 1) * PIECE].reshape(GW, GW) for at in range(3)]
    whole = [m.astype(F32) for m in mats]
    loss = 0.25 * (
        jnp.sum(whole[0] * whole[0], keepdims=True)
        + 2.0 * jnp.sum(whole[1] * whole[1], keepdims=True)
        + jnp.sum(whole[2] * whole[2], keepdims=True)
    )
    away, offset = [], []
    for g in range(2):
        mean = jnp.mean(means[g], axis=0, keepdims=True)
        loss = loss + jnp.sum(mean * mean, keepdims=True)
        away.append(2.0 * mean)
        own = mine[g:g + 1] + mine[2 + g:3 + g] + mine[4 + g:5 + g]
        offset.append(jnp.concatenate(list(split3(own - mean)) + [jnp.zeros((13, GW), F32)], axis=0).astype(BF16))
    tail = [jnp.broadcast_to(part, (1, LANES)) for part in split3(loss)]
    tail = jnp.concatenate(tail + [jnp.zeros((TAIL - 3, LANES), F32)], axis=0).astype(BF16)
    tail = jnp.broadcast_to(tail[None], (CHIPS, TAIL, LANES))
    plain, crossed = (((1,), (0,)), ((), ())), (((1,), (1,)), ((), ()))

    def both(lhs, g):
        (at, first), (bt, second) = ((0, plain), (1, crossed)) if g == 0 else ((1, plain), (2, plain))
        return lax.dot_general(lhs[0], mats[at], first, preferred_element_type=F32) + lax.dot_general(
            lhs[1], mats[bt], second, preferred_element_type=F32
        )

    rows = []
    for g in range(2):
        row = both(offset, g)
        rows.append(row[0:1] + row[1:2] + row[2:3] + away[g])
    size = HOME // CHUNKS
    chips = CHIPS // CHUNKS
    for copy in reads:
        copy.wait()
    for n in range(CHUNKS):
        for g in range(2):
            pull = both([zc_ref[side, n * size:(n + 1) * size] for side in range(2)], g) + rows[g]
            pull = pull.astype(BF16).reshape(chips, HALF, GW)
            out_ref[g, n * chips:(n + 1) * chips, 0:HALF] = pull[:, :, 0:LANES]
            out_ref[g, n * chips:(n + 1) * chips, HALF:2 * HALF] = pull[:, :, LANES:]
    for g in range(2):
        out_ref[g, :, 2 * HALF:] = tail


def backward_kernel(q_ref, own_in, other_in, slope_in, out_ref, w_ref, slope_ref, sems, slope_sem):
    core = lax.axis_index("c")
    arrivals = [weight_reads(own_in, other_in, w_ref, core, sems, layer) for layer in range(LAYERS)]
    parts = [pl.ds(LAYERS - FIRST, FIRST), pl.ds(0, LAYERS - FIRST)]
    slopes = [pltpu.make_async_copy(slope_in.at[at], slope_ref.at[at], slope_sem.at[n]) for n, at in enumerate(parts)]
    arrivals = [sum(arrivals[LAYERS - FIRST:], []) + slopes[:1], sum(arrivals[:LAYERS - FIRST], []) + slopes[1:]]
    for copy in arrivals[0] + arrivals[1]:
        copy.start()
    loss = jnp.zeros((1, LANES), F32)
    grad = None
    for layer in reversed(range(LAYERS)):
        rows = q_ref[0, layer, 2 * HALF:].astype(F32)
        loss = loss + (rows[0:1] + rows[1:2] + rows[2:3])
        pull = jnp.concatenate(
            [q_ref[:, layer, 0:HALF].reshape(ROWS, LANES), q_ref[:, layer, HALF:2 * HALF].reshape(ROWS, LANES)], axis=1
        )
        if layer in (LAYERS - 1, LAYERS - 1 - FIRST):
            for copy in arrivals[0 if layer == LAYERS - 1 else 1]:
                copy.wait()
        if grad is not None:
            pull = (grad * slope_ref[layer].astype(F32) + pull.astype(F32)).astype(BF16)
        grad = lax.dot_general(
            pull, w_ref[layer].reshape(GW, GW), (((1,), (1,)), ((), ())), preferred_element_type=F32
        )
    loss = jnp.concatenate([loss, loss], axis=1)
    tail = jnp.concatenate(list(split3(loss)) + [jnp.zeros((TAIL - 3, GW), F32)], axis=0).astype(BF16)
    grad = grad.astype(BF16)
    for strip in range(8):
        slot = strip % 2 * 4 + strip // 2
        out_ref[slot, 0:16] = grad[strip * 16:strip * 16 + 16]
        out_ref[slot, 16:16 + TAIL] = tail


def output_kernel(r_ref, grad_ref, loss_ref):
    loss = jnp.zeros((1, 1), F32)
    for k in range(BLOCKS):
        for g in range(2):
            at = 2 * k + g
            grad_ref[0, :, at * GW:(at + 1) * GW] = r_ref[4 * g + k, 0:16]
        loss = loss + jnp.sum(r_ref[k, 16:16 + TAIL].astype(F32)[0:3, 0:1], axis=0, keepdims=True)
    loss_ref[...] = loss * (1.0 / (LAYERS * BLOCKS * 2 * GW))


def near(array):
    return pltpu.with_memory_space_constraint(array, pltpu.VMEM)


def kernel_call(kernel, outs, name, *args, scalars=(), scratch=()):
    vmem = pl.BlockSpec(memory_space=pltpu.VMEM)
    smem = pl.BlockSpec(memory_space=pltpu.SMEM)
    return pl.pallas_call(
        kernel,
        out_shape=[pltpu.VMEM(*out) for out in outs],
        in_specs=[smem] * len(scalars) + [vmem] * len(args),
        out_specs=[vmem] * len(outs),
        scratch_shapes=list(scratch),
        name=name,
    )(*scalars, *[near(arg) for arg in args])


def shards(images, weights, bn_mean, bn_var, bn_gain, bn_bias):
    part = lax.axis_index(("g", "h", "c")).astype(jnp.int32).reshape(1)

    hbm, vmem = pl.BlockSpec(memory_space=pl.ANY), pl.BlockSpec(memory_space=pltpu.VMEM)
    message, rows = pl.pallas_call(
        pack_kernel,
        out_shape=[pltpu.VMEM((2, 4, 2, SLICE + PROWS, GW), BF16), pltpu.VMEM((ROWS, GW), BF16)],
        in_specs=[hbm] * 6,
        out_specs=[vmem, vmem],
        scratch_shapes=[pltpu.VMEM((2 * BLOCKS, SLICE, GW), BF16)]
        + [pltpu.VMEM((1, 2 * BLOCKS * GW), F32)] * 4
        + [pltpu.SemaphoreType.DMA((9,))],
        name="pack",
    )(weights, images, bn_mean, bn_var, bn_gain, bn_bias)
    message = message.reshape(LAYERS, SLICE + PROWS, GW)
    layer_parts = lax.all_to_all(message, ("h", "k", "g"), 0, 0, tiled=True)

    own = layer_parts[:, 0:SLICE]
    own = lax.all_to_all(jnp.broadcast_to(own[None], (CHIPS, LAYERS, SLICE, GW)), ("y", "x"), 0, 0, tiled=True)
    other = lax.ppermute(own, "c", [(0, 1), (1, 0)])

    layers = [pltpu.VMEM((LAYERS, 2, CHIPS, SLICE, GW), BF16), pltpu.VMEM((LAYERS, ROWS, GW), BF16)]
    sems = pltpu.SemaphoreType.DMA((2, LAYERS))
    pieces_shape = (2, LAYERS, HALF, GW)
    xs, slope = pl.pallas_call(
        forward_kernel,
        out_shape=[jax.ShapeDtypeStruct(pieces_shape, BF16), jax.ShapeDtypeStruct((LAYERS, ROWS, GW), BF16)],
        in_specs=[vmem, vmem, hbm, vmem],
        out_specs=[hbm, hbm],
        scratch_shapes=layers
        + [pltpu.VMEM((LAYERS, 4, GW), F32), pltpu.VMEM(pieces_shape, BF16)]
        + [sems, pltpu.SemaphoreType.DMA((4,))],
        name="fwd",
    )(near(rows), near(layer_parts), own, near(other))

    home = lax.all_to_all(xs.reshape(2 * CHIPS, HALF, GW), ("g", "x", "y"), 0, 0, tiled=True)
    mine = lax.dynamic_index_in_dim(layer_parts, slot(lax.axis_index(("x", "y"))), 0, keepdims=False)[SLICE:]
    mine = lax.optimization_barrier((mine, xs))[0]
    theirs = lax.ppermute(mine, "g", [(0, 1), (1, 0)])
    held = pltpu.VMEM((2, HOME, GW), BF16)
    keep, send, tail, params, centered = pl.pallas_call(
        gram_kernel,
        out_shape=[
            pltpu.VMEM((4 * 3 * PIECE, GW), F32),
            pltpu.VMEM((4 * 3 * PIECE + TAIL, GW), BF16),
            pltpu.VMEM((TAIL, GW), BF16),
            pltpu.VMEM((2, 4, GW), F32),
            jax.ShapeDtypeStruct((2, HOME, GW), BF16),
        ],
        in_specs=[vmem] * 3,
        out_specs=[vmem] * 4 + [hbm],
        scratch_shapes=[held, pltpu.SemaphoreType.DMA((2,))],
        name="gram",
    )(near(home.reshape(2, CHIPS, HALF, GW)), near(mine), near(theirs))
    got = lax.ppermute(send, "c", [(0, 1), (1, 0)])
    (pieces,) = kernel_call(
        chip_kernel, [((4, 3 * PIECE + 2 * TAIL, GW), BF16)], "chip", keep, tail, got, scalars=[part]
    )
    pieces = lax.all_to_all(pieces, ("g", "h"), 0, 0, tiled=True)
    (deviation,) = kernel_call(
        deviation_kernel,
        [((4, 3 * PIECE, GW), BF16)],
        "deviation",
        pieces,
        params,
        scalars=[part],
        scratch=[pltpu.VMEM((GW, GW), F32)],
    )
    deviation = lax.all_gather(lax.all_to_all(deviation, ("g", "h"), 0, 0, tiled=True), "c", axis=0)
    pulls = pl.pallas_call(
        pull_kernel,
        out_shape=pltpu.VMEM((2, CHIPS, 2 * HALF + TAIL, LANES), BF16),
        in_specs=[vmem] * 3 + [hbm],
        out_specs=vmem,
        scratch_shapes=[held, pltpu.SemaphoreType.DMA((CHUNKS,))],
        name="pull",
    )(near(deviation), near(pieces), near(tail), centered)
    pulls = lax.all_to_all(pulls.reshape(2 * CHIPS, 2 * HALF + TAIL, LANES), ("g", "x", "y"), 0, 0, tiled=True)

    grads = pl.pallas_call(
        backward_kernel,
        out_shape=pltpu.VMEM((8, 16 + TAIL, GW), BF16),
        in_specs=[vmem, hbm, hbm, hbm],
        out_specs=vmem,
        scratch_shapes=layers + [sems, pltpu.SemaphoreType.DMA((2,))],
        name="bwd",
    )(near(pulls.reshape(2, LAYERS, 2 * HALF + TAIL, LANES)), own, other, slope)
    grads = lax.all_to_all(grads, ("g", "k"), 0, 0, tiled=True)
    image_grad, loss = pl.pallas_call(
        output_kernel,
        out_shape=[jax.ShapeDtypeStruct((1, 16, BLOCKS * 2 * GW), BF16), jax.ShapeDtypeStruct((1, 1), F32)],
        in_specs=[vmem],
        out_specs=[vmem, vmem],
        name="outputs",
    )(near(grads))
    return image_grad, loss.reshape(())


def solution(mesh):
    fine = Mesh(np.asarray(mesh.devices).reshape(4, 2, 2, 4, 4, 2), ("k", "h", "g", "x", "y", "c"))
    batch, section = ("x", "y", "c"), ("k", "h", "g")
    return jax.shard_map(
        shards,
        mesh=fine,
        in_specs=(
            P(batch, None, None),
            P(section, None, None, None),
            P(section, None),
            P(section, None),
            P(section, None),
            P(section, None),
        ),
        out_specs=(P(batch, section, None), P()),
        check_vma=False,
    )
```

```python
import math

import jax
import jax.numpy as jnp
import numpy as np
from jax import lax
from jax.experimental import pallas as pl
from jax.experimental.pallas import tpu as pltpu
from jax.sharding import Mesh, PartitionSpec as P

EPS = 1e-05
LOG2E = math.log2(math.e)
F32 = jnp.float32
BF16 = jnp.bfloat16

LAYERS = 16
GW = 256
BLOCKS = 3
CHIPS = 16
SLICE = GW // (2 * CHIPS)
PROWS = 8
ROWS = 128
HALF = ROWS // 2
HOME = CHIPS * HALF
LANES = 128
PARTS = 8
PIECE = GW // PARTS
TAIL = 8
TOTAL = HOME * PARTS


def split3(value):
    high = value.astype(BF16).astype(F32)
    rest = value - high
    middle = rest.astype(BF16).astype(F32)
    return high, middle, rest - middle


def pack_kernel(w_ref, images_ref, *refs):
    inputs, (out_ref, x_ref, slab_ref), held, sems = refs[:4], refs[4:7], refs[7:11], refs[11]
    reads = [pltpu.make_async_copy(source, target, sems.at[5 + at]) for at, (source, target) in enumerate(zip(inputs, held))]
    for copy in reads:
        copy.start()
    mean_ref, var_ref, gain_ref, bias_ref = held
    chip = lax.axis_index("x") * 4 + lax.axis_index("y")
    row = (lax.axis_index("c") * CHIPS + chip) * SLICE
    half = lax.axis_index("h")
    group = 2 * jnp.minimum(lax.axis_index("k"), BLOCKS - 1) + lax.axis_index("g")
    slab = pltpu.make_async_copy(w_ref.at[0, :, pl.ds(pl.multiple_of(row, SLICE), SLICE), :], slab_ref, sems.at[0])
    slab.start()
    copies = []
    for strip in range(4):
        source = images_ref.at[
            0, pl.ds(pl.multiple_of(strip * 64 + half * 32, 32), 32), pl.ds(pl.multiple_of(group * GW, GW), GW)
        ]
        copies.append(pltpu.make_async_copy(source, x_ref.at[strip * 32:strip * 32 + 32], sems.at[1 + strip]))
        copies[-1].start()
    for copy in reads:
        copy.wait()
    scale = gain_ref[...] * lax.rsqrt(var_ref[...] + EPS)
    packed = [scale, bias_ref[...] - mean_ref[...] * scale, mean_ref[...], var_ref[...]]
    high = [value.astype(BF16).astype(F32) for value in packed]
    packed = jnp.concatenate(high + [value - top for value, top in zip(packed, high)], axis=0).astype(BF16)
    slab.wait()
    for k in range(4):
        for g in range(2):
            at = 2 * min(k, BLOCKS - 1) + g
            for h in range(2):
                out_ref[h, k, g, 0:SLICE] = slab_ref[at]
                out_ref[h, k, g, SLICE:] = packed[:, at * GW:(at + 1) * GW]
    for copy in copies:
        copy.wait()


def in_order(own, other, core):
    return jnp.concatenate([lax.select(core == 0, own, other), lax.select(core == 0, other, own)], axis=0)


FIRST = 4


def slot(layer):
    return layer // 2 % 2 * 8 + layer // 4 * 2 + layer % 2


def weight_reads(own_in, other_in, w_ref, core, sems, layer):
    return [
        pltpu.make_async_copy(own_in.at[:, slot(layer)], w_ref.at[layer, core], sems.at[0, layer]),
        pltpu.make_async_copy(other_in.at[:, slot(layer)], w_ref.at[layer, 1 - core], sems.at[1, layer]),
    ]


def forward_kernel(
    x_ref, par_ref, own_in, other_in, xs_out, slope_out, w_ref, slope_ref, rows_ref, xs_ref, sems, out_sems
):
    core = lax.axis_index("c")
    arrivals = [weight_reads(own_in, other_in, w_ref, core, sems, layer) for layer in range(LAYERS)]
    for copy in sum(arrivals, []):
        copy.start()
    for layer in range(LAYERS):
        packed = par_ref[slot(layer), SLICE:SLICE + PROWS].astype(F32)
        rows_ref[layer] = packed[0:4] + packed[4:8]
    writes = []

    def write(first, last):
        span = pl.ds(first, last - first)
        at = len(writes)
        writes.append(pltpu.make_async_copy(xs_ref.at[:, span], xs_out.at[:, span], out_sems.at[at]))
        writes.append(pltpu.make_async_copy(slope_ref.at[span], slope_out.at[span], out_sems.at[at + 1]))
        for copy in writes[-2:]:
            copy.start()

    x = x_ref[...]
    for layer in range(LAYERS):
        if layer in (0, FIRST):
            for copy in sum(arrivals[0:FIRST] if layer == 0 else arrivals[FIRST:], []):
                copy.wait()
        z = jnp.dot(x, w_ref[layer].reshape(GW, GW), preferred_element_type=F32)
        scale, shift = rows_ref[layer, 0:1], rows_ref[layer, 1:2]
        active = z * scale + shift
        gate = 1.0 / (1.0 + jnp.exp2(z * (scale * -LOG2E) + shift * -LOG2E))
        after = active * gate
        x = after.astype(BF16)
        slope_ref[layer] = (gate * ((active - after) + 1.0) * scale).astype(BF16)
        away = (z - rows_ref[layer, 2:3]).astype(BF16)
        for half in range(2):
            xs_ref[half, layer] = away[half * HALF:(half + 1) * HALF]
        if layer == LAYERS // 2:
            write(0, LAYERS // 2)
    write(LAYERS // 2, LAYERS)
    for copy in writes:
        copy.wait()


def gram_kernel(x_ref, mine_ref, theirs_ref, keep_ref, send_ref, tail_ref, par_ref, zc_out, zc_ref, sems):
    core, side = lax.axis_index("c"), lax.axis_index("g")
    means, writes = [], []
    for g in range(2):
        rows = x_ref[g].reshape(HOME, GW).astype(F32)
        means.append(jnp.sum(rows, axis=0, keepdims=True) * (1.0 / HOME))
        zc_ref[g] = (rows - means[g]).astype(BF16)
        writes.append(pltpu.make_async_copy(zc_ref.at[g], zc_out.at[g], sems.at[g]))
        writes[g].start()
        packed = lax.select(side == g, mine_ref[...], theirs_ref[...]).astype(F32)
        par_ref[g] = packed[0:4] + packed[4:8]
    parts = [split3(mean) for mean in means]
    tail = [parts[g][term] for term in range(3) for g in range(2)]
    tail = jnp.concatenate(tail + [jnp.zeros((2, GW), F32)], axis=0).astype(BF16)
    tail_ref[...] = tail
    send_ref[4 * 3 * PIECE:] = tail
    for at, (a, b) in enumerate(((0, 0), (0, 1), (1, 1))):
        gram = lax.dot_general(zc_ref[a], zc_ref[b], (((0,), (0,)), ((), ())), preferred_element_type=F32)
        low, high = gram[0:GW // 2], gram[GW // 2:]
        keep, send = lax.select(core == 0, low, high), lax.select(core == 0, high, low).astype(BF16)
        for j in range(4):
            rows = pl.ds((3 * j + at) * PIECE, PIECE)
            keep_ref[rows] = keep[j * PIECE:(j + 1) * PIECE]
            send_ref[rows] = send[j * PIECE:(j + 1) * PIECE]
    for copy in writes:
        copy.wait()


def chip_kernel(j_ref, keep_ref, tail_ref, got_ref, out_ref):
    core = j_ref[0] % 2
    tails = in_order(tail_ref[...], got_ref[4 * 3 * PIECE:], core)
    for j in range(4):
        rows = pl.ds(3 * j * PIECE, 3 * PIECE)
        out_ref[j, 0:3 * PIECE] = (keep_ref[rows] + got_ref[rows].astype(F32)).astype(BF16)
        out_ref[j, 3 * PIECE:] = tails


def mean_of(rows, g):
    return rows[..., g, :] + rows[..., 2 + g, :] + rows[..., 4 + g, :]


def all_means(r_ref):
    rows = r_ref[:, 3 * PIECE:].astype(F32)
    cores = rows[:, 0:TAIL], rows[:, TAIL:]
    return [jnp.concatenate([mean_of(core, g) for core in cores], axis=0) for g in range(2)]


def deviation_kernel(j_ref, r_ref, par_ref, e_ref, scratch_ref):
    row_at = (j_ref[0] % 2 * 4 + j_ref[0] // 2) * PIECE
    means = all_means(r_ref)
    shifted = [m - jnp.mean(m, axis=0, keepdims=True) for m in means]
    highs = [m.astype(BF16).astype(F32) for m in shifted]
    lows = [m - high for m, high in zip(shifted, highs)]
    spare = jnp.zeros((PARTS, GW), F32)
    firsts = [jnp.concatenate([high, high, low, spare], axis=0).astype(BF16) for high, low in zip(highs, lows)]
    seconds = [jnp.concatenate([high, low, high, spare], axis=0).astype(BF16) for high, low in zip(highs, lows)]
    total = jnp.sum(r_ref[:, 0:3 * PIECE].astype(F32), axis=0) * (1.0 / TOTAL)
    diagonal = (
        lax.broadcasted_iota(jnp.int32, (PIECE, GW), 0) + row_at
        == lax.broadcasted_iota(jnp.int32, (PIECE, GW), 1)
    )
    for at, (a, b) in enumerate(((0, 0), (0, 1), (1, 1))):
        scratch_ref[...] = lax.dot_general(
            firsts[a], seconds[b], (((0,), (0,)), ((), ())), preferred_element_type=F32
        )
        part = total[at * PIECE:(at + 1) * PIECE] + scratch_ref[pl.ds(row_at, PIECE), :] * (1.0 / PARTS)
        if a == b:
            part = part - jnp.where(diagonal, par_ref[a, 3:4], 0.0)
        for j in range(4):
            e_ref[j, at * PIECE:(at + 1) * PIECE] = part.astype(BF16)


CHUNKS = 1


def pull_kernel(e_ref, r_ref, tail_ref, zc_in, out_ref, zc_ref, sems):
    reads = []
    for n in range(CHUNKS):
        rows = pl.ds(n * (HOME // CHUNKS), HOME // CHUNKS)
        reads.append(pltpu.make_async_copy(zc_in.at[:, rows], zc_ref.at[:, rows], sems.at[n]))
        reads[n].start()
    means = all_means(r_ref)
    mine = tail_ref[...].astype(F32)
    mats = [e_ref[:, :, at * PIECE:(at + 1) * PIECE].reshape(GW, GW) for at in range(3)]
    whole = [m.astype(F32) for m in mats]
    loss = 0.25 * (
        jnp.sum(whole[0] * whole[0], keepdims=True)
        + 2.0 * jnp.sum(whole[1] * whole[1], keepdims=True)
        + jnp.sum(whole[2] * whole[2], keepdims=True)
    )
    away, offset = [], []
    for g in range(2):
        mean = jnp.mean(means[g], axis=0, keepdims=True)
        loss = loss + jnp.sum(mean * mean, keepdims=True)
        away.append(2.0 * mean)
        own = mine[g:g + 1] + mine[2 + g:3 + g] + mine[4 + g:5 + g]
        offset.append(jnp.concatenate(list(split3(own - mean)) + [jnp.zeros((13, GW), F32)], axis=0).astype(BF16))
    tail = [jnp.broadcast_to(part, (1, LANES)) for part in split3(loss)]
    tail = jnp.concatenate(tail + [jnp.zeros((TAIL - 3, LANES), F32)], axis=0).astype(BF16)
    tail = jnp.broadcast_to(tail[None], (CHIPS, TAIL, LANES))
    plain, crossed = (((1,), (0,)), ((), ())), (((1,), (1,)), ((), ()))

    def both(lhs, g):
        (at, first), (bt, second) = ((0, plain), (1, crossed)) if g == 0 else ((1, plain), (2, plain))
        return lax.dot_general(lhs[0], mats[at], first, preferred_element_type=F32) + lax.dot_general(
            lhs[1], mats[bt], second, preferred_element_type=F32
        )

    rows = []
    for g in range(2):
        row = both(offset, g)
        rows.append(row[0:1] + row[1:2] + row[2:3] + away[g])
    size = HOME // CHUNKS
    chips = CHIPS // CHUNKS
    for copy in reads:
        copy.wait()
    for n in range(CHUNKS):
        for g in range(2):
            pull = both([zc_ref[side, n * size:(n + 1) * size] for side in range(2)], g) + rows[g]
            pull = pull.astype(BF16).reshape(chips, HALF, GW)
            out_ref[g, n * chips:(n + 1) * chips, 0:HALF] = pull[:, :, 0:LANES]
            out_ref[g, n * chips:(n + 1) * chips, HALF:2 * HALF] = pull[:, :, LANES:]
    for g in range(2):
        out_ref[g, :, 2 * HALF:] = tail


def backward_kernel(q_ref, own_in, other_in, slope_in, out_ref, w_ref, slope_ref, sems, slope_sem):
    core = lax.axis_index("c")
    arrivals = [weight_reads(own_in, other_in, w_ref, core, sems, layer) for layer in range(LAYERS)]
    parts = [pl.ds(LAYERS - FIRST, FIRST), pl.ds(0, LAYERS - FIRST)]
    slopes = [pltpu.make_async_copy(slope_in.at[at], slope_ref.at[at], slope_sem.at[n]) for n, at in enumerate(parts)]
    arrivals = [sum(arrivals[LAYERS - FIRST:], []) + slopes[:1], sum(arrivals[:LAYERS - FIRST], []) + slopes[1:]]
    for copy in arrivals[0] + arrivals[1]:
        copy.start()
    loss = jnp.zeros((1, LANES), F32)
    grad = None
    for layer in reversed(range(LAYERS)):
        rows = q_ref[0, layer, 2 * HALF:].astype(F32)
        loss = loss + (rows[0:1] + rows[1:2] + rows[2:3])
        pull = jnp.concatenate(
            [q_ref[:, layer, 0:HALF].reshape(ROWS, LANES), q_ref[:, layer, HALF:2 * HALF].reshape(ROWS, LANES)], axis=1
        )
        if layer in (LAYERS - 1, LAYERS - 1 - FIRST):
            for copy in arrivals[0 if layer == LAYERS - 1 else 1]:
                copy.wait()
        if grad is not None:
            pull = (grad * slope_ref[layer].astype(F32) + pull.astype(F32)).astype(BF16)
        grad = lax.dot_general(
            pull, w_ref[layer].reshape(GW, GW), (((1,), (1,)), ((), ())), preferred_element_type=F32
        )
    loss = jnp.concatenate([loss, loss], axis=1)
    tail = jnp.concatenate(list(split3(loss)) + [jnp.zeros((TAIL - 3, GW), F32)], axis=0).astype(BF16)
    grad = grad.astype(BF16)
    for strip in range(8):
        slot = strip % 2 * 4 + strip // 2
        out_ref[slot, 0:16] = grad[strip * 16:strip * 16 + 16]
        out_ref[slot, 16:16 + TAIL] = tail


def output_kernel(r_ref, grad_ref, loss_ref):
    loss = jnp.zeros((1, 1), F32)
    for k in range(BLOCKS):
        for g in range(2):
            at = 2 * k + g
            grad_ref[0, :, at * GW:(at + 1) * GW] = r_ref[4 * g + k, 0:16]
        loss = loss + jnp.sum(r_ref[k, 16:16 + TAIL].astype(F32)[0:3, 0:1], axis=0, keepdims=True)
    loss_ref[...] = loss * (1.0 / (LAYERS * BLOCKS * 2 * GW))


def near(array):
    return pltpu.with_memory_space_constraint(array, pltpu.VMEM)


def kernel_call(kernel, outs, name, *args, scalars=(), scratch=()):
    vmem = pl.BlockSpec(memory_space=pltpu.VMEM)
    smem = pl.BlockSpec(memory_space=pltpu.SMEM)
    return pl.pallas_call(
        kernel,
        out_shape=[pltpu.VMEM(*out) for out in outs],
        in_specs=[smem] * len(scalars) + [vmem] * len(args),
        out_specs=[vmem] * len(outs),
        scratch_shapes=list(scratch),
        name=name,
    )(*scalars, *[near(arg) for arg in args])


def shards(images, weights, bn_mean, bn_var, bn_gain, bn_bias):
    part = lax.axis_index(("g", "h", "c")).astype(jnp.int32).reshape(1)

    hbm, vmem = pl.BlockSpec(memory_space=pl.ANY), pl.BlockSpec(memory_space=pltpu.VMEM)
    message, rows = pl.pallas_call(
        pack_kernel,
        out_shape=[pltpu.VMEM((2, 4, 2, SLICE + PROWS, GW), BF16), pltpu.VMEM((ROWS, GW), BF16)],
        in_specs=[hbm] * 6,
        out_specs=[vmem, vmem],
        scratch_shapes=[pltpu.VMEM((2 * BLOCKS, SLICE, GW), BF16)]
        + [pltpu.VMEM((1, 2 * BLOCKS * GW), F32)] * 4
        + [pltpu.SemaphoreType.DMA((9,))],
        name="pack",
    )(weights, images, bn_mean, bn_var, bn_gain, bn_bias)
    message = message.reshape(LAYERS, SLICE + PROWS, GW)
    layer_parts = lax.all_to_all(message, ("h", "k", "g"), 0, 0, tiled=True)

    own = layer_parts[:, 0:SLICE]
    own = lax.all_to_all(jnp.broadcast_to(own[None], (CHIPS, LAYERS, SLICE, GW)), ("x", "y"), 0, 0, tiled=True)
    other = lax.ppermute(own, "c", [(0, 1), (1, 0)])

    layers = [pltpu.VMEM((LAYERS, 2, CHIPS, SLICE, GW), BF16), pltpu.VMEM((LAYERS, ROWS, GW), BF16)]
    sems = pltpu.SemaphoreType.DMA((2, LAYERS))
    pieces_shape = (2, LAYERS, HALF, GW)
    xs, slope = pl.pallas_call(
        forward_kernel,
        out_shape=[jax.ShapeDtypeStruct(pieces_shape, BF16), jax.ShapeDtypeStruct((LAYERS, ROWS, GW), BF16)],
        in_specs=[vmem, vmem, hbm, vmem],
        out_specs=[hbm, hbm],
        scratch_shapes=layers
        + [pltpu.VMEM((LAYERS, 4, GW), F32), pltpu.VMEM(pieces_shape, BF16)]
        + [sems, pltpu.SemaphoreType.DMA((4,))],
        name="fwd",
    )(near(rows), near(layer_parts), own, near(other))

    home = lax.all_to_all(xs.reshape(2 * CHIPS, HALF, GW), ("g", "x", "y"), 0, 0, tiled=True)
    mine = lax.dynamic_index_in_dim(layer_parts, slot(lax.axis_index(("x", "y"))), 0, keepdims=False)[SLICE:]
    mine = lax.optimization_barrier((mine, xs))[0]
    theirs = lax.ppermute(mine, "g", [(0, 1), (1, 0)])
    held = pltpu.VMEM((2, HOME, GW), BF16)
    keep, send, tail, params, centered = pl.pallas_call(
        gram_kernel,
        out_shape=[
            pltpu.VMEM((4 * 3 * PIECE, GW), F32),
            pltpu.VMEM((4 * 3 * PIECE + TAIL, GW), BF16),
            pltpu.VMEM((TAIL, GW), BF16),
            pltpu.VMEM((2, 4, GW), F32),
            jax.ShapeDtypeStruct((2, HOME, GW), BF16),
        ],
        in_specs=[vmem] * 3,
        out_specs=[vmem] * 4 + [hbm],
        scratch_shapes=[held, pltpu.SemaphoreType.DMA((2,))],
        name="gram",
    )(near(home.reshape(2, CHIPS, HALF, GW)), near(mine), near(theirs))
    got = lax.ppermute(send, "c", [(0, 1), (1, 0)])
    (pieces,) = kernel_call(
        chip_kernel, [((4, 3 * PIECE + 2 * TAIL, GW), BF16)], "chip", keep, tail, got, scalars=[part]
    )
    pieces = lax.all_to_all(pieces, ("g", "h"), 0, 0, tiled=True)
    (deviation,) = kernel_call(
        deviation_kernel,
        [((4, 3 * PIECE, GW), BF16)],
        "deviation",
        pieces,
        params,
        scalars=[part],
        scratch=[pltpu.VMEM((GW, GW), F32)],
    )
    deviation = lax.all_gather(lax.all_to_all(deviation, ("g", "h"), 0, 0, tiled=True), "c", axis=0)
    pulls = pl.pallas_call(
        pull_kernel,
        out_shape=pltpu.VMEM((2, CHIPS, 2 * HALF + TAIL, LANES), BF16),
        in_specs=[vmem] * 3 + [hbm],
        out_specs=vmem,
        scratch_shapes=[held, pltpu.SemaphoreType.DMA((CHUNKS,))],
        name="pull",
    )(near(deviation), near(pieces), near(tail), centered)
    pulls = lax.all_to_all(pulls.reshape(2 * CHIPS, 2 * HALF + TAIL, LANES), ("g", "x", "y"), 0, 0, tiled=True)

    grads = pl.pallas_call(
        backward_kernel,
        out_shape=pltpu.VMEM((8, 16 + TAIL, GW), BF16),
        in_specs=[vmem, hbm, hbm, hbm],
        out_specs=vmem,
        scratch_shapes=layers + [sems, pltpu.SemaphoreType.DMA((2,))],
        name="bwd",
    )(near(pulls.reshape(2, LAYERS, 2 * HALF + TAIL, LANES)), own, other, slope)
    grads = lax.all_to_all(grads, ("g", "k"), 0, 0, tiled=True)
    image_grad, loss = pl.pallas_call(
        output_kernel,
        out_shape=[jax.ShapeDtypeStruct((1, 16, BLOCKS * 2 * GW), BF16), jax.ShapeDtypeStruct((1, 1), F32)],
        in_specs=[vmem],
        out_specs=[vmem, vmem],
        name="outputs",
    )(near(grads))
    return image_grad, loss.reshape(())


def solution(mesh):
    fine = Mesh(np.asarray(mesh.devices).reshape(4, 2, 2, 4, 4, 2), ("k", "h", "g", "x", "y", "c"))
    batch, section = ("x", "y", "c"), ("k", "h", "g")
    return jax.shard_map(
        shards,
        mesh=fine,
        in_specs=(
            P(batch, None, None),
            P(section, None, None, None),
            P(section, None),
            P(section, None),
            P(section, None),
            P(section, None),
        ),
        out_specs=(P(batch, section, None), P()),
        check_vma=False,
    )
```
